128 devices in a mesh: group: 8 (over x_lo, z), tensor: 16 (over x_hi, y, core).
Axes of the slice: x: 4 (x_hi: 2, x_lo: 2; x = x_hi * 2 + x_lo), y: 4, z: 4, core: 2. Of those that a mesh axis runs over, the one named last changes fastest.
Arguments:
- hidden: bfloat16 [12288, 2048], P(('group', 'tensor')), may hold values from -20 to 20
- request_of: int32 [12288], P('group'), may hold values from 0 to 191, as said below
- positions: int32 [12288], P('group'), may hold values from 0 to 511, as said below
- page_table: int32 [8, 64], P('group'), may hold values from 0 to 63, each once within a row
- attn_gain: float32 [2048], replicated, may hold values from 0.5 to 1.5
- mlp_gain: float32 [2048], replicated, may hold values from 0.5 to 1.5
- wq: float32 [2048, 2048], P('group', 'tensor'), may hold values from -2 to 2
- wk: float32 [2048, 1024], P('group', 'tensor'), may hold values from -1 to 1
- wv: float32 [2048, 1024], P('group', 'tensor'), may hold values from -0.125 to 0.125
- wo: float32 [2048, 2048], P('tensor', 'group'), may hold values from -0.125 to 0.125
- w_gate: float32 [2048, 8192], P('group', 'tensor'), may hold values from -0.125 to 0.125
- w_up: float32 [2048, 8192], P('group', 'tensor'), may hold values from -0.125 to 0.125
- w_down: float32 [8192, 2048], P('tensor', 'group'), may hold values from -0.0625 to 0.0625
Outputs:
- layer_out: bfloat16 [12288, 2048], P(('group', 'tensor'))
- kv_pages: bfloat16 [512, 128, 2048], P('group', None, 'tensor')
The draws below stay inside these ranges and needn't reach their ends.
Inputs may be any that keep to these rules, and one draw needn't show every extreme that they name: `request_of`: prompt numbers rise strictly along the token stream, starting at 0, and the last prompt of the stream has the number 12288 // 64 - 1; a prompt's rows are consecutive, and a prompt that reaches the last row of one block of 1536 rows continues at the first row of the next block. A prompt's rows have positions 0, 1, 2 and so on in order; a prompt has at most 512 rows, and one has exactly 512.
All inputs are finite; a program needn't handle non-finite values.
Results may differ from the reference program's by a relative error of at most 0.014.
Values may be sent and summed in bfloat16 or wider, within the bound.
A program may use at most 128 MiB of HBM per device.

```python
import jax
import jax.numpy as jnp
from jax import lax

D = 2048
QH = 16
KVH = 8
HD = 128
FF = 8192
TOK_GRP = 1536
MAXLEN = 512
MINLEN = 64
PAGE = 128
TOKENS = 12288
PAGES_GRP = 64
N_GROUP = 8


def request_stream(key):
    count = TOKENS // MINLEN + 1
    stream_key = jax.random.fold_in(key, 7101)
    first_key, second_key, third_key = jax.random.split(stream_key, 3)
    expo = jax.random.randint(first_key, (count,), 0, 4)
    extra = jax.random.randint(second_key, (count,), 0, MINLEN)
    lengths = jnp.minimum(MAXLEN, jnp.left_shift(jnp.int32(MINLEN), expo) + extra).astype(jnp.int32)
    longest = jax.random.randint(third_key, (), 0, TOKENS // MAXLEN)
    lengths = lengths.at[longest].set(MAXLEN)
    ends = jnp.cumsum(lengths).astype(jnp.int32)
    rows = jnp.arange(TOKENS, dtype=jnp.int32)
    finished = (ends[None, :] <= rows[:, None]).astype(jnp.int32)
    number = jnp.sum(finished, axis=1).astype(jnp.int32)
    begin = jnp.sum(finished * lengths[None, :], axis=1).astype(jnp.int32)
    final_number = number[TOKENS - 1]
    renamed = jnp.where(number == final_number, jnp.int32(TOKENS // MINLEN - 1), number).astype(jnp.int32)
    return (renamed, (rows - begin).astype(jnp.int32))


def draw_request_of(key, part):
    return request_stream(key)[0]


def draw_positions(key, part):
    return request_stream(key)[1]


def draw_hidden(key, part):
    base_key = jax.random.fold_in(jax.random.fold_in(key, 3301), 0)
    values = jax.random.normal(base_key, (TOKENS, D), jnp.float32)
    return jnp.clip(values, -20.0, 20.0).astype(jnp.bfloat16)


def key_basis(key):
    basis_key = jax.random.fold_in(key, 5501)
    basis = jnp.clip(jax.random.normal(basis_key, (D, KVH, HD), jnp.float32), -6.0, 6.0)
    return basis * D ** (-0.5)


def draw_wk(key, part):
    return jnp.clip(key_basis(key), -1.0, 1.0).reshape(D, KVH * HD)


def draw_wq(key, part):
    own_key = jax.random.fold_in(key, 5502)
    values = jnp.clip(jax.random.normal(own_key, (D, QH, HD), jnp.float32), -6.0, 6.0) * D ** (-0.5)
    return jnp.clip(values, -2.0, 2.0).reshape(D, QH * HD)


def block_levels(rng, shape, shards, least, top_value):
    factor_of, own = 1.0, jax.random.fold_in(rng, 6)
    for axis_at, blocks in shards:
        draws = jnp.exp(jax.random.uniform(jax.random.fold_in(own, axis_at), (blocks,), jnp.float32, least / len(shards), top_value / len(shards)))
        factor_of = factor_of * jnp.repeat(draws, shape[axis_at] // blocks).reshape([-1 if axis == axis_at else 1 for axis in range(len(shape))])
    return factor_of


def gaussian(key, dims, deviation, most, cuts=(), held_as=jnp.bfloat16):
    drawn = deviation * jax.random.normal(key, dims, jnp.float32)
    if cuts:
        drawn = drawn * block_levels(key, dims, cuts, -0.22, 0.18)
    return jnp.clip(drawn, -most, most).astype(held_as)


def setup_inputs(seed: int = 0) -> dict:
    seeds = jax.random.split(jax.random.key(seed), 14)
    return {
        "hidden": draw_hidden(jax.random.fold_in(seeds[13], 71), 0),
        "request_of": draw_request_of(jax.random.fold_in(seeds[13], 71), 0),
        "positions": draw_positions(jax.random.fold_in(seeds[13], 71), 0),
        "page_table": jax.vmap(lambda own: jax.random.permutation(own, PAGES_GRP))(jax.random.split(seeds[3], N_GROUP)).reshape((N_GROUP, PAGES_GRP)).astype(jnp.int32),
        "attn_gain": jnp.clip(jax.random.uniform(seeds[4], (D,), jnp.float32, 0.5, 1.5), 0.5, 1.5),
        "mlp_gain": jnp.clip(jax.random.uniform(seeds[5], (D,), jnp.float32, 0.5, 1.5), 0.5, 1.5),
        "wq": draw_wq(jax.random.fold_in(seeds[13], 71), 0),
        "wk": draw_wk(jax.random.fold_in(seeds[13], 71), 0),
        "wv": gaussian(seeds[8], (D, KVH * HD), D ** -0.5, 0.125, ((0, 8), (1, 16)), jnp.float32),
        "wo": gaussian(seeds[9], (QH * HD, D), (QH * HD) ** -0.5, 0.125, ((0, 16), (1, 8)), jnp.float32),
        "w_gate": gaussian(seeds[10], (D, FF), D ** -0.5, 0.125, ((0, 8), (1, 16)), jnp.float32),
        "w_up": gaussian(seeds[11], (D, FF), D ** -0.5, 0.125, ((0, 8), (1, 16)), jnp.float32),
        "w_down": gaussian(seeds[12], (FF, D), FF ** -0.5, 0.0625, ((0, 16), (1, 8)), jnp.float32),
    }


rope_base = 1000000.0
norm_eps = 1e-06

def rms_scale(values, gain):
    square = lax.optimization_barrier(jnp.mean(values * values, axis=-1, keepdims=True))
    return (values * lax.rsqrt(square + norm_eps) * gain).astype(jnp.bfloat16)

def rotate(values, places):
    half_dim = values.shape[-1] // 2
    frequency = rope_base ** (-(jnp.arange(half_dim, dtype=jnp.float32) * 2.0 / values.shape[-1]))
    angle = places.astype(jnp.float32)[:, None] * frequency[None, :]
    cosine = jnp.cos(angle)[:, None, :]
    sine = jnp.sin(angle)[:, None, :]
    widened = values.astype(jnp.float32)
    first = widened[..., :half_dim]
    second = widened[..., half_dim:]
    return jnp.concatenate([first * cosine - second * sine, second * cosine + first * sine], axis=-1).astype(jnp.bfloat16)

def attend_group(index, queries, keys, values, request_of, positions):
    start = (index * TOK_GRP).astype(jnp.int32)
    before = jnp.maximum(start - TOK_GRP, 0).astype(jnp.int32)
    query_block = lax.dynamic_slice_in_dim(queries, start, TOK_GRP, 0)
    key_block = jnp.concatenate([lax.dynamic_slice_in_dim(keys, before, TOK_GRP, 0), lax.dynamic_slice_in_dim(keys, start, TOK_GRP, 0)], axis=0)
    value_block = jnp.concatenate([lax.dynamic_slice_in_dim(values, before, TOK_GRP, 0), lax.dynamic_slice_in_dim(values, start, TOK_GRP, 0)], axis=0)
    own_request = lax.dynamic_slice_in_dim(request_of, start, TOK_GRP, 0)
    earlier_request = jnp.where(index > 0, lax.dynamic_slice_in_dim(request_of, before, TOK_GRP, 0), -1).astype(jnp.int32)
    key_request = jnp.concatenate([earlier_request, own_request], axis=0)
    own_position = lax.dynamic_slice_in_dim(positions, start, TOK_GRP, 0)
    key_position = jnp.concatenate([lax.dynamic_slice_in_dim(positions, before, TOK_GRP, 0), own_position], axis=0)
    visible = (own_request[:, None] == key_request[None, :]) & (key_position[None, :] <= own_position[:, None])
    ratio = QH // KVH
    key_wide = jnp.repeat(key_block, ratio, axis=1).astype(jnp.float32)
    value_wide = jnp.repeat(value_block, ratio, axis=1).astype(jnp.float32)
    scores = jnp.einsum('qhd,khd->hqk', query_block.astype(jnp.float32), key_wide, precision=lax.Precision.HIGHEST) * HD ** (-0.5)
    scores = jnp.where(visible[None], scores, -1e+30)
    row_peak = lax.optimization_barrier(jnp.max(scores, axis=-1, keepdims=True))
    probs = jnp.where(visible[None], jnp.exp(scores - row_peak), 0.0)
    total = lax.optimization_barrier(jnp.sum(probs, axis=-1, keepdims=True))
    rounded = lax.optimization_barrier(probs.astype(jnp.bfloat16)).astype(jnp.float32)
    mixed_heads = jnp.einsum('hqk,khd->qhd', rounded, value_wide, precision=lax.Precision.HIGHEST) / jnp.transpose(total, (1, 0, 2))
    return mixed_heads.astype(jnp.bfloat16).reshape(TOK_GRP, QH * HD)

def reference(hidden, request_of, positions, page_table, attn_gain, mlp_gain, wq, wk, wv, wo, w_gate, w_up, w_down):
    query_w = wq.astype(jnp.bfloat16)
    key_w = wk.astype(jnp.bfloat16)
    value_w = wv.astype(jnp.bfloat16)
    out_w = wo.astype(jnp.bfloat16)
    gate_w = w_gate.astype(jnp.bfloat16)
    up_w = w_up.astype(jnp.bfloat16)
    down_w = w_down.astype(jnp.bfloat16)
    residual = hidden.astype(jnp.float32)
    normed = rms_scale(residual, attn_gain)
    query_raw = jnp.dot(normed, query_w, preferred_element_type=jnp.float32).astype(jnp.bfloat16).reshape(TOKENS, QH, HD)
    key_raw = jnp.dot(normed, key_w, preferred_element_type=jnp.float32).astype(jnp.bfloat16).reshape(TOKENS, KVH, HD)
    value_rows = jnp.dot(normed, value_w, preferred_element_type=jnp.float32).astype(jnp.bfloat16).reshape(TOKENS, KVH, HD)
    queries = rotate(query_raw, positions)
    keys = rotate(key_raw, positions)

    def one_group(index):
        return attend_group(index, queries, keys, value_rows, request_of, positions)
    attended = lax.map(one_group, jnp.arange(N_GROUP, dtype=jnp.int32)).reshape(TOKENS, QH * HD)
    mixed = residual + jnp.dot(attended, out_w, preferred_element_type=jnp.float32)
    normed_mlp = rms_scale(mixed, mlp_gain)
    gate = jnp.dot(normed_mlp, gate_w, preferred_element_type=jnp.float32)
    upward = jnp.dot(normed_mlp, up_w, preferred_element_type=jnp.float32)
    activation = (jax.nn.silu(gate) * upward).astype(jnp.bfloat16)
    layer_out = (mixed + jnp.dot(activation, down_w, preferred_element_type=jnp.float32)).astype(jnp.bfloat16)
    rows = jnp.arange(TOKENS, dtype=jnp.int32)
    changed = jnp.concatenate([jnp.ones((1,), dtype=bool), request_of[1:] != request_of[:-1]])
    opens = changed | (rows % TOK_GRP == 0) | (positions % PAGE == 0)
    logical = (jnp.cumsum(opens.reshape(N_GROUP, TOK_GRP).astype(jnp.int32), axis=1) - 1).astype(jnp.int32)
    chosen = jnp.take_along_axis(page_table, logical, axis=1).astype(jnp.int32)
    owner = (rows // TOK_GRP).reshape(N_GROUP, TOK_GRP).astype(jnp.int32)
    slots = (positions % PAGE).reshape(N_GROUP, TOK_GRP).astype(jnp.int32)
    target = ((owner * PAGES_GRP + chosen) * PAGE + slots).reshape(TOKENS).astype(jnp.int32)
    kv_rows = jnp.stack([keys, value_rows], axis=2).reshape(TOKENS, KVH * 2 * HD)
    cache = jnp.zeros((N_GROUP * PAGES_GRP * PAGE, KVH * 2 * HD), jnp.bfloat16).at[target].set(kv_rows)
    return (layer_out, cache.reshape(N_GROUP * PAGES_GRP, PAGE, KVH * 2 * HD))
```

```python
import jax
import jax.numpy as jnp
from jax import lax
from jax.sharding import PartitionSpec as P

QH = 16
KVH = 8
HD = 128
PAGE = 128
MAXLEN = 512


rope_base = 1000000.0
norm_eps = 1e-06


def partner(value, axis, distance):
    mask = 2**distance
    pairs = [(source, source ^ mask) for source in range(lax.axis_size(axis))]
    return lax.ppermute(value, axis, pairs)


def from_behind(block, axis, distance):
    devices = range(lax.axis_size(axis))
    route = [(i - distance, i) for i in devices if i - distance in devices]
    return lax.ppermute(block, axis, route)


def rms_scale(values, gain):
    square = jnp.mean(values * values, axis=-1, keepdims=True)
    return (values * lax.rsqrt(square + norm_eps) * gain).astype(jnp.bfloat16)


def rotate(values, places):
    half_dim = values.shape[-1] // 2
    frequency = rope_base ** (-(jnp.arange(half_dim, dtype=jnp.float32) * 2.0 / values.shape[-1]))
    angle = places.astype(jnp.float32)[:, None] * frequency[None, :]
    cosine = jnp.cos(angle)[:, None, :]
    sine = jnp.sin(angle)[:, None, :]
    widened = values.astype(jnp.float32)
    first = widened[..., :half_dim]
    second = widened[..., half_dim:]
    return jnp.concatenate(
        [first * cosine - second * sine, second * cosine + first * sine], axis=-1
    ).astype(jnp.bfloat16)


def join_halves(own_part, other_part):
    even = lax.axis_index("tensor") % 2 == 0
    lower = jnp.where(even, own_part, other_part)
    upper = jnp.where(even, other_part, own_part)
    return jnp.concatenate([lower, upper], axis=-1)


def dot_t(acts, weight_t):
    return lax.dot_general(
        acts, weight_t, (((1,), (1,)), ((), ())), preferred_element_type=jnp.float32
    )


def body(
    hidden,
    request_of,
    positions,
    page_table,
    attn_gain,
    mlp_gain,
    wq,
    wk,
    wv,
    wo,
    w_gate,
    w_up,
    w_down,
):
    tensor_count = lax.axis_size("tensor")
    tok_group = request_of.shape[0]
    query_heads = QH // tensor_count
    key_heads = max(1, KVH // tensor_count)
    group_ratio = QH // KVH
    bf = jnp.bfloat16
    residual = hidden.astype(jnp.float32)
    normed = lax.all_gather(rms_scale(residual, attn_gain), "tensor", axis=0, tiled=True)
    key_rows = wk.astype(bf)
    value_rows = wv.astype(bf)
    other_key, other_value = partner((key_rows, value_rows), "tensor", 0)
    key_rows = join_halves(key_rows, other_key)
    value_rows = join_halves(value_rows, other_value)
    q_cols = query_heads * HD
    kv_cols = key_heads * HD
    attn_w = jnp.concatenate([wq.astype(bf), key_rows, value_rows, wo.astype(bf).T], axis=1)
    attn_w = lax.all_gather(attn_w, "group", axis=0, tiled=True)
    query_w = attn_w[:, :q_cols]
    key_w = attn_w[:, q_cols : q_cols + kv_cols]
    value_w = attn_w[:, q_cols + kv_cols : q_cols + 2 * kv_cols]
    out_w_t = attn_w[:, q_cols + 2 * kv_cols :]
    ff_cols = w_gate.shape[1]
    mlp_w = jnp.concatenate([w_gate.astype(bf), w_up.astype(bf), w_down.astype(bf).T], axis=1)
    mlp_w = lax.all_gather(mlp_w, "group", axis=0, tiled=True)
    gate_w = mlp_w[:, :ff_cols]
    up_w = mlp_w[:, ff_cols : 2 * ff_cols]
    down_w_t = mlp_w[:, 2 * ff_cols :]
    query_raw = jnp.dot(normed, query_w, preferred_element_type=jnp.float32).astype(bf)
    key_raw = jnp.dot(normed, key_w, preferred_element_type=jnp.float32).astype(bf)
    value_raw = jnp.dot(normed, value_w, preferred_element_type=jnp.float32).astype(bf)
    queries = rotate(query_raw.reshape(tok_group, query_heads, HD), positions)
    keys = rotate(key_raw.reshape(tok_group, key_heads, HD), positions)
    values = value_raw.reshape(tok_group, key_heads, HD)
    kv_rows = jnp.stack([keys, values], axis=2)
    earlier_rows = min(MAXLEN, tok_group)
    earlier = from_behind(kv_rows[tok_group - earlier_rows :], "group", 1)
    all_rows = jnp.concatenate([earlier, kv_rows], axis=0)
    all_keys = jnp.repeat(all_rows[:, :, 0], group_ratio, axis=1)[:, :query_heads]
    all_values = jnp.repeat(all_rows[:, :, 1], group_ratio, axis=1)[:, :query_heads]
    first_request = request_of[0]
    first_position = positions[0]
    same_local = (request_of[:, None] == request_of[None, :]) & (
        positions[None, :] <= positions[:, None]
    )
    same_earlier = (request_of[:, None] == first_request) & (
        jnp.arange(earlier_rows)[None, :] >= earlier_rows - first_position
    )
    visible = jnp.concatenate([same_earlier, same_local], axis=1)
    scores = jnp.einsum(
        "qhd,khd->hqk", queries, all_keys, preferred_element_type=jnp.float32
    ) * HD ** (-0.5)
    scores = jnp.where(visible[None], scores, -1e30)
    row_peak = jnp.max(scores, axis=-1, keepdims=True)
    probs = jnp.where(visible[None], jnp.exp(scores - row_peak), 0.0)
    total = jnp.sum(probs, axis=-1, keepdims=True)
    mixed_heads = jnp.einsum(
        "hqk,khd->qhd", probs.astype(bf), all_values, preferred_element_type=jnp.float32
    ) / jnp.transpose(total, (1, 0, 2))
    attended = mixed_heads.astype(bf).reshape(tok_group, query_heads * HD)
    attn_part = dot_t(attended, out_w_t)
    attn_sum = lax.psum_scatter(attn_part.astype(bf), "tensor", scatter_dimension=0, tiled=True)
    mixed = residual + attn_sum.astype(jnp.float32)
    normed_mlp = lax.all_gather(rms_scale(mixed, mlp_gain), "tensor", axis=0, tiled=True)
    gate_sum = jnp.dot(normed_mlp, gate_w, preferred_element_type=jnp.float32)
    up_sum = jnp.dot(normed_mlp, up_w, preferred_element_type=jnp.float32)
    activation = (jax.nn.silu(gate_sum) * up_sum).astype(bf)
    down_part = dot_t(activation, down_w_t)
    summed = lax.psum_scatter(down_part.astype(bf), "tensor", scatter_dimension=0, tiled=True)
    layer_out = (mixed + summed.astype(jnp.float32)).astype(bf)
    pages = page_table.shape[1]
    changed = jnp.concatenate(
        [jnp.ones((1,), jnp.int32), (request_of[1:] != request_of[:-1]).astype(jnp.int32)]
    )
    opens = jnp.maximum(changed, (positions % PAGE == 0).astype(jnp.int32))
    logical = jnp.cumsum(opens) - 1
    chosen = jnp.sum(
        jnp.where(logical[:, None] == jnp.arange(pages)[None, :], page_table, 0), axis=1
    )
    target = chosen * PAGE + positions % PAGE
    width = 2 * KVH * HD // tensor_count
    flat_rows = kv_rows.reshape(tok_group, key_heads * 2 * HD)
    offset = lax.axis_index("tensor") * width % (key_heads * 2 * HD)
    own_slice = lax.dynamic_slice_in_dim(flat_rows, offset, width, 1)
    cache = jnp.zeros((pages * PAGE, width), jnp.bfloat16).at[target].set(own_slice)
    return (layer_out, cache.reshape(pages, PAGE, width))


def solution(mesh):
    placed = (
        P(("group", "tensor"), None),
        P("group"),
        P("group"),
        P("group", None),
        P(),
        P(),
        P("group", "tensor"),
        P("group", "tensor"),
        P("group", "tensor"),
        P("tensor", "group"),
        P("group", "tensor"),
        P("group", "tensor"),
        P("tensor", "group"),
    )
    return jax.shard_map(
        body,
        mesh=mesh,
        in_specs=placed,
        out_specs=(P(("group", "tensor"), None), P("group", None, "tensor")),
        check_vma=False,
    )
```

```python
import jax
import jax.numpy as jnp
from jax import lax
from jax.sharding import PartitionSpec as P

QH = 16
KVH = 8
HD = 128
PAGE = 128
MAXLEN = 512


rope_base = 1000000.0
norm_eps = 1e-06


def partner(value, axis, distance):
    mask = 2**distance
    pairs = [(source, source ^ mask) for source in range(lax.axis_size(axis))]
    return lax.ppermute(value, axis, pairs)


def from_behind(block, axis, distance):
    devices = range(lax.axis_size(axis))
    route = [(i - distance, i) for i in devices if i - distance in devices]
    return lax.ppermute(block, axis, route)


def gather_group(block):
    count = lax.axis_size("group")
    pieces = [block]
    for shift in range(1, count):
        route = [(source, (source + shift) % count) for source in range(count)]
        pieces.append(lax.ppermute(block, "group", route))
    stacked = jnp.stack(pieces)
    order = (lax.axis_index("group") - jnp.arange(count)) % count
    return jnp.take(stacked, order, axis=0).reshape(count * block.shape[0], block.shape[1])


def rms_scale(values, gain):
    square = jnp.mean(values * values, axis=-1, keepdims=True)
    return (values * lax.rsqrt(square + norm_eps) * gain).astype(jnp.bfloat16)


def rotate(values, places):
    half_dim = values.shape[-1] // 2
    frequency = rope_base ** (-(jnp.arange(half_dim, dtype=jnp.float32) * 2.0 / values.shape[-1]))
    angle = places.astype(jnp.float32)[:, None] * frequency[None, :]
    cosine = jnp.cos(angle)[:, None, :]
    sine = jnp.sin(angle)[:, None, :]
    widened = values.astype(jnp.float32)
    first = widened[..., :half_dim]
    second = widened[..., half_dim:]
    return jnp.concatenate(
        [first * cosine - second * sine, second * cosine + first * sine], axis=-1
    ).astype(jnp.bfloat16)


def join_halves(own_part, other_part):
    even = lax.axis_index("tensor") % 2 == 0
    lower = jnp.where(even, own_part, other_part)
    upper = jnp.where(even, other_part, own_part)
    return jnp.concatenate([lower, upper], axis=-1)


def dot_t(acts, weight_t):
    return lax.dot_general(
        acts, weight_t, (((1,), (1,)), ((), ())), preferred_element_type=jnp.float32
    )


def body(
    hidden,
    request_of,
    positions,
    page_table,
    attn_gain,
    mlp_gain,
    wq,
    wk,
    wv,
    wo,
    w_gate,
    w_up,
    w_down,
):
    tensor_count = lax.axis_size("tensor")
    tok_group = request_of.shape[0]
    query_heads = QH // tensor_count
    key_heads = max(1, KVH // tensor_count)
    group_ratio = QH // KVH
    bf = jnp.bfloat16
    residual = hidden.astype(jnp.float32)
    normed = lax.all_gather(rms_scale(residual, attn_gain), "tensor", axis=0, tiled=True)
    key_rows = wk.astype(bf)
    value_rows = wv.astype(bf)
    other_key, other_value = partner((key_rows, value_rows), "tensor", 0)
    key_rows = join_halves(key_rows, other_key)
    value_rows = join_halves(value_rows, other_value)
    q_cols = query_heads * HD
    kv_cols = key_heads * HD
    attn_w = jnp.concatenate([wq.astype(bf), key_rows, value_rows, wo.astype(bf).T], axis=1)
    attn_w = gather_group(attn_w)
    query_w = attn_w[:, :q_cols]
    key_w = attn_w[:, q_cols : q_cols + kv_cols]
    value_w = attn_w[:, q_cols + kv_cols : q_cols + 2 * kv_cols]
    out_w_t = attn_w[:, q_cols + 2 * kv_cols :]
    ff_cols = w_gate.shape[1]
    mlp_w = jnp.concatenate([w_gate.astype(bf), w_up.astype(bf), w_down.astype(bf).T], axis=1)
    mlp_w = gather_group(mlp_w)
    gate_w = mlp_w[:, :ff_cols]
    up_w = mlp_w[:, ff_cols : 2 * ff_cols]
    down_w_t = mlp_w[:, 2 * ff_cols :]
    query_raw = jnp.dot(normed, query_w, preferred_element_type=jnp.float32).astype(bf)
    key_raw = jnp.dot(normed, key_w, preferred_element_type=jnp.float32).astype(bf)
    value_raw = jnp.dot(normed, value_w, preferred_element_type=jnp.float32).astype(bf)
    queries = rotate(query_raw.reshape(tok_group, query_heads, HD), positions)
    keys = rotate(key_raw.reshape(tok_group, key_heads, HD), positions)
    values = value_raw.reshape(tok_group, key_heads, HD)
    kv_rows = jnp.stack([keys, values], axis=2)
    earlier_rows = min(MAXLEN, tok_group)
    earlier = from_behind(kv_rows[tok_group - earlier_rows :], "group", 1)
    all_rows = jnp.concatenate([earlier, kv_rows], axis=0)
    all_keys = jnp.repeat(all_rows[:, :, 0], group_ratio, axis=1)[:, :query_heads]
    all_values = jnp.repeat(all_rows[:, :, 1], group_ratio, axis=1)[:, :query_heads]
    first_request = request_of[0]
    first_position = positions[0]
    same_local = (request_of[:, None] == request_of[None, :]) & (
        positions[None, :] <= positions[:, None]
    )
    same_earlier = (request_of[:, None] == first_request) & (
        jnp.arange(earlier_rows)[None, :] >= earlier_rows - first_position
    )
    visible = jnp.concatenate([same_earlier, same_local], axis=1)
    scores = jnp.einsum(
        "qhd,khd->hqk", queries, all_keys, preferred_element_type=jnp.float32
    ) * HD ** (-0.5)
    scores = jnp.where(visible[None], scores, -1e30)
    row_peak = jnp.max(scores, axis=-1, keepdims=True)
    probs = jnp.where(visible[None], jnp.exp(scores - row_peak), 0.0)
    total = jnp.sum(probs, axis=-1, keepdims=True)
    mixed_heads = jnp.einsum(
        "hqk,khd->qhd", probs.astype(bf), all_values, preferred_element_type=jnp.float32
    ) / jnp.transpose(total, (1, 0, 2))
    attended = mixed_heads.astype(bf).reshape(tok_group, query_heads * HD)
    attn_part = dot_t(attended, out_w_t)
    attn_sum = lax.psum_scatter(attn_part.astype(bf), "tensor", scatter_dimension=0, tiled=True)
    mixed = residual + attn_sum.astype(jnp.float32)
    normed_mlp = lax.all_gather(rms_scale(mixed, mlp_gain), "tensor", axis=0, tiled=True)
    gate_sum = jnp.dot(normed_mlp, gate_w, preferred_element_type=jnp.float32)
    up_sum = jnp.dot(normed_mlp, up_w, preferred_element_type=jnp.float32)
    activation = (jax.nn.silu(gate_sum) * up_sum).astype(bf)
    down_part = dot_t(activation, down_w_t)
    summed = lax.psum_scatter(down_part.astype(bf), "tensor", scatter_dimension=0, tiled=True)
    layer_out = (mixed + summed.astype(jnp.float32)).astype(bf)
    pages = page_table.shape[1]
    changed = jnp.concatenate(
        [jnp.ones((1,), jnp.int32), (request_of[1:] != request_of[:-1]).astype(jnp.int32)]
    )
    opens = jnp.maximum(changed, (positions % PAGE == 0).astype(jnp.int32))
    logical = jnp.cumsum(opens) - 1
    chosen = jnp.sum(
        jnp.where(logical[:, None] == jnp.arange(pages)[None, :], page_table, 0), axis=1
    )
    target = chosen * PAGE + positions % PAGE
    width = 2 * KVH * HD // tensor_count
    flat_rows = kv_rows.reshape(tok_group, key_heads * 2 * HD)
    offset = lax.axis_index("tensor") * width % (key_heads * 2 * HD)
    own_slice = lax.dynamic_slice_in_dim(flat_rows, offset, width, 1)
    cache = jnp.zeros((pages * PAGE, width), jnp.bfloat16).at[target].set(own_slice)
    return (layer_out, cache.reshape(pages, PAGE, width))


def solution(mesh):
    placed = (
        P(("group", "tensor"), None),
        P("group"),
        P("group"),
        P("group", None),
        P(),
        P(),
        P("group", "tensor"),
        P("group", "tensor"),
        P("group", "tensor"),
        P("tensor", "group"),
        P("group", "tensor"),
        P("group", "tensor"),
        P("tensor", "group"),
    )
    return jax.shard_map(
        body,
        mesh=mesh,
        in_specs=placed,
        out_specs=(P(("group", "tensor"), None), P("group", None, "tensor")),
        check_vma=False,
    )
```

```python
import jax
import jax.numpy as jnp
from jax import lax
from jax.sharding import Mesh
from jax.sharding import PartitionSpec as P

QH = 16
KVH = 8
HD = 128
PAGE = 128
MAXLEN = 512


rope_base = 1000000.0
norm_eps = 1e-06


def swap_cores(value):
    return lax.ppermute(value, "core", [(0, 1), (1, 0)])


def from_behind(block, axis, distance):
    devices = range(lax.axis_size(axis))
    route = [(i - distance, i) for i in devices if i - distance in devices]
    return lax.ppermute(block, axis, route)


def gather_group(block):
    count = lax.axis_size("group")
    pieces = [block]
    for shift in range(1, count):
        route = [(source, (source + shift) % count) for source in range(count)]
        pieces.append(lax.ppermute(block, "group", route))
    stacked = jnp.stack(pieces)
    order = (lax.axis_index("group") - jnp.arange(count)) % count
    return jnp.take(stacked, order, axis=0).reshape(count * block.shape[0], block.shape[1])


def rms_scale(values, gain):
    square = jnp.mean(values * values, axis=-1, keepdims=True)
    return (values * lax.rsqrt(square + norm_eps) * gain).astype(jnp.bfloat16)


def rotate(values, places):
    half_dim = values.shape[-1] // 2
    frequency = rope_base ** (-(jnp.arange(half_dim, dtype=jnp.float32) * 2.0 / values.shape[-1]))
    angle = places.astype(jnp.float32)[:, None] * frequency[None, :]
    cosine = jnp.cos(angle)[:, None, :]
    sine = jnp.sin(angle)[:, None, :]
    widened = values.astype(jnp.float32)
    first = widened[..., :half_dim]
    second = widened[..., half_dim:]
    return jnp.concatenate(
        [first * cosine - second * sine, second * cosine + first * sine], axis=-1
    ).astype(jnp.bfloat16)


def by_core(own_part, other_part):
    first = lax.axis_index("core") == 0
    return jnp.where(first, own_part, other_part), jnp.where(first, other_part, own_part)


def dot(acts, weight):
    return jnp.dot(acts, weight, preferred_element_type=jnp.float32)


def dot_t(acts, weight_t):
    return lax.dot_general(
        acts, weight_t, (((1,), (1,)), ((), ())), preferred_element_type=jnp.float32
    )


def core_rows(values, chips, rows_dev):
    blocks = values.reshape(chips, 2, rows_dev, *values.shape[1:])
    own = lax.dynamic_index_in_dim(blocks, lax.axis_index("core"), axis=1, keepdims=False)
    return own.reshape(chips * rows_dev, *values.shape[1:])


def body(
    hidden,
    request_of,
    positions,
    page_table,
    attn_gain,
    mlp_gain,
    wq,
    wk,
    wv,
    wo,
    w_gate,
    w_up,
    w_down,
):
    chips = lax.axis_size("chip")
    rows_dev = hidden.shape[0]
    tok_group = request_of.shape[0]
    bf = jnp.bfloat16
    residual = hidden.astype(jnp.float32)
    normed = lax.all_gather(rms_scale(residual, attn_gain), "chip", axis=0, tiled=True)
    q_cols = wq.shape[1]
    kv_half = wk.shape[1]
    own_attn = jnp.concatenate([wq.astype(bf), wk.astype(bf), wv.astype(bf), wo.astype(bf).T], axis=1)
    own_attn = gather_group(own_attn)
    other_attn = swap_cores(own_attn)
    query_w = jnp.concatenate([own_attn[:, :q_cols], other_attn[:, :q_cols]], axis=1)
    out_w_t = jnp.concatenate(
        [own_attn[:, q_cols + 2 * kv_half :], other_attn[:, q_cols + 2 * kv_half :]], axis=1
    )
    key_lo, key_hi = by_core(own_attn[:, q_cols : q_cols + kv_half], other_attn[:, q_cols : q_cols + kv_half])
    value_lo, value_hi = by_core(
        own_attn[:, q_cols + kv_half : q_cols + 2 * kv_half],
        other_attn[:, q_cols + kv_half : q_cols + 2 * kv_half],
    )
    key_w = jnp.concatenate([key_lo, key_hi], axis=1)
    value_w = jnp.concatenate([value_lo, value_hi], axis=1)
    ff_cols = w_gate.shape[1]
    own_mlp = jnp.concatenate([w_gate.astype(bf), w_up.astype(bf), w_down.astype(bf).T], axis=1)
    own_mlp = gather_group(own_mlp)
    other_mlp = swap_cores(own_mlp)
    half_pos = core_rows(positions, chips, rows_dev)
    half_req = core_rows(request_of, chips, rows_dev)
    heads = 2 * q_cols // HD
    queries = rotate(dot(normed, query_w).astype(bf).reshape(-1, heads, HD), half_pos)
    keys_half = rotate(dot(normed, key_w).astype(bf).reshape(-1, 1, HD), half_pos)
    values_half = dot(normed, value_w).astype(bf).reshape(-1, 1, HD)
    kv_own = jnp.stack([keys_half[:, 0], values_half[:, 0]], axis=1)
    kv_other = swap_cores(kv_own)
    kv_lo, kv_hi = by_core(kv_own, kv_other)
    kv_rows = jnp.stack(
        [kv_lo.reshape(chips, rows_dev, 2, HD), kv_hi.reshape(chips, rows_dev, 2, HD)], axis=1
    ).reshape(tok_group, 2, HD)
    earlier_rows = min(MAXLEN, tok_group)
    earlier = from_behind(kv_rows[tok_group - earlier_rows :], "group", 1)
    all_rows = jnp.concatenate([earlier, kv_rows], axis=0)
    all_keys = all_rows[:, 0]
    all_values = all_rows[:, 1]
    first_request = request_of[0]
    first_position = positions[0]
    same_local = (half_req[:, None] == request_of[None, :]) & (
        positions[None, :] <= half_pos[:, None]
    )
    same_earlier = (half_req[:, None] == first_request) & (
        jnp.arange(earlier_rows)[None, :] >= earlier_rows - first_position
    )
    visible = jnp.concatenate([same_earlier, same_local], axis=1)
    scores = jnp.einsum(
        "qhd,kd->hqk", queries, all_keys, preferred_element_type=jnp.float32
    ) * HD ** (-0.5)
    scores = jnp.where(visible[None], scores, -1e30)
    row_peak = jnp.max(scores, axis=-1, keepdims=True)
    probs = jnp.where(visible[None], jnp.exp(scores - row_peak), 0.0)
    total = jnp.sum(probs, axis=-1, keepdims=True)
    mixed_heads = jnp.einsum(
        "hqk,kd->qhd", probs.astype(bf), all_values, preferred_element_type=jnp.float32
    ) / jnp.transpose(total, (1, 0, 2))
    attended = mixed_heads.astype(bf).reshape(-1, heads * HD)
    attn_part = dot_t(attended, out_w_t)
    attn_sum = lax.psum_scatter(attn_part.astype(bf), "chip", scatter_dimension=0, tiled=True)
    mixed = residual + attn_sum.astype(jnp.float32)
    normed_mlp = lax.all_gather(rms_scale(mixed, mlp_gain), "chip", axis=0, tiled=True)
    gate_sum = jnp.concatenate(
        [dot(normed_mlp, own_mlp[:, :ff_cols]), dot(normed_mlp, other_mlp[:, :ff_cols])], axis=1
    )
    up_sum = jnp.concatenate(
        [
            dot(normed_mlp, own_mlp[:, ff_cols : 2 * ff_cols]),
            dot(normed_mlp, other_mlp[:, ff_cols : 2 * ff_cols]),
        ],
        axis=1,
    )
    activation = (jax.nn.silu(gate_sum) * up_sum).astype(bf)
    down_w_t = jnp.concatenate([own_mlp[:, 2 * ff_cols :], other_mlp[:, 2 * ff_cols :]], axis=1)
    down_part = dot_t(activation, down_w_t)
    summed = lax.psum_scatter(down_part.astype(bf), "chip", scatter_dimension=0, tiled=True)
    layer_out = (mixed + summed.astype(jnp.float32)).astype(bf)
    pages = page_table.shape[1]
    changed = jnp.concatenate(
        [jnp.ones((1,), jnp.int32), (request_of[1:] != request_of[:-1]).astype(jnp.int32)]
    )
    opens = jnp.maximum(changed, (positions % PAGE == 0).astype(jnp.int32))
    logical = jnp.cumsum(opens) - 1
    chosen = jnp.sum(
        jnp.where(logical[:, None] == jnp.arange(pages)[None, :], page_table, 0), axis=1
    )
    target = chosen * PAGE + positions % PAGE
    own_slice = lax.dynamic_index_in_dim(kv_rows, lax.axis_index("core"), axis=1, keepdims=False)
    width = own_slice.shape[1]
    cache = jnp.zeros((pages * PAGE, width), jnp.bfloat16).at[target].set(own_slice)
    return (layer_out, cache.reshape(pages, PAGE, width))


def solution(mesh):
    groups, tensors = mesh.devices.shape
    split = Mesh(mesh.devices.reshape(groups, tensors // 2, 2), ("group", "chip", "core"))
    tensor = ("chip", "core")
    placed = (
        P(("group",) + tensor, None),
        P("group"),
        P("group"),
        P("group", None),
        P(),
        P(),
        P("group", tensor),
        P("group", tensor),
        P("group", tensor),
        P(tensor, "group"),
        P("group", tensor),
        P("group", tensor),
        P(tensor, "group"),
    )
    return jax.shard_map(
        body,
        mesh=split,
        in_specs=placed,
        out_specs=(P(("group",) + tensor, None), P("group", None, tensor)),
        check_vma=False,
    )
```

```python
import functools

import jax
import jax.numpy as jnp
from jax import lax
from jax.experimental import pallas as pl
from jax.experimental.pallas import tpu as pltpu
from jax.sharding import Mesh
from jax.sharding import PartitionSpec as P

QH = 16
KVH = 8
HD = 128
PAGE = 128
MAXLEN = 512


rope_base = 1000000.0
norm_eps = 1e-06


def swap_cores(value):
    return lax.ppermute(value, "core", [(0, 1), (1, 0)])


def from_behind(block, axis, distance):
    devices = range(lax.axis_size(axis))
    route = [(i - distance, i) for i in devices if i - distance in devices]
    return lax.ppermute(block, axis, route)


def exchange_kernel(count, spread, source, slots, send_sems, recv_sems, local_sem):
    me = lax.axis_index("chip")
    group = lax.axis_index("group")
    core = lax.axis_index("core")
    mesh_ids = pl.DeviceIdType.MESH
    barrier = pltpu.get_barrier_semaphore()
    for shift in range(1, count):
        peer = lax.rem(me + shift, count)
        pl.semaphore_signal(barrier, inc=1, device_id=(group, peer, core), device_id_type=mesh_ids)
    pl.semaphore_wait(barrier, count - 1)
    local = pltpu.make_async_copy(source.at[me] if spread else source, slots.at[me], local_sem)
    local.start()
    copies = []
    for shift in range(1, count):
        peer = lax.rem(me + shift, count)
        copy = pltpu.make_async_remote_copy(
            src_ref=source.at[peer] if spread else source,
            dst_ref=slots.at[me],
            send_sem=send_sems.at[shift],
            recv_sem=recv_sems.at[shift],
            device_id=(group, peer, core),
            device_id_type=mesh_ids,
        )
        copy.start()
        copies.append(copy)
    for shift in range(1, count):
        sender = lax.rem(me + count - shift, count)
        arrival = pltpu.make_async_remote_copy(
            src_ref=slots.at[sender],
            dst_ref=slots.at[sender],
            send_sem=send_sems.at[shift],
            recv_sem=recv_sems.at[shift],
            device_id=(group, sender, core),
            device_id_type=mesh_ids,
        )
        arrival.wait_recv()
    for copy in copies:
        copy.wait_send()
    local.wait()


def exchange(block, spread, tag):
    count = lax.axis_size("chip")
    rows, cols = block.shape[-2:]
    moved = count * rows * cols * block.dtype.itemsize
    return pl.pallas_call(
        functools.partial(exchange_kernel, count, spread),
        out_shape=jax.ShapeDtypeStruct((count, rows, cols), block.dtype),
        in_specs=[pl.BlockSpec(memory_space=pl.ANY)],
        out_specs=pl.BlockSpec(memory_space=pl.ANY),
        scratch_shapes=[
            pltpu.SemaphoreType.DMA((count,)),
            pltpu.SemaphoreType.DMA((count,)),
            pltpu.SemaphoreType.DMA(()),
        ],
        compiler_params=pltpu.CompilerParams(collective_id=tag, has_side_effects=True),
        cost_estimate=pl.CostEstimate(flops=0, bytes_accessed=2 * moved, transcendentals=0),
    )(block)


def gather_chip(block, tag):
    slots = exchange(block, False, tag)
    return slots.reshape(-1, block.shape[1])


def scatter_chip(partial, tag):
    count = lax.axis_size("chip")
    slots = exchange(partial.reshape(count, -1, partial.shape[1]), True, tag)
    return jnp.sum(slots.astype(jnp.float32), axis=0)


def gather_group(block):
    count = lax.axis_size("group")
    pieces = [block]
    for shift in range(1, count):
        route = [(source, (source + shift) % count) for source in range(count)]
        pieces.append(lax.ppermute(block, "group", route))
    stacked = jnp.stack(pieces)
    order = (lax.axis_index("group") - jnp.arange(count)) % count
    return jnp.take(stacked, order, axis=0).reshape(count * block.shape[0], block.shape[1])


def rms_scale(values, gain):
    square = jnp.mean(values * values, axis=-1, keepdims=True)
    return (values * lax.rsqrt(square + norm_eps) * gain).astype(jnp.bfloat16)


def rotate(values, places):
    half_dim = values.shape[-1] // 2
    frequency = rope_base ** (-(jnp.arange(half_dim, dtype=jnp.float32) * 2.0 / values.shape[-1]))
    angle = places.astype(jnp.float32)[:, None] * frequency[None, :]
    cosine = jnp.cos(angle)[:, None, :]
    sine = jnp.sin(angle)[:, None, :]
    widened = values.astype(jnp.float32)
    first = widened[..., :half_dim]
    second = widened[..., half_dim:]
    return jnp.concatenate(
        [first * cosine - second * sine, second * cosine + first * sine], axis=-1
    ).astype(jnp.bfloat16)


def by_core(own_part, other_part):
    first = lax.axis_index("core") == 0
    return jnp.where(first, own_part, other_part), jnp.where(first, other_part, own_part)


def dot(acts, weight):
    return jnp.dot(acts, weight, preferred_element_type=jnp.float32)


def dot_t(acts, weight_t):
    return lax.dot_general(
        acts, weight_t, (((1,), (1,)), ((), ())), preferred_element_type=jnp.float32
    )


def core_rows(values, chips, rows_dev):
    blocks = values.reshape(chips, 2, rows_dev, *values.shape[1:])
    own = lax.dynamic_index_in_dim(blocks, lax.axis_index("core"), axis=1, keepdims=False)
    return own.reshape(chips * rows_dev, *values.shape[1:])


def body(
    hidden,
    request_of,
    positions,
    page_table,
    attn_gain,
    mlp_gain,
    wq,
    wk,
    wv,
    wo,
    w_gate,
    w_up,
    w_down,
):
    chips = lax.axis_size("chip")
    rows_dev = hidden.shape[0]
    tok_group = request_of.shape[0]
    bf = jnp.bfloat16
    residual = hidden.astype(jnp.float32)
    normed = gather_chip(rms_scale(residual, attn_gain), 0)
    q_cols = wq.shape[1]
    kv_half = wk.shape[1]
    own_attn = jnp.concatenate([wq.astype(bf), wk.astype(bf), wv.astype(bf), wo.astype(bf).T], axis=1)
    own_attn = gather_group(own_attn)
    other_attn = swap_cores(own_attn)
    query_w = jnp.concatenate([own_attn[:, :q_cols], other_attn[:, :q_cols]], axis=1)
    out_w_t = jnp.concatenate(
        [own_attn[:, q_cols + 2 * kv_half :], other_attn[:, q_cols + 2 * kv_half :]], axis=1
    )
    key_lo, key_hi = by_core(own_attn[:, q_cols : q_cols + kv_half], other_attn[:, q_cols : q_cols + kv_half])
    value_lo, value_hi = by_core(
        own_attn[:, q_cols + kv_half : q_cols + 2 * kv_half],
        other_attn[:, q_cols + kv_half : q_cols + 2 * kv_half],
    )
    key_w = jnp.concatenate([key_lo, key_hi], axis=1)
    value_w = jnp.concatenate([value_lo, value_hi], axis=1)
    ff_cols = w_gate.shape[1]
    own_mlp = jnp.concatenate([w_gate.astype(bf), w_up.astype(bf), w_down.astype(bf).T], axis=1)
    own_mlp = gather_group(own_mlp)
    other_mlp = swap_cores(own_mlp)
    half_pos = core_rows(positions, chips, rows_dev)
    half_req = core_rows(request_of, chips, rows_dev)
    heads = 2 * q_cols // HD
    queries = rotate(dot(normed, query_w).astype(bf).reshape(-1, heads, HD), half_pos)
    keys_half = rotate(dot(normed, key_w).astype(bf).reshape(-1, 1, HD), half_pos)
    values_half = dot(normed, value_w).astype(bf).reshape(-1, 1, HD)
    kv_own = jnp.stack([keys_half[:, 0], values_half[:, 0]], axis=1)
    kv_other = swap_cores(kv_own)
    kv_lo, kv_hi = by_core(kv_own, kv_other)
    kv_rows = jnp.stack(
        [kv_lo.reshape(chips, rows_dev, 2, HD), kv_hi.reshape(chips, rows_dev, 2, HD)], axis=1
    ).reshape(tok_group, 2, HD)
    earlier_rows = min(MAXLEN, tok_group)
    earlier = from_behind(kv_rows[tok_group - earlier_rows :], "group", 1)
    all_rows = jnp.concatenate([earlier, kv_rows], axis=0)
    all_keys = all_rows[:, 0]
    all_values = all_rows[:, 1]
    first_request = request_of[0]
    first_position = positions[0]
    same_local = (half_req[:, None] == request_of[None, :]) & (
        positions[None, :] <= half_pos[:, None]
    )
    same_earlier = (half_req[:, None] == first_request) & (
        jnp.arange(earlier_rows)[None, :] >= earlier_rows - first_position
    )
    visible = jnp.concatenate([same_earlier, same_local], axis=1)
    scores = jnp.einsum(
        "qhd,kd->hqk", queries, all_keys, preferred_element_type=jnp.float32
    ) * HD ** (-0.5)
    scores = jnp.where(visible[None], scores, -1e30)
    row_peak = jnp.max(scores, axis=-1, keepdims=True)
    probs = jnp.where(visible[None], jnp.exp(scores - row_peak), 0.0)
    total = jnp.sum(probs, axis=-1, keepdims=True)
    mixed_heads = jnp.einsum(
        "hqk,kd->qhd", probs.astype(bf), all_values, preferred_element_type=jnp.float32
    ) / jnp.transpose(total, (1, 0, 2))
    attended = mixed_heads.astype(bf).reshape(-1, heads * HD)
    attn_part = dot_t(attended, out_w_t)
    mixed = residual + scatter_chip(attn_part.astype(bf), 1)
    normed_mlp = gather_chip(rms_scale(mixed, mlp_gain), 2)
    gate_sum = jnp.concatenate(
        [dot(normed_mlp, own_mlp[:, :ff_cols]), dot(normed_mlp, other_mlp[:, :ff_cols])], axis=1
    )
    up_sum = jnp.concatenate(
        [
            dot(normed_mlp, own_mlp[:, ff_cols : 2 * ff_cols]),
            dot(normed_mlp, other_mlp[:, ff_cols : 2 * ff_cols]),
        ],
        axis=1,
    )
    activation = (jax.nn.silu(gate_sum) * up_sum).astype(bf)
    down_w_t = jnp.concatenate([own_mlp[:, 2 * ff_cols :], other_mlp[:, 2 * ff_cols :]], axis=1)
    down_part = dot_t(activation, down_w_t)
    layer_out = (mixed + scatter_chip(down_part.astype(bf), 3)).astype(bf)
    pages = page_table.shape[1]
    changed = jnp.concatenate(
        [jnp.ones((1,), jnp.int32), (request_of[1:] != request_of[:-1]).astype(jnp.int32)]
    )
    opens = jnp.maximum(changed, (positions % PAGE == 0).astype(jnp.int32))
    logical = jnp.cumsum(opens) - 1
    chosen = jnp.sum(
        jnp.where(logical[:, None] == jnp.arange(pages)[None, :], page_table, 0), axis=1
    )
    target = chosen * PAGE + positions % PAGE
    own_slice = lax.dynamic_index_in_dim(kv_rows, lax.axis_index("core"), axis=1, keepdims=False)
    width = own_slice.shape[1]
    cache = jnp.zeros((pages * PAGE, width), jnp.bfloat16).at[target].set(own_slice)
    return (layer_out, cache.reshape(pages, PAGE, width))


def solution(mesh):
    groups, tensors = mesh.devices.shape
    split = Mesh(mesh.devices.reshape(groups, tensors // 2, 2), ("group", "chip", "core"))
    tensor = ("chip", "core")
    placed = (
        P(("group",) + tensor, None),
        P("group"),
        P("group"),
        P("group", None),
        P(),
        P(),
        P("group", tensor),
        P("group", tensor),
        P("group", tensor),
        P(tensor, "group"),
        P("group", tensor),
        P("group", tensor),
        P(tensor, "group"),
    )
    return jax.shard_map(
        body,
        mesh=split,
        in_specs=placed,
        out_specs=(P(("group",) + tensor, None), P("group", None, tensor)),
        check_vma=False,
    )
```

```python
import functools

import jax
import jax.numpy as jnp
from jax import lax
from jax.experimental import pallas as pl
from jax.experimental.pallas import tpu as pltpu
from jax.sharding import Mesh
from jax.sharding import PartitionSpec as P

QH = 16
KVH = 8
HD = 128
PAGE = 128
MAXLEN = 512


rope_base = 1000000.0
norm_eps = 1e-06


def swap_cores(value):
    return lax.ppermute(value, "core", [(0, 1), (1, 0)])


def from_behind(block, axis, distance):
    devices = range(lax.axis_size(axis))
    route = [(i - distance, i) for i in devices if i - distance in devices]
    return lax.ppermute(block, axis, route)


def exchange_kernel(count, spread, extra, *refs):
    if extra:
        source, weights, slots, weight_slots, send_sems, recv_sems, local_sem = refs
    else:
        source, slots, send_sems, recv_sems, local_sem = refs
    me = lax.axis_index("chip")
    group = lax.axis_index("group")
    core = lax.axis_index("core")
    groups = lax.axis_size("group")
    mesh_ids = pl.DeviceIdType.MESH
    barrier = pltpu.get_barrier_semaphore()
    for shift in range(1, count):
        peer = lax.rem(me + shift, count)
        pl.semaphore_signal(barrier, inc=1, device_id=(group, peer, core), device_id_type=mesh_ids)
    if extra:
        for shift in range(1, groups):
            peer = lax.rem(group + shift, groups)
            pl.semaphore_signal(barrier, inc=1, device_id=(peer, me, core), device_id_type=mesh_ids)
        pl.semaphore_wait(barrier, count - 1 + groups - 1)
    else:
        pl.semaphore_wait(barrier, count - 1)
    local = pltpu.make_async_copy(source.at[me] if spread else source, slots.at[me], local_sem.at[0])
    local.start()
    copies = [local]
    if extra:
        weight_local = pltpu.make_async_copy(weights, weight_slots.at[group], local_sem.at[1])
        weight_local.start()
        copies.append(weight_local)
        for shift in range(1, groups):
            peer = lax.rem(group + shift, groups)
            copy = pltpu.make_async_remote_copy(
                src_ref=weights,
                dst_ref=weight_slots.at[group],
                send_sem=send_sems.at[count + shift],
                recv_sem=recv_sems.at[count + shift],
                device_id=(peer, me, core),
                device_id_type=mesh_ids,
            )
            copy.start()
            copies.append(copy)
    for shift in range(1, count):
        peer = lax.rem(me + shift, count)
        copy = pltpu.make_async_remote_copy(
            src_ref=source.at[peer] if spread else source,
            dst_ref=slots.at[me],
            send_sem=send_sems.at[shift],
            recv_sem=recv_sems.at[shift],
            device_id=(group, peer, core),
            device_id_type=mesh_ids,
        )
        copy.start()
        copies.append(copy)
    for shift in range(1, count):
        sender = lax.rem(me + count - shift, count)
        pltpu.make_async_remote_copy(
            src_ref=slots.at[sender],
            dst_ref=slots.at[sender],
            send_sem=send_sems.at[shift],
            recv_sem=recv_sems.at[shift],
            device_id=(group, sender, core),
            device_id_type=mesh_ids,
        ).wait_recv()
    if extra:
        for shift in range(1, groups):
            sender = lax.rem(group + groups - shift, groups)
            pltpu.make_async_remote_copy(
                src_ref=weight_slots.at[sender],
                dst_ref=weight_slots.at[sender],
                send_sem=send_sems.at[count + shift],
                recv_sem=recv_sems.at[count + shift],
                device_id=(sender, me, core),
                device_id_type=mesh_ids,
            ).wait_recv()
    for copy in copies[:1 + extra]:
        copy.wait()
    for copy in copies[1 + extra:]:
        copy.wait_send()


def exchange(block, spread, tag, weights=None):
    count = lax.axis_size("chip")
    groups = lax.axis_size("group")
    rows, cols = block.shape[-2:]
    moved = count * rows * cols * block.dtype.itemsize
    out_shape = [jax.ShapeDtypeStruct((count, rows, cols), block.dtype)]
    operands = [block]
    extra = weights is not None
    if extra:
        out_shape.append(jax.ShapeDtypeStruct((groups,) + weights.shape, weights.dtype))
        operands.append(weights)
        moved += groups * weights.size * weights.dtype.itemsize
    outs = pl.pallas_call(
        functools.partial(exchange_kernel, count, spread, extra),
        out_shape=tuple(out_shape),
        in_specs=[pl.BlockSpec(memory_space=pl.ANY)] * len(operands),
        out_specs=tuple(pl.BlockSpec(memory_space=pl.ANY) for _ in out_shape),
        scratch_shapes=[
            pltpu.SemaphoreType.DMA((count + groups,)),
            pltpu.SemaphoreType.DMA((count + groups,)),
            pltpu.SemaphoreType.DMA((2,)),
        ],
        compiler_params=pltpu.CompilerParams(collective_id=tag, has_side_effects=True),
        cost_estimate=pl.CostEstimate(flops=0, bytes_accessed=2 * moved, transcendentals=0),
    )(*operands)
    return outs


def gather_chip(block, tag, weights=None):
    outs = exchange(block, False, tag, weights)
    rows = outs[0].reshape(-1, block.shape[1])
    if weights is None:
        return rows
    return rows, outs[1].reshape(-1, weights.shape[1])


def scatter_chip(partial, tag, weights=None):
    count = lax.axis_size("chip")
    outs = exchange(partial.reshape(count, -1, partial.shape[1]), True, tag, weights)
    summed = jnp.sum(outs[0].astype(jnp.float32), axis=0)
    if weights is None:
        return summed
    return summed, outs[1].reshape(-1, weights.shape[1])


def gather_group(block):
    count = lax.axis_size("group")
    pieces = [block]
    for shift in range(1, count):
        route = [(source, (source + shift) % count) for source in range(count)]
        pieces.append(lax.ppermute(block, "group", route))
    stacked = jnp.stack(pieces)
    order = (lax.axis_index("group") - jnp.arange(count)) % count
    return jnp.take(stacked, order, axis=0).reshape(count * block.shape[0], block.shape[1])


def rms_scale(values, gain):
    square = jnp.mean(values * values, axis=-1, keepdims=True)
    return (values * lax.rsqrt(square + norm_eps) * gain).astype(jnp.bfloat16)


def rotate(values, places):
    half_dim = values.shape[-1] // 2
    frequency = rope_base ** (-(jnp.arange(half_dim, dtype=jnp.float32) * 2.0 / values.shape[-1]))
    angle = places.astype(jnp.float32)[:, None] * frequency[None, :]
    cosine = jnp.cos(angle)[:, None, :]
    sine = jnp.sin(angle)[:, None, :]
    widened = values.astype(jnp.float32)
    first = widened[..., :half_dim]
    second = widened[..., half_dim:]
    return jnp.concatenate(
        [first * cosine - second * sine, second * cosine + first * sine], axis=-1
    ).astype(jnp.bfloat16)


def by_core(own_part, other_part):
    first = lax.axis_index("core") == 0
    return jnp.where(first, own_part, other_part), jnp.where(first, other_part, own_part)


def dot(acts, weight):
    return jnp.dot(acts, weight, preferred_element_type=jnp.float32)


def dot_t(acts, weight_t):
    return lax.dot_general(
        acts, weight_t, (((1,), (1,)), ((), ())), preferred_element_type=jnp.float32
    )


def core_rows(values, chips, rows_dev):
    blocks = values.reshape(chips, 2, rows_dev, *values.shape[1:])
    own = lax.dynamic_index_in_dim(blocks, lax.axis_index("core"), axis=1, keepdims=False)
    return own.reshape(chips * rows_dev, *values.shape[1:])


def body(
    hidden,
    request_of,
    positions,
    page_table,
    attn_gain,
    mlp_gain,
    wq,
    wk,
    wv,
    wo,
    w_gate,
    w_up,
    w_down,
):
    chips = lax.axis_size("chip")
    rows_dev = hidden.shape[0]
    tok_group = request_of.shape[0]
    bf = jnp.bfloat16
    residual = hidden.astype(jnp.float32)
    q_cols = wq.shape[1]
    kv_half = wk.shape[1]
    own_attn = jnp.concatenate([wq.astype(bf), wk.astype(bf), wv.astype(bf), wo.astype(bf).T], axis=1)
    normed, own_attn = gather_chip(rms_scale(residual, attn_gain), 0, own_attn)
    other_attn = swap_cores(own_attn)
    query_w = jnp.concatenate([own_attn[:, :q_cols], other_attn[:, :q_cols]], axis=1)
    out_w_t = jnp.concatenate(
        [own_attn[:, q_cols + 2 * kv_half :], other_attn[:, q_cols + 2 * kv_half :]], axis=1
    )
    key_lo, key_hi = by_core(own_attn[:, q_cols : q_cols + kv_half], other_attn[:, q_cols : q_cols + kv_half])
    value_lo, value_hi = by_core(
        own_attn[:, q_cols + kv_half : q_cols + 2 * kv_half],
        other_attn[:, q_cols + kv_half : q_cols + 2 * kv_half],
    )
    key_w = jnp.concatenate([key_lo, key_hi], axis=1)
    value_w = jnp.concatenate([value_lo, value_hi], axis=1)
    ff_cols = w_gate.shape[1]
    own_mlp = jnp.concatenate([w_gate.astype(bf), w_up.astype(bf), w_down.astype(bf).T], axis=1)
    half_pos = core_rows(positions, chips, rows_dev)
    half_req = core_rows(request_of, chips, rows_dev)
    heads = 2 * q_cols // HD
    queries = rotate(dot(normed, query_w).astype(bf).reshape(-1, heads, HD), half_pos)
    keys_half = rotate(dot(normed, key_w).astype(bf).reshape(-1, 1, HD), half_pos)
    values_half = dot(normed, value_w).astype(bf).reshape(-1, 1, HD)
    kv_own = jnp.stack([keys_half[:, 0], values_half[:, 0]], axis=1)
    kv_other = swap_cores(kv_own)
    kv_lo, kv_hi = by_core(kv_own, kv_other)
    kv_rows = jnp.stack(
        [kv_lo.reshape(chips, rows_dev, 2, HD), kv_hi.reshape(chips, rows_dev, 2, HD)], axis=1
    ).reshape(tok_group, 2, HD)
    earlier_rows = min(MAXLEN, tok_group)
    earlier = from_behind(kv_rows[tok_group - earlier_rows :], "group", 1)
    all_rows = jnp.concatenate([earlier, kv_rows], axis=0)
    all_keys = all_rows[:, 0]
    all_values = all_rows[:, 1]
    first_request = request_of[0]
    first_position = positions[0]
    same_local = (half_req[:, None] == request_of[None, :]) & (
        positions[None, :] <= half_pos[:, None]
    )
    same_earlier = (half_req[:, None] == first_request) & (
        jnp.arange(earlier_rows)[None, :] >= earlier_rows - first_position
    )
    visible = jnp.concatenate([same_earlier, same_local], axis=1)
    scores = jnp.einsum(
        "qhd,kd->hqk", queries, all_keys, preferred_element_type=jnp.float32
    ) * HD ** (-0.5)
    scores = jnp.where(visible[None], scores, -1e30)
    row_peak = jnp.max(scores, axis=-1, keepdims=True)
    probs = jnp.where(visible[None], jnp.exp(scores - row_peak), 0.0)
    total = jnp.sum(probs, axis=-1, keepdims=True)
    mixed_heads = jnp.einsum(
        "hqk,kd->qhd", probs.astype(bf), all_values, preferred_element_type=jnp.float32
    ) / jnp.transpose(total, (1, 0, 2))
    attended = mixed_heads.astype(bf).reshape(-1, heads * HD)
    attn_part = dot_t(attended, out_w_t)
    attn_sum, own_mlp = scatter_chip(attn_part.astype(bf), 1, own_mlp)
    other_mlp = swap_cores(own_mlp)
    mixed = residual + attn_sum
    normed_mlp = gather_chip(rms_scale(mixed, mlp_gain), 2)
    gate_sum = jnp.concatenate(
        [dot(normed_mlp, own_mlp[:, :ff_cols]), dot(normed_mlp, other_mlp[:, :ff_cols])], axis=1
    )
    up_sum = jnp.concatenate(
        [
            dot(normed_mlp, own_mlp[:, ff_cols : 2 * ff_cols]),
            dot(normed_mlp, other_mlp[:, ff_cols : 2 * ff_cols]),
        ],
        axis=1,
    )
    activation = (jax.nn.silu(gate_sum) * up_sum).astype(bf)
    down_w_t = jnp.concatenate([own_mlp[:, 2 * ff_cols :], other_mlp[:, 2 * ff_cols :]], axis=1)
    down_part = dot_t(activation, down_w_t)
    layer_out = (mixed + scatter_chip(down_part.astype(bf), 3)).astype(bf)
    pages = page_table.shape[1]
    changed = jnp.concatenate(
        [jnp.ones((1,), jnp.int32), (request_of[1:] != request_of[:-1]).astype(jnp.int32)]
    )
    opens = jnp.maximum(changed, (positions % PAGE == 0).astype(jnp.int32))
    logical = jnp.cumsum(opens) - 1
    chosen = jnp.sum(
        jnp.where(logical[:, None] == jnp.arange(pages)[None, :], page_table, 0), axis=1
    )
    target = chosen * PAGE + positions % PAGE
    own_slice = lax.dynamic_index_in_dim(kv_rows, lax.axis_index("core"), axis=1, keepdims=False)
    width = own_slice.shape[1]
    cache = jnp.zeros((pages * PAGE, width), jnp.bfloat16).at[target].set(own_slice)
    return (layer_out, cache.reshape(pages, PAGE, width))


def solution(mesh):
    groups, tensors = mesh.devices.shape
    split = Mesh(mesh.devices.reshape(groups, tensors // 2, 2), ("group", "chip", "core"))
    tensor = ("chip", "core")
    placed = (
        P(("group",) + tensor, None),
        P("group"),
        P("group"),
        P("group", None),
        P(),
        P(),
        P("group", tensor),
        P("group", tensor),
        P("group", tensor),
        P(tensor, "group"),
        P("group", tensor),
        P("group", tensor),
        P(tensor, "group"),
    )
    return jax.shard_map(
        body,
        mesh=split,
        in_specs=placed,
        out_specs=(P(("group",) + tensor, None), P("group", None, tensor)),
        check_vma=False,
    )
```

```python
import functools

import jax
import jax.numpy as jnp
from jax import lax
from jax.experimental import pallas as pl
from jax.experimental.pallas import tpu as pltpu
from jax.sharding import Mesh
from jax.sharding import PartitionSpec as P

QH = 16
KVH = 8
HD = 128
PAGE = 128
MAXLEN = 512


rope_base = 1000000.0
norm_eps = 1e-06


def swap_cores(value):
    return lax.ppermute(value, "core", [(0, 1), (1, 0)])


def from_behind(block, axis, distance):
    devices = range(lax.axis_size(axis))
    route = [(i - distance, i) for i in devices if i - distance in devices]
    return lax.ppermute(block, axis, route)


def exchange_kernel(count, spread, extra, *refs):
    if extra:
        source, weights, slots, weight_slots, send_sems, recv_sems, local_sem = refs
    else:
        source, slots, send_sems, recv_sems, local_sem = refs
    me = lax.axis_index("chip")
    group = lax.axis_index("group")
    core = lax.axis_index("core")
    groups = lax.axis_size("group")
    mesh_ids = pl.DeviceIdType.MESH
    barrier = pltpu.get_barrier_semaphore()
    for shift in range(1, count):
        peer = lax.rem(me + shift, count)
        pl.semaphore_signal(barrier, inc=1, device_id=(group, peer, core), device_id_type=mesh_ids)
    if extra:
        for shift in range(1, groups):
            peer = lax.rem(group + shift, groups)
            pl.semaphore_signal(barrier, inc=1, device_id=(peer, me, core), device_id_type=mesh_ids)
        pl.semaphore_wait(barrier, count - 1 + groups - 1)
    else:
        pl.semaphore_wait(barrier, count - 1)
    local = pltpu.make_async_copy(source.at[me] if spread else source, slots.at[me], local_sem.at[0])
    local.start()
    copies = [local]
    if extra:
        weight_local = pltpu.make_async_copy(weights, weight_slots.at[group], local_sem.at[1])
        weight_local.start()
        copies.append(weight_local)
        for shift in range(1, groups):
            peer = lax.rem(group + shift, groups)
            copy = pltpu.make_async_remote_copy(
                src_ref=weights,
                dst_ref=weight_slots.at[group],
                send_sem=send_sems.at[count + shift],
                recv_sem=recv_sems.at[count + shift],
                device_id=(peer, me, core),
                device_id_type=mesh_ids,
            )
            copy.start()
            copies.append(copy)
    for shift in range(1, count):
        peer = lax.rem(me + shift, count)
        copy = pltpu.make_async_remote_copy(
            src_ref=source.at[peer] if spread else source,
            dst_ref=slots.at[me],
            send_sem=send_sems.at[shift],
            recv_sem=recv_sems.at[shift],
            device_id=(group, peer, core),
            device_id_type=mesh_ids,
        )
        copy.start()
        copies.append(copy)
    for shift in range(1, count):
        sender = lax.rem(me + count - shift, count)
        pltpu.make_async_remote_copy(
            src_ref=slots.at[sender],
            dst_ref=slots.at[sender],
            send_sem=send_sems.at[shift],
            recv_sem=recv_sems.at[shift],
            device_id=(group, sender, core),
            device_id_type=mesh_ids,
        ).wait_recv()
    if extra:
        for shift in range(1, groups):
            sender = lax.rem(group + groups - shift, groups)
            pltpu.make_async_remote_copy(
                src_ref=weight_slots.at[sender],
                dst_ref=weight_slots.at[sender],
                send_sem=send_sems.at[count + shift],
                recv_sem=recv_sems.at[count + shift],
                device_id=(sender, me, core),
                device_id_type=mesh_ids,
            ).wait_recv()
    for copy in copies[:1 + extra]:
        copy.wait()
    for copy in copies[1 + extra:]:
        copy.wait_send()


def exchange(block, spread, tag, weights=None):
    count = lax.axis_size("chip")
    groups = lax.axis_size("group")
    rows, cols = block.shape[-2:]
    moved = count * rows * cols * block.dtype.itemsize
    out_shape = [jax.ShapeDtypeStruct((count, rows, cols), block.dtype)]
    operands = [block]
    extra = weights is not None
    if extra:
        out_shape.append(jax.ShapeDtypeStruct((groups,) + weights.shape, weights.dtype))
        operands.append(weights)
        moved += groups * weights.size * weights.dtype.itemsize
    outs = pl.pallas_call(
        functools.partial(exchange_kernel, count, spread, extra),
        out_shape=tuple(out_shape),
        in_specs=[pl.BlockSpec(memory_space=pl.ANY)] * len(operands),
        out_specs=tuple(pl.BlockSpec(memory_space=pl.ANY) for _ in out_shape),
        scratch_shapes=[
            pltpu.SemaphoreType.DMA((count + groups,)),
            pltpu.SemaphoreType.DMA((count + groups,)),
            pltpu.SemaphoreType.DMA((2,)),
        ],
        compiler_params=pltpu.CompilerParams(collective_id=tag, has_side_effects=True),
        cost_estimate=pl.CostEstimate(flops=0, bytes_accessed=2 * moved, transcendentals=0),
    )(*operands)
    return outs


def gather_chip(block, tag, weights=None):
    outs = exchange(block, False, tag, weights)
    rows = outs[0].reshape(-1, block.shape[1])
    if weights is None:
        return rows
    return rows, outs[1].reshape(-1, weights.shape[1])


def scatter_chip(partial, tag, weights=None):
    count = lax.axis_size("chip")
    outs = exchange(partial.reshape(count, -1, partial.shape[1]), True, tag, weights)
    summed = jnp.sum(outs[0].astype(jnp.float32), axis=0)
    if weights is None:
        return summed
    return summed, outs[1].reshape(-1, weights.shape[1])


def gather_group(block):
    count = lax.axis_size("group")
    pieces = [block]
    for shift in range(1, count):
        route = [(source, (source + shift) % count) for source in range(count)]
        pieces.append(lax.ppermute(block, "group", route))
    stacked = jnp.stack(pieces)
    order = (lax.axis_index("group") - jnp.arange(count)) % count
    return jnp.take(stacked, order, axis=0).reshape(count * block.shape[0], block.shape[1])


def rms_scale(values, gain):
    square = jnp.mean(values * values, axis=-1, keepdims=True)
    return (values * lax.rsqrt(square + norm_eps) * gain).astype(jnp.bfloat16)


def rotate(values, places):
    half_dim = values.shape[-1] // 2
    frequency = rope_base ** (-(jnp.arange(half_dim, dtype=jnp.float32) * 2.0 / values.shape[-1]))
    angle = places.astype(jnp.float32)[:, None] * frequency[None, :]
    cosine = jnp.cos(angle)[:, None, :]
    sine = jnp.sin(angle)[:, None, :]
    widened = values.astype(jnp.float32)
    first = widened[..., :half_dim]
    second = widened[..., half_dim:]
    return jnp.concatenate(
        [first * cosine - second * sine, second * cosine + first * sine], axis=-1
    ).astype(jnp.bfloat16)


def by_core(own_part, other_part):
    first = lax.axis_index("core") == 0
    return jnp.where(first, own_part, other_part), jnp.where(first, other_part, own_part)


def dot(acts, weight):
    return jnp.dot(acts, weight, preferred_element_type=jnp.float32)


def dot_t(acts, weight_t):
    return lax.dot_general(
        acts, weight_t, (((1,), (1,)), ((), ())), preferred_element_type=jnp.float32
    )


def core_rows(values, chips, rows_dev):
    blocks = values.reshape(chips, 2, rows_dev, *values.shape[1:])
    own = lax.dynamic_index_in_dim(blocks, lax.axis_index("core"), axis=1, keepdims=False)
    return own.reshape(chips * rows_dev, *values.shape[1:])


def body(
    hidden,
    request_of,
    positions,
    page_table,
    attn_gain,
    mlp_gain,
    wq,
    wk,
    wv,
    wo,
    w_gate,
    w_up,
    w_down,
):
    chips = lax.axis_size("chip")
    rows_dev = hidden.shape[0]
    tok_group = request_of.shape[0]
    bf = jnp.bfloat16
    residual = hidden.astype(jnp.float32)
    q_cols = wq.shape[1]
    kv_half = wk.shape[1]
    own_attn = jnp.concatenate([wq.astype(bf), wk.astype(bf), wv.astype(bf), wo.astype(bf).T], axis=1)
    own_attn = lax.all_gather(own_attn, "group", axis=0, tiled=True)
    normed = gather_chip(rms_scale(residual, attn_gain), 0)
    other_attn = swap_cores(own_attn)
    query_w = jnp.concatenate([own_attn[:, :q_cols], other_attn[:, :q_cols]], axis=1)
    out_w_t = jnp.concatenate(
        [own_attn[:, q_cols + 2 * kv_half :], other_attn[:, q_cols + 2 * kv_half :]], axis=1
    )
    key_lo, key_hi = by_core(own_attn[:, q_cols : q_cols + kv_half], other_attn[:, q_cols : q_cols + kv_half])
    value_lo, value_hi = by_core(
        own_attn[:, q_cols + kv_half : q_cols + 2 * kv_half],
        other_attn[:, q_cols + kv_half : q_cols + 2 * kv_half],
    )
    key_w = jnp.concatenate([key_lo, key_hi], axis=1)
    value_w = jnp.concatenate([value_lo, value_hi], axis=1)
    ff_cols = w_gate.shape[1]
    own_mlp = jnp.concatenate([w_gate.astype(bf), w_up.astype(bf), w_down.astype(bf).T], axis=1)
    own_mlp = lax.all_gather(own_mlp, "group", axis=0, tiled=True)
    half_pos = core_rows(positions, chips, rows_dev)
    half_req = core_rows(request_of, chips, rows_dev)
    heads = 2 * q_cols // HD
    queries = rotate(dot(normed, query_w).astype(bf).reshape(-1, heads, HD), half_pos)
    keys_half = rotate(dot(normed, key_w).astype(bf).reshape(-1, 1, HD), half_pos)
    values_half = dot(normed, value_w).astype(bf).reshape(-1, 1, HD)
    kv_own = jnp.stack([keys_half[:, 0], values_half[:, 0]], axis=1)
    kv_other = swap_cores(kv_own)
    kv_lo, kv_hi = by_core(kv_own, kv_other)
    kv_rows = jnp.stack(
        [kv_lo.reshape(chips, rows_dev, 2, HD), kv_hi.reshape(chips, rows_dev, 2, HD)], axis=1
    ).reshape(tok_group, 2, HD)
    earlier_rows = min(MAXLEN, tok_group)
    earlier = from_behind(kv_rows[tok_group - earlier_rows :], "group", 1)
    all_rows = jnp.concatenate([earlier, kv_rows], axis=0)
    all_keys = all_rows[:, 0]
    all_values = all_rows[:, 1]
    first_request = request_of[0]
    first_position = positions[0]
    same_local = (half_req[:, None] == request_of[None, :]) & (
        positions[None, :] <= half_pos[:, None]
    )
    same_earlier = (half_req[:, None] == first_request) & (
        jnp.arange(earlier_rows)[None, :] >= earlier_rows - first_position
    )
    visible = jnp.concatenate([same_earlier, same_local], axis=1)
    scores = jnp.einsum(
        "qhd,kd->hqk", queries, all_keys, preferred_element_type=jnp.float32
    ) * HD ** (-0.5)
    scores = jnp.where(visible[None], scores, -1e30)
    row_peak = jnp.max(scores, axis=-1, keepdims=True)
    probs = jnp.where(visible[None], jnp.exp(scores - row_peak), 0.0)
    total = jnp.sum(probs, axis=-1, keepdims=True)
    mixed_heads = jnp.einsum(
        "hqk,kd->qhd", probs.astype(bf), all_values, preferred_element_type=jnp.float32
    ) / jnp.transpose(total, (1, 0, 2))
    attended = mixed_heads.astype(bf).reshape(-1, heads * HD)
    attn_part = dot_t(attended, out_w_t)
    other_mlp = swap_cores(own_mlp)
    attn_sum = scatter_chip(attn_part.astype(bf), 1)
    mixed = residual + attn_sum
    normed_mlp = gather_chip(rms_scale(mixed, mlp_gain), 2)
    gate_sum = jnp.concatenate(
        [dot(normed_mlp, own_mlp[:, :ff_cols]), dot(normed_mlp, other_mlp[:, :ff_cols])], axis=1
    )
    up_sum = jnp.concatenate(
        [
            dot(normed_mlp, own_mlp[:, ff_cols : 2 * ff_cols]),
            dot(normed_mlp, other_mlp[:, ff_cols : 2 * ff_cols]),
        ],
        axis=1,
    )
    activation = (jax.nn.silu(gate_sum) * up_sum).astype(bf)
    down_w_t = jnp.concatenate([own_mlp[:, 2 * ff_cols :], other_mlp[:, 2 * ff_cols :]], axis=1)
    down_part = dot_t(activation, down_w_t)
    layer_out = (mixed + scatter_chip(down_part.astype(bf), 3)).astype(bf)
    pages = page_table.shape[1]
    changed = jnp.concatenate(
        [jnp.ones((1,), jnp.int32), (request_of[1:] != request_of[:-1]).astype(jnp.int32)]
    )
    opens = jnp.maximum(changed, (positions % PAGE == 0).astype(jnp.int32))
    logical = jnp.cumsum(opens) - 1
    chosen = jnp.sum(
        jnp.where(logical[:, None] == jnp.arange(pages)[None, :], page_table, 0), axis=1
    )
    target = chosen * PAGE + positions % PAGE
    own_slice = lax.dynamic_index_in_dim(kv_rows, lax.axis_index("core"), axis=1, keepdims=False)
    width = own_slice.shape[1]
    cache = jnp.zeros((pages * PAGE, width), jnp.bfloat16).at[target].set(own_slice)
    return (layer_out, cache.reshape(pages, PAGE, width))


def solution(mesh):
    groups, tensors = mesh.devices.shape
    split = Mesh(mesh.devices.reshape(groups, tensors // 2, 2), ("group", "chip", "core"))
    tensor = ("chip", "core")
    placed = (
        P(("group",) + tensor, None),
        P("group"),
        P("group"),
        P("group", None),
        P(),
        P(),
        P("group", tensor),
        P("group", tensor),
        P("group", tensor),
        P(tensor, "group"),
        P("group", tensor),
        P("group", tensor),
        P(tensor, "group"),
    )
    return jax.shard_map(
        body,
        mesh=split,
        in_specs=placed,
        out_specs=(P(("group",) + tensor, None), P("group", None, tensor)),
        check_vma=False,
    )
```

```python
import functools

import jax
import jax.numpy as jnp
from jax import lax
from jax.experimental import pallas as pl
from jax.experimental.pallas import tpu as pltpu
from jax.sharding import Mesh
from jax.sharding import PartitionSpec as P

QH = 16
KVH = 8
HD = 128
PAGE = 128
MAXLEN = 512


rope_base = 1000000.0
norm_eps = 1e-06


def swap_cores(value):
    return lax.ppermute(value, "core", [(0, 1), (1, 0)])


def from_behind(block, axis, distance):
    devices = range(lax.axis_size(axis))
    route = [(i - distance, i) for i in devices if i - distance in devices]
    return lax.ppermute(block, axis, route)


def exchange_kernel(count, spread, extra, *refs):
    if extra:
        source, weights, slots, swapped, send_sems, recv_sems, local_sem = refs
    else:
        source, slots, send_sems, recv_sems, local_sem = refs
    me = lax.axis_index("chip")
    group = lax.axis_index("group")
    core = lax.axis_index("core")
    mesh_ids = pl.DeviceIdType.MESH
    barrier = pltpu.get_barrier_semaphore()
    for shift in range(1, count):
        peer = lax.rem(me + shift, count)
        pl.semaphore_signal(barrier, inc=1, device_id=(group, peer, core), device_id_type=mesh_ids)
    if extra:
        pl.semaphore_signal(barrier, inc=1, device_id=(group, me, 1 - core), device_id_type=mesh_ids)
    pl.semaphore_wait(barrier, count - 1 + extra)
    local = pltpu.make_async_copy(source.at[me] if spread else source, slots.at[me], local_sem)
    local.start()
    copies = []
    if extra:
        swap = pltpu.make_async_remote_copy(
            src_ref=weights,
            dst_ref=swapped,
            send_sem=send_sems.at[0],
            recv_sem=recv_sems.at[0],
            device_id=(group, me, 1 - core),
            device_id_type=mesh_ids,
        )
        swap.start()
        copies.append(swap)
    for shift in range(1, count):
        peer = lax.rem(me + shift, count)
        copy = pltpu.make_async_remote_copy(
            src_ref=source.at[peer] if spread else source,
            dst_ref=slots.at[me],
            send_sem=send_sems.at[shift],
            recv_sem=recv_sems.at[shift],
            device_id=(group, peer, core),
            device_id_type=mesh_ids,
        )
        copy.start()
        copies.append(copy)
    for shift in range(1, count):
        sender = lax.rem(me + count - shift, count)
        pltpu.make_async_remote_copy(
            src_ref=slots.at[sender],
            dst_ref=slots.at[sender],
            send_sem=send_sems.at[shift],
            recv_sem=recv_sems.at[shift],
            device_id=(group, sender, core),
            device_id_type=mesh_ids,
        ).wait_recv()
    if extra:
        swap.wait_recv()
    for copy in copies:
        copy.wait_send()
    local.wait()


def exchange(block, spread, tag, weights=None):
    count = lax.axis_size("chip")
    rows, cols = block.shape[-2:]
    moved = count * rows * cols * block.dtype.itemsize
    out_shape = [jax.ShapeDtypeStruct((count, rows, cols), block.dtype)]
    operands = [block]
    extra = weights is not None
    if extra:
        out_shape.append(jax.ShapeDtypeStruct(weights.shape, weights.dtype))
        operands.append(weights)
        moved += weights.size * weights.dtype.itemsize
    outs = pl.pallas_call(
        functools.partial(exchange_kernel, count, spread, extra),
        out_shape=tuple(out_shape),
        in_specs=[pl.BlockSpec(memory_space=pl.ANY)] * len(operands),
        out_specs=tuple(pl.BlockSpec(memory_space=pl.ANY) for _ in out_shape),
        scratch_shapes=[
            pltpu.SemaphoreType.DMA((count,)),
            pltpu.SemaphoreType.DMA((count,)),
            pltpu.SemaphoreType.DMA(()),
        ],
        compiler_params=pltpu.CompilerParams(collective_id=tag, has_side_effects=True),
        cost_estimate=pl.CostEstimate(flops=0, bytes_accessed=2 * moved, transcendentals=0),
    )(*operands)
    return outs


def gather_chip(block, tag):
    outs = exchange(block, False, tag)
    return outs[0].reshape(-1, block.shape[1])


def scatter_chip(partial, tag, weights=None):
    count = lax.axis_size("chip")
    outs = exchange(partial.reshape(count, -1, partial.shape[1]), True, tag, weights)
    summed = jnp.sum(outs[0].astype(jnp.float32), axis=0)
    if weights is None:
        return summed
    return summed, outs[1]


def gather_group(block):
    count = lax.axis_size("group")
    pieces = [block]
    for shift in range(1, count):
        route = [(source, (source + shift) % count) for source in range(count)]
        pieces.append(lax.ppermute(block, "group", route))
    stacked = jnp.stack(pieces)
    order = (lax.axis_index("group") - jnp.arange(count)) % count
    return jnp.take(stacked, order, axis=0).reshape(count * block.shape[0], block.shape[1])


def rms_scale(values, gain):
    square = jnp.mean(values * values, axis=-1, keepdims=True)
    return (values * lax.rsqrt(square + norm_eps) * gain).astype(jnp.bfloat16)


def rotate(values, places):
    half_dim = values.shape[-1] // 2
    frequency = rope_base ** (-(jnp.arange(half_dim, dtype=jnp.float32) * 2.0 / values.shape[-1]))
    angle = places.astype(jnp.float32)[:, None] * frequency[None, :]
    cosine = jnp.cos(angle)[:, None, :]
    sine = jnp.sin(angle)[:, None, :]
    widened = values.astype(jnp.float32)
    first = widened[..., :half_dim]
    second = widened[..., half_dim:]
    return jnp.concatenate(
        [first * cosine - second * sine, second * cosine + first * sine], axis=-1
    ).astype(jnp.bfloat16)


def by_core(own_part, other_part):
    first = lax.axis_index("core") == 0
    return jnp.where(first, own_part, other_part), jnp.where(first, other_part, own_part)


def dot(acts, weight):
    return jnp.dot(acts, weight, preferred_element_type=jnp.float32)


def dot_t(acts, weight_t):
    return lax.dot_general(
        acts, weight_t, (((1,), (1,)), ((), ())), preferred_element_type=jnp.float32
    )


def core_rows(values, chips, rows_dev):
    blocks = values.reshape(chips, 2, rows_dev, *values.shape[1:])
    own = lax.dynamic_index_in_dim(blocks, lax.axis_index("core"), axis=1, keepdims=False)
    return own.reshape(chips * rows_dev, *values.shape[1:])


def body(
    hidden,
    request_of,
    positions,
    page_table,
    attn_gain,
    mlp_gain,
    wq,
    wk,
    wv,
    wo,
    w_gate,
    w_up,
    w_down,
):
    chips = lax.axis_size("chip")
    rows_dev = hidden.shape[0]
    tok_group = request_of.shape[0]
    bf = jnp.bfloat16
    residual = hidden.astype(jnp.float32)
    q_cols = wq.shape[1]
    kv_half = wk.shape[1]
    own_attn = jnp.concatenate([wq.astype(bf), wk.astype(bf), wv.astype(bf), wo.astype(bf).T], axis=1)
    own_attn = lax.all_gather(own_attn, "group", axis=0, tiled=True)
    normed = gather_chip(rms_scale(residual, attn_gain), 0)
    other_attn = swap_cores(own_attn)
    query_w = jnp.concatenate([own_attn[:, :q_cols], other_attn[:, :q_cols]], axis=1)
    out_w_t = jnp.concatenate(
        [own_attn[:, q_cols + 2 * kv_half :], other_attn[:, q_cols + 2 * kv_half :]], axis=1
    )
    key_lo, key_hi = by_core(own_attn[:, q_cols : q_cols + kv_half], other_attn[:, q_cols : q_cols + kv_half])
    value_lo, value_hi = by_core(
        own_attn[:, q_cols + kv_half : q_cols + 2 * kv_half],
        other_attn[:, q_cols + kv_half : q_cols + 2 * kv_half],
    )
    key_w = jnp.concatenate([key_lo, key_hi], axis=1)
    value_w = jnp.concatenate([value_lo, value_hi], axis=1)
    ff_cols = w_gate.shape[1]
    own_mlp = jnp.concatenate([w_gate.astype(bf), w_up.astype(bf), w_down.astype(bf).T], axis=1)
    own_mlp = lax.all_gather(own_mlp, "group", axis=0, tiled=True)
    half_pos = core_rows(positions, chips, rows_dev)
    half_req = core_rows(request_of, chips, rows_dev)
    heads = 2 * q_cols // HD
    queries = rotate(dot(normed, query_w).astype(bf).reshape(-1, heads, HD), half_pos)
    keys_half = rotate(dot(normed, key_w).astype(bf).reshape(-1, 1, HD), half_pos)
    values_half = dot(normed, value_w).astype(bf).reshape(-1, 1, HD)
    kv_own = jnp.stack([keys_half[:, 0], values_half[:, 0]], axis=1)
    kv_other = swap_cores(kv_own)
    kv_lo, kv_hi = by_core(kv_own, kv_other)
    kv_rows = jnp.stack(
        [kv_lo.reshape(chips, rows_dev, 2, HD), kv_hi.reshape(chips, rows_dev, 2, HD)], axis=1
    ).reshape(tok_group, 2, HD)
    earlier_rows = min(MAXLEN, tok_group)
    earlier = from_behind(kv_rows[tok_group - earlier_rows :], "group", 1)
    all_rows = jnp.concatenate([earlier, kv_rows], axis=0)
    all_keys = all_rows[:, 0]
    all_values = all_rows[:, 1]
    first_request = request_of[0]
    first_position = positions[0]
    same_local = (half_req[:, None] == request_of[None, :]) & (
        positions[None, :] <= half_pos[:, None]
    )
    same_earlier = (half_req[:, None] == first_request) & (
        jnp.arange(earlier_rows)[None, :] >= earlier_rows - first_position
    )
    visible = jnp.concatenate([same_earlier, same_local], axis=1)
    scores = jnp.einsum(
        "qhd,kd->hqk", queries, all_keys, preferred_element_type=jnp.float32
    ) * HD ** (-0.5)
    scores = jnp.where(visible[None], scores, -1e30)
    row_peak = jnp.max(scores, axis=-1, keepdims=True)
    probs = jnp.where(visible[None], jnp.exp(scores - row_peak), 0.0)
    total = jnp.sum(probs, axis=-1, keepdims=True)
    mixed_heads = jnp.einsum(
        "hqk,kd->qhd", probs.astype(bf), all_values, preferred_element_type=jnp.float32
    ) / jnp.transpose(total, (1, 0, 2))
    attended = mixed_heads.astype(bf).reshape(-1, heads * HD)
    attn_part = dot_t(attended, out_w_t)
    attn_sum, other_mlp = scatter_chip(attn_part.astype(bf), 1, own_mlp)
    mixed = residual + attn_sum
    normed_mlp = gather_chip(rms_scale(mixed, mlp_gain), 2)
    gate_sum = jnp.concatenate(
        [dot(normed_mlp, own_mlp[:, :ff_cols]), dot(normed_mlp, other_mlp[:, :ff_cols])], axis=1
    )
    up_sum = jnp.concatenate(
        [
            dot(normed_mlp, own_mlp[:, ff_cols : 2 * ff_cols]),
            dot(normed_mlp, other_mlp[:, ff_cols : 2 * ff_cols]),
        ],
        axis=1,
    )
    activation = (jax.nn.silu(gate_sum) * up_sum).astype(bf)
    down_w_t = jnp.concatenate([own_mlp[:, 2 * ff_cols :], other_mlp[:, 2 * ff_cols :]], axis=1)
    down_part = dot_t(activation, down_w_t)
    layer_out = (mixed + scatter_chip(down_part.astype(bf), 3)).astype(bf)
    pages = page_table.shape[1]
    changed = jnp.concatenate(
        [jnp.ones((1,), jnp.int32), (request_of[1:] != request_of[:-1]).astype(jnp.int32)]
    )
    opens = jnp.maximum(changed, (positions % PAGE == 0).astype(jnp.int32))
    logical = jnp.cumsum(opens) - 1
    chosen = jnp.sum(
        jnp.where(logical[:, None] == jnp.arange(pages)[None, :], page_table, 0), axis=1
    )
    target = chosen * PAGE + positions % PAGE
    own_slice = lax.dynamic_index_in_dim(kv_rows, lax.axis_index("core"), axis=1, keepdims=False)
    width = own_slice.shape[1]
    cache = jnp.zeros((pages * PAGE, width), jnp.bfloat16).at[target].set(own_slice)
    return (layer_out, cache.reshape(pages, PAGE, width))


def solution(mesh):
    groups, tensors = mesh.devices.shape
    split = Mesh(mesh.devices.reshape(groups, tensors // 2, 2), ("group", "chip", "core"))
    tensor = ("chip", "core")
    placed = (
        P(("group",) + tensor, None),
        P("group"),
        P("group"),
        P("group", None),
        P(),
        P(),
        P("group", tensor),
        P("group", tensor),
        P("group", tensor),
        P(tensor, "group"),
        P("group", tensor),
        P("group", tensor),
        P(tensor, "group"),
    )
    return jax.shard_map(
        body,
        mesh=split,
        in_specs=placed,
        out_specs=(P(("group",) + tensor, None), P("group", None, tensor)),
        check_vma=False,
    )
```

```python
import functools

import jax
import jax.numpy as jnp
from jax import lax
from jax.experimental import pallas as pl
from jax.experimental.pallas import tpu as pltpu
from jax.sharding import Mesh
from jax.sharding import PartitionSpec as P

QH = 16
KVH = 8
HD = 128
PAGE = 128
MAXLEN = 512


rope_base = 1000000.0
norm_eps = 1e-06


def swap_cores(value):
    return lax.ppermute(value, "core", [(0, 1), (1, 0)])


def from_behind(block, axis, distance):
    devices = range(lax.axis_size(axis))
    route = [(i - distance, i) for i in devices if i - distance in devices]
    return lax.ppermute(block, axis, route)


def exchange_kernel(count, spread, spreads, swaps, *refs):
    source = refs[0]
    weights = refs[1] if (spreads or swaps) else None
    outs = refs[1 + (spreads or swaps) :]
    slots = outs[0]
    moved = outs[1] if (spreads or swaps) else None
    send_sems, recv_sems, local_sem = outs[-3:]
    me = lax.axis_index("chip")
    group = lax.axis_index("group")
    core = lax.axis_index("core")
    groups = lax.axis_size("group")
    mesh_ids = pl.DeviceIdType.MESH
    barrier = pltpu.get_barrier_semaphore()
    for shift in range(1, count):
        peer = lax.rem(me + shift, count)
        pl.semaphore_signal(barrier, inc=1, device_id=(group, peer, core), device_id_type=mesh_ids)
    greeted = count - 1
    if swaps:
        pl.semaphore_signal(barrier, inc=1, device_id=(group, me, 1 - core), device_id_type=mesh_ids)
        greeted += 1
    if spreads:
        for shift in range(1, groups):
            peer = lax.rem(group + shift, groups)
            pl.semaphore_signal(barrier, inc=1, device_id=(peer, me, core), device_id_type=mesh_ids)
        greeted += groups - 1
    pl.semaphore_wait(barrier, greeted)
    local = pltpu.make_async_copy(source.at[me] if spread else source, slots.at[me], local_sem.at[0])
    local.start()
    locals_ = [local]
    copies = []
    if swaps:
        swap = pltpu.make_async_remote_copy(
            src_ref=weights,
            dst_ref=moved,
            send_sem=send_sems.at[0],
            recv_sem=recv_sems.at[0],
            device_id=(group, me, 1 - core),
            device_id_type=mesh_ids,
        )
        swap.start()
        copies.append(swap)
    if spreads:
        own_weights = pltpu.make_async_copy(weights, moved.at[group], local_sem.at[1])
        own_weights.start()
        locals_.append(own_weights)
        for shift in range(1, groups):
            peer = lax.rem(group + shift, groups)
            copy = pltpu.make_async_remote_copy(
                src_ref=weights,
                dst_ref=moved.at[group],
                send_sem=send_sems.at[count + shift],
                recv_sem=recv_sems.at[count + shift],
                device_id=(peer, me, core),
                device_id_type=mesh_ids,
            )
            copy.start()
            copies.append(copy)
    for shift in range(1, count):
        peer = lax.rem(me + shift, count)
        copy = pltpu.make_async_remote_copy(
            src_ref=source.at[peer] if spread else source,
            dst_ref=slots.at[me],
            send_sem=send_sems.at[shift],
            recv_sem=recv_sems.at[shift],
            device_id=(group, peer, core),
            device_id_type=mesh_ids,
        )
        copy.start()
        copies.append(copy)
    for shift in range(1, count):
        sender = lax.rem(me + count - shift, count)
        pltpu.make_async_remote_copy(
            src_ref=slots.at[sender],
            dst_ref=slots.at[sender],
            send_sem=send_sems.at[shift],
            recv_sem=recv_sems.at[shift],
            device_id=(group, sender, core),
            device_id_type=mesh_ids,
        ).wait_recv()
    if swaps:
        swap.wait_recv()
    if spreads:
        for shift in range(1, groups):
            sender = lax.rem(group + groups - shift, groups)
            pltpu.make_async_remote_copy(
                src_ref=moved.at[sender],
                dst_ref=moved.at[sender],
                send_sem=send_sems.at[count + shift],
                recv_sem=recv_sems.at[count + shift],
                device_id=(sender, me, core),
                device_id_type=mesh_ids,
            ).wait_recv()
    for copy in copies:
        copy.wait_send()
    for copy in locals_:
        copy.wait()


def exchange(block, spread, tag, weights=None, spreads=False):
    count = lax.axis_size("chip")
    groups = lax.axis_size("group")
    rows, cols = block.shape[-2:]
    moved = count * rows * cols * block.dtype.itemsize
    out_shape = [jax.ShapeDtypeStruct((count, rows, cols), block.dtype)]
    operands = [block]
    swaps = weights is not None and not spreads
    if weights is not None:
        copies = groups if spreads else 1
        out_shape.append(jax.ShapeDtypeStruct((copies,) * spreads + weights.shape, weights.dtype))
        operands.append(weights)
        moved += copies * weights.size * weights.dtype.itemsize
    outs = pl.pallas_call(
        functools.partial(exchange_kernel, count, spread, spreads, swaps),
        out_shape=tuple(out_shape),
        in_specs=[pl.BlockSpec(memory_space=pl.ANY)] * len(operands),
        out_specs=tuple(pl.BlockSpec(memory_space=pl.ANY) for _ in out_shape),
        scratch_shapes=[
            pltpu.SemaphoreType.DMA((count + groups,)),
            pltpu.SemaphoreType.DMA((count + groups,)),
            pltpu.SemaphoreType.DMA((2,)),
        ],
        compiler_params=pltpu.CompilerParams(collective_id=tag, has_side_effects=True),
        cost_estimate=pl.CostEstimate(flops=0, bytes_accessed=2 * moved, transcendentals=0),
    )(*operands)
    return outs


def gather_chip(block, tag, weights=None):
    outs = exchange(block, False, tag, weights, spreads=weights is not None)
    rows = outs[0].reshape(-1, block.shape[1])
    if weights is None:
        return rows
    return rows, outs[1].reshape(-1, weights.shape[1])


def scatter_chip(partial, tag, weights=None):
    count = lax.axis_size("chip")
    outs = exchange(partial.reshape(count, -1, partial.shape[1]), True, tag, weights)
    summed = jnp.sum(outs[0].astype(jnp.float32), axis=0)
    if weights is None:
        return summed
    return summed, outs[1]


def gather_group(block):
    count = lax.axis_size("group")
    pieces = [block]
    for shift in range(1, count):
        route = [(source, (source + shift) % count) for source in range(count)]
        pieces.append(lax.ppermute(block, "group", route))
    stacked = jnp.stack(pieces)
    order = (lax.axis_index("group") - jnp.arange(count)) % count
    return jnp.take(stacked, order, axis=0).reshape(count * block.shape[0], block.shape[1])


def rms_scale(values, gain):
    square = jnp.mean(values * values, axis=-1, keepdims=True)
    return (values * lax.rsqrt(square + norm_eps) * gain).astype(jnp.bfloat16)


def rotate(values, places):
    half_dim = values.shape[-1] // 2
    frequency = rope_base ** (-(jnp.arange(half_dim, dtype=jnp.float32) * 2.0 / values.shape[-1]))
    angle = places.astype(jnp.float32)[:, None] * frequency[None, :]
    cosine = jnp.cos(angle)[:, None, :]
    sine = jnp.sin(angle)[:, None, :]
    widened = values.astype(jnp.float32)
    first = widened[..., :half_dim]
    second = widened[..., half_dim:]
    return jnp.concatenate(
        [first * cosine - second * sine, second * cosine + first * sine], axis=-1
    ).astype(jnp.bfloat16)


def by_core(own_part, other_part):
    first = lax.axis_index("core") == 0
    return jnp.where(first, own_part, other_part), jnp.where(first, other_part, own_part)


def dot(acts, weight):
    return jnp.dot(acts, weight, preferred_element_type=jnp.float32)


def dot_t(acts, weight_t):
    return lax.dot_general(
        acts, weight_t, (((1,), (1,)), ((), ())), preferred_element_type=jnp.float32
    )


def core_rows(values, chips, rows_dev):
    blocks = values.reshape(chips, 2, rows_dev, *values.shape[1:])
    own = lax.dynamic_index_in_dim(blocks, lax.axis_index("core"), axis=1, keepdims=False)
    return own.reshape(chips * rows_dev, *values.shape[1:])


def body(
    hidden,
    request_of,
    positions,
    page_table,
    attn_gain,
    mlp_gain,
    wq,
    wk,
    wv,
    wo,
    w_gate,
    w_up,
    w_down,
):
    chips = lax.axis_size("chip")
    rows_dev = hidden.shape[0]
    tok_group = request_of.shape[0]
    bf = jnp.bfloat16
    residual = hidden.astype(jnp.float32)
    q_cols = wq.shape[1]
    kv_half = wk.shape[1]
    own_attn = jnp.concatenate([wq.astype(bf), wk.astype(bf), wv.astype(bf), wo.astype(bf).T], axis=1)
    normed, own_attn = gather_chip(rms_scale(residual, attn_gain), 0, own_attn)
    other_attn = swap_cores(own_attn)
    query_w = jnp.concatenate([own_attn[:, :q_cols], other_attn[:, :q_cols]], axis=1)
    out_w_t = jnp.concatenate(
        [own_attn[:, q_cols + 2 * kv_half :], other_attn[:, q_cols + 2 * kv_half :]], axis=1
    )
    key_lo, key_hi = by_core(own_attn[:, q_cols : q_cols + kv_half], other_attn[:, q_cols : q_cols + kv_half])
    value_lo, value_hi = by_core(
        own_attn[:, q_cols + kv_half : q_cols + 2 * kv_half],
        other_attn[:, q_cols + kv_half : q_cols + 2 * kv_half],
    )
    key_w = jnp.concatenate([key_lo, key_hi], axis=1)
    value_w = jnp.concatenate([value_lo, value_hi], axis=1)
    ff_cols = w_gate.shape[1]
    own_mlp = jnp.concatenate([w_gate.astype(bf), w_up.astype(bf), w_down.astype(bf).T], axis=1)
    own_mlp = lax.all_gather(own_mlp, "group", axis=0, tiled=True)
    half_pos = core_rows(positions, chips, rows_dev)
    half_req = core_rows(request_of, chips, rows_dev)
    heads = 2 * q_cols // HD
    queries = rotate(dot(normed, query_w).astype(bf).reshape(-1, heads, HD), half_pos)
    keys_half = rotate(dot(normed, key_w).astype(bf).reshape(-1, 1, HD), half_pos)
    values_half = dot(normed, value_w).astype(bf).reshape(-1, 1, HD)
    kv_own = jnp.stack([keys_half[:, 0], values_half[:, 0]], axis=1)
    kv_other = swap_cores(kv_own)
    kv_lo, kv_hi = by_core(kv_own, kv_other)
    kv_rows = jnp.stack(
        [kv_lo.reshape(chips, rows_dev, 2, HD), kv_hi.reshape(chips, rows_dev, 2, HD)], axis=1
    ).reshape(tok_group, 2, HD)
    earlier_rows = min(MAXLEN, tok_group)
    earlier = from_behind(kv_rows[tok_group - earlier_rows :], "group", 1)
    all_rows = jnp.concatenate([earlier, kv_rows], axis=0)
    all_keys = all_rows[:, 0]
    all_values = all_rows[:, 1]
    first_request = request_of[0]
    first_position = positions[0]
    same_local = (half_req[:, None] == request_of[None, :]) & (
        positions[None, :] <= half_pos[:, None]
    )
    same_earlier = (half_req[:, None] == first_request) & (
        jnp.arange(earlier_rows)[None, :] >= earlier_rows - first_position
    )
    visible = jnp.concatenate([same_earlier, same_local], axis=1)
    scores = jnp.einsum(
        "qhd,kd->hqk", queries, all_keys, preferred_element_type=jnp.float32
    ) * HD ** (-0.5)
    scores = jnp.where(visible[None], scores, -1e30)
    row_peak = jnp.max(scores, axis=-1, keepdims=True)
    probs = jnp.where(visible[None], jnp.exp(scores - row_peak), 0.0)
    total = jnp.sum(probs, axis=-1, keepdims=True)
    mixed_heads = jnp.einsum(
        "hqk,kd->qhd", probs.astype(bf), all_values, preferred_element_type=jnp.float32
    ) / jnp.transpose(total, (1, 0, 2))
    attended = mixed_heads.astype(bf).reshape(-1, heads * HD)
    attn_part = dot_t(attended, out_w_t)
    attn_sum, other_mlp = scatter_chip(attn_part.astype(bf), 1, own_mlp)
    mixed = residual + attn_sum
    normed_mlp = gather_chip(rms_scale(mixed, mlp_gain), 2)
    gate_sum = jnp.concatenate(
        [dot(normed_mlp, own_mlp[:, :ff_cols]), dot(normed_mlp, other_mlp[:, :ff_cols])], axis=1
    )
    up_sum = jnp.concatenate(
        [
            dot(normed_mlp, own_mlp[:, ff_cols : 2 * ff_cols]),
            dot(normed_mlp, other_mlp[:, ff_cols : 2 * ff_cols]),
        ],
        axis=1,
    )
    activation = (jax.nn.silu(gate_sum) * up_sum).astype(bf)
    down_w_t = jnp.concatenate([own_mlp[:, 2 * ff_cols :], other_mlp[:, 2 * ff_cols :]], axis=1)
    down_part = dot_t(activation, down_w_t)
    layer_out = (mixed + scatter_chip(down_part.astype(bf), 3)).astype(bf)
    pages = page_table.shape[1]
    changed = jnp.concatenate(
        [jnp.ones((1,), jnp.int32), (request_of[1:] != request_of[:-1]).astype(jnp.int32)]
    )
    opens = jnp.maximum(changed, (positions % PAGE == 0).astype(jnp.int32))
    logical = jnp.cumsum(opens) - 1
    chosen = jnp.sum(
        jnp.where(logical[:, None] == jnp.arange(pages)[None, :], page_table, 0), axis=1
    )
    target = chosen * PAGE + positions % PAGE
    own_slice = lax.dynamic_index_in_dim(kv_rows, lax.axis_index("core"), axis=1, keepdims=False)
    width = own_slice.shape[1]
    cache = jnp.zeros((pages * PAGE, width), jnp.bfloat16).at[target].set(own_slice)
    return (layer_out, cache.reshape(pages, PAGE, width))


def solution(mesh):
    groups, tensors = mesh.devices.shape
    split = Mesh(mesh.devices.reshape(groups, tensors // 2, 2), ("group", "chip", "core"))
    tensor = ("chip", "core")
    placed = (
        P(("group",) + tensor, None),
        P("group"),
        P("group"),
        P("group", None),
        P(),
        P(),
        P("group", tensor),
        P("group", tensor),
        P("group", tensor),
        P(tensor, "group"),
        P("group", tensor),
        P("group", tensor),
        P(tensor, "group"),
    )
    return jax.shard_map(
        body,
        mesh=split,
        in_specs=placed,
        out_specs=(P(("group",) + tensor, None), P("group", None, tensor)),
        check_vma=False,
    )
```

```python
import functools

import jax
import jax.numpy as jnp
from jax import lax
from jax.experimental import pallas as pl
from jax.experimental.pallas import tpu as pltpu
from jax.sharding import Mesh
from jax.sharding import PartitionSpec as P

QH = 16
KVH = 8
HD = 128
PAGE = 128
MAXLEN = 512


rope_base = 1000000.0
norm_eps = 1e-06


def swap_cores(value):
    return lax.ppermute(value, "core", [(0, 1), (1, 0)])


def from_behind(block, axis, distance):
    devices = range(lax.axis_size(axis))
    route = [(i - distance, i) for i in devices if i - distance in devices]
    return lax.ppermute(block, axis, route)


def exchange_kernel(count, spread, spreads, swaps, *refs):
    source = refs[0]
    weights = refs[1] if (spreads or swaps) else None
    outs = refs[1 + (spreads or swaps) :]
    slots = outs[0]
    moved = outs[1] if (spreads or swaps) else None
    send_sems, recv_sems, local_sem = outs[-3:]
    me = lax.axis_index("chip")
    group = lax.axis_index("group")
    core = lax.axis_index("core")
    groups = lax.axis_size("group")
    mesh_ids = pl.DeviceIdType.MESH
    barrier = pltpu.get_barrier_semaphore()
    for shift in range(1, count):
        peer = lax.rem(me + shift, count)
        pl.semaphore_signal(barrier, inc=1, device_id=(group, peer, core), device_id_type=mesh_ids)
    greeted = count - 1
    if swaps:
        pl.semaphore_signal(barrier, inc=1, device_id=(group, me, 1 - core), device_id_type=mesh_ids)
        greeted += 1
    if spreads:
        for shift in range(1, groups):
            peer = lax.rem(group + shift, groups)
            pl.semaphore_signal(barrier, inc=1, device_id=(peer, me, core), device_id_type=mesh_ids)
        greeted += groups - 1
    pl.semaphore_wait(barrier, greeted)
    local = pltpu.make_async_copy(source.at[me] if spread else source, slots.at[me], local_sem.at[0])
    local.start()
    locals_ = [local]
    copies = []
    if swaps:
        swap = pltpu.make_async_remote_copy(
            src_ref=weights,
            dst_ref=moved,
            send_sem=send_sems.at[0],
            recv_sem=recv_sems.at[0],
            device_id=(group, me, 1 - core),
            device_id_type=mesh_ids,
        )
        swap.start()
        copies.append(swap)
    if spreads:
        own_weights = pltpu.make_async_copy(weights, moved.at[group], local_sem.at[1])
        own_weights.start()
        locals_.append(own_weights)
        for shift in range(1, groups):
            peer = lax.rem(group + shift, groups)
            copy = pltpu.make_async_remote_copy(
                src_ref=weights,
                dst_ref=moved.at[group],
                send_sem=send_sems.at[count + shift],
                recv_sem=recv_sems.at[count + shift],
                device_id=(peer, me, core),
                device_id_type=mesh_ids,
            )
            copy.start()
            copies.append(copy)
    for shift in range(1, count):
        peer = lax.rem(me + shift, count)
        copy = pltpu.make_async_remote_copy(
            src_ref=source.at[peer] if spread else source,
            dst_ref=slots.at[me],
            send_sem=send_sems.at[shift],
            recv_sem=recv_sems.at[shift],
            device_id=(group, peer, core),
            device_id_type=mesh_ids,
        )
        copy.start()
        copies.append(copy)
    for shift in range(1, count):
        sender = lax.rem(me + count - shift, count)
        pltpu.make_async_remote_copy(
            src_ref=slots.at[sender],
            dst_ref=slots.at[sender],
            send_sem=send_sems.at[shift],
            recv_sem=recv_sems.at[shift],
            device_id=(group, sender, core),
            device_id_type=mesh_ids,
        ).wait_recv()
    if swaps:
        swap.wait_recv()
    if spreads:
        for shift in range(1, groups):
            sender = lax.rem(group + groups - shift, groups)
            pltpu.make_async_remote_copy(
                src_ref=moved.at[sender],
                dst_ref=moved.at[sender],
                send_sem=send_sems.at[count + shift],
                recv_sem=recv_sems.at[count + shift],
                device_id=(sender, me, core),
                device_id_type=mesh_ids,
            ).wait_recv()
    for copy in copies:
        copy.wait_send()
    for copy in locals_:
        copy.wait()


def exchange(block, spread, tag, weights=None, spreads=False):
    count = lax.axis_size("chip")
    groups = lax.axis_size("group")
    rows, cols = block.shape[-2:]
    moved = count * rows * cols * block.dtype.itemsize
    out_shape = [jax.ShapeDtypeStruct((count, rows, cols), block.dtype)]
    operands = [block]
    swaps = weights is not None and not spreads
    if weights is not None:
        copies = groups if spreads else 1
        out_shape.append(jax.ShapeDtypeStruct((copies,) * spreads + weights.shape, weights.dtype))
        operands.append(weights)
        moved += copies * weights.size * weights.dtype.itemsize
    outs = pl.pallas_call(
        functools.partial(exchange_kernel, count, spread, spreads, swaps),
        out_shape=tuple(out_shape),
        in_specs=[pl.BlockSpec(memory_space=pl.ANY)] * len(operands),
        out_specs=tuple(pl.BlockSpec(memory_space=pl.ANY) for _ in out_shape),
        scratch_shapes=[
            pltpu.SemaphoreType.DMA((count + groups,)),
            pltpu.SemaphoreType.DMA((count + groups,)),
            pltpu.SemaphoreType.DMA((2,)),
        ],
        compiler_params=pltpu.CompilerParams(collective_id=tag, has_side_effects=True),
        cost_estimate=pl.CostEstimate(flops=0, bytes_accessed=2 * moved, transcendentals=0),
    )(*operands)
    return outs


def gather_chip(block, tag):
    outs = exchange(block, False, tag)
    return outs[0].reshape(-1, block.shape[1])


def gather_swap(block, tag, weights):
    outs = exchange(block, False, tag, weights)
    return outs[0].reshape(-1, block.shape[1]), outs[1]


def scatter_chip(partial, tag):
    count = lax.axis_size("chip")
    outs = exchange(partial.reshape(count, -1, partial.shape[1]), True, tag)
    return jnp.sum(outs[0].astype(jnp.float32), axis=0)


def gather_group(block):
    count = lax.axis_size("group")
    pieces = [block]
    for shift in range(1, count):
        route = [(source, (source + shift) % count) for source in range(count)]
        pieces.append(lax.ppermute(block, "group", route))
    stacked = jnp.stack(pieces)
    order = (lax.axis_index("group") - jnp.arange(count)) % count
    return jnp.take(stacked, order, axis=0).reshape(count * block.shape[0], block.shape[1])


def rms_scale(values, gain):
    square = jnp.mean(values * values, axis=-1, keepdims=True)
    return (values * lax.rsqrt(square + norm_eps) * gain).astype(jnp.bfloat16)


def rotate(values, places):
    half_dim = values.shape[-1] // 2
    frequency = rope_base ** (-(jnp.arange(half_dim, dtype=jnp.float32) * 2.0 / values.shape[-1]))
    angle = places.astype(jnp.float32)[:, None] * frequency[None, :]
    cosine = jnp.cos(angle)[:, None, :]
    sine = jnp.sin(angle)[:, None, :]
    widened = values.astype(jnp.float32)
    first = widened[..., :half_dim]
    second = widened[..., half_dim:]
    return jnp.concatenate(
        [first * cosine - second * sine, second * cosine + first * sine], axis=-1
    ).astype(jnp.bfloat16)


def by_core(own_part, other_part):
    first = lax.axis_index("core") == 0
    return jnp.where(first, own_part, other_part), jnp.where(first, other_part, own_part)


def dot(acts, weight):
    return jnp.dot(acts, weight, preferred_element_type=jnp.float32)


def dot_t(acts, weight_t):
    return lax.dot_general(
        acts, weight_t, (((1,), (1,)), ((), ())), preferred_element_type=jnp.float32
    )


def core_rows(values, chips, rows_dev):
    blocks = values.reshape(chips, 2, rows_dev, *values.shape[1:])
    own = lax.dynamic_index_in_dim(blocks, lax.axis_index("core"), axis=1, keepdims=False)
    return own.reshape(chips * rows_dev, *values.shape[1:])


def body(
    hidden,
    request_of,
    positions,
    page_table,
    attn_gain,
    mlp_gain,
    wq,
    wk,
    wv,
    wo,
    w_gate,
    w_up,
    w_down,
):
    chips = lax.axis_size("chip")
    rows_dev = hidden.shape[0]
    tok_group = request_of.shape[0]
    bf = jnp.bfloat16
    residual = hidden.astype(jnp.float32)
    q_cols = wq.shape[1]
    kv_half = wk.shape[1]
    own_attn = jnp.concatenate([wq.astype(bf), wk.astype(bf), wv.astype(bf), wo.astype(bf).T], axis=1)
    own_attn = lax.all_gather(own_attn, "group", axis=0, tiled=True)
    normed = gather_chip(rms_scale(residual, attn_gain), 0)
    other_attn = swap_cores(own_attn)
    query_w = jnp.concatenate([own_attn[:, :q_cols], other_attn[:, :q_cols]], axis=1)
    out_w_t = jnp.concatenate(
        [own_attn[:, q_cols + 2 * kv_half :], other_attn[:, q_cols + 2 * kv_half :]], axis=1
    )
    key_lo, key_hi = by_core(own_attn[:, q_cols : q_cols + kv_half], other_attn[:, q_cols : q_cols + kv_half])
    value_lo, value_hi = by_core(
        own_attn[:, q_cols + kv_half : q_cols + 2 * kv_half],
        other_attn[:, q_cols + kv_half : q_cols + 2 * kv_half],
    )
    key_w = jnp.concatenate([key_lo, key_hi], axis=1)
    value_w = jnp.concatenate([value_lo, value_hi], axis=1)
    ff_cols = w_gate.shape[1]
    own_mlp = jnp.concatenate([w_gate.astype(bf), w_up.astype(bf), w_down.astype(bf).T], axis=1)
    own_mlp = lax.all_gather(own_mlp, "group", axis=0, tiled=True)
    half_pos = core_rows(positions, chips, rows_dev)
    half_req = core_rows(request_of, chips, rows_dev)
    heads = 2 * q_cols // HD
    queries = rotate(dot(normed, query_w).astype(bf).reshape(-1, heads, HD), half_pos)
    keys_half = rotate(dot(normed, key_w).astype(bf).reshape(-1, 1, HD), half_pos)
    values_half = dot(normed, value_w).astype(bf).reshape(-1, 1, HD)
    kv_own = jnp.stack([keys_half[:, 0], values_half[:, 0]], axis=1)
    kv_other = swap_cores(kv_own)
    kv_lo, kv_hi = by_core(kv_own, kv_other)
    kv_rows = jnp.stack(
        [kv_lo.reshape(chips, rows_dev, 2, HD), kv_hi.reshape(chips, rows_dev, 2, HD)], axis=1
    ).reshape(tok_group, 2, HD)
    earlier_rows = min(MAXLEN, tok_group)
    earlier = from_behind(kv_rows[tok_group - earlier_rows :], "group", 1)
    all_rows = jnp.concatenate([earlier, kv_rows], axis=0)
    all_keys = all_rows[:, 0]
    all_values = all_rows[:, 1]
    first_request = request_of[0]
    first_position = positions[0]
    same_local = (half_req[:, None] == request_of[None, :]) & (
        positions[None, :] <= half_pos[:, None]
    )
    same_earlier = (half_req[:, None] == first_request) & (
        jnp.arange(earlier_rows)[None, :] >= earlier_rows - first_position
    )
    visible = jnp.concatenate([same_earlier, same_local], axis=1)
    scores = jnp.einsum(
        "qhd,kd->hqk", queries, all_keys, preferred_element_type=jnp.float32
    ) * HD ** (-0.5)
    scores = jnp.where(visible[None], scores, -1e30)
    row_peak = jnp.max(scores, axis=-1, keepdims=True)
    probs = jnp.where(visible[None], jnp.exp(scores - row_peak), 0.0)
    total = jnp.sum(probs, axis=-1, keepdims=True)
    mixed_heads = jnp.einsum(
        "hqk,kd->qhd", probs.astype(bf), all_values, preferred_element_type=jnp.float32
    ) / jnp.transpose(total, (1, 0, 2))
    attended = mixed_heads.astype(bf).reshape(-1, heads * HD)
    attn_part = dot_t(attended, out_w_t)
    attn_sum = scatter_chip(attn_part.astype(bf), 1)
    mixed = residual + attn_sum
    normed_mlp, other_mlp = gather_swap(rms_scale(mixed, mlp_gain), 2, own_mlp)
    gate_sum = jnp.concatenate(
        [dot(normed_mlp, own_mlp[:, :ff_cols]), dot(normed_mlp, other_mlp[:, :ff_cols])], axis=1
    )
    up_sum = jnp.concatenate(
        [
            dot(normed_mlp, own_mlp[:, ff_cols : 2 * ff_cols]),
            dot(normed_mlp, other_mlp[:, ff_cols : 2 * ff_cols]),
        ],
        axis=1,
    )
    activation = (jax.nn.silu(gate_sum) * up_sum).astype(bf)
    down_w_t = jnp.concatenate([own_mlp[:, 2 * ff_cols :], other_mlp[:, 2 * ff_cols :]], axis=1)
    down_part = dot_t(activation, down_w_t)
    layer_out = (mixed + scatter_chip(down_part.astype(bf), 3)).astype(bf)
    pages = page_table.shape[1]
    changed = jnp.concatenate(
        [jnp.ones((1,), jnp.int32), (request_of[1:] != request_of[:-1]).astype(jnp.int32)]
    )
    opens = jnp.maximum(changed, (positions % PAGE == 0).astype(jnp.int32))
    logical = jnp.cumsum(opens) - 1
    chosen = jnp.sum(
        jnp.where(logical[:, None] == jnp.arange(pages)[None, :], page_table, 0), axis=1
    )
    target = chosen * PAGE + positions % PAGE
    own_slice = lax.dynamic_index_in_dim(kv_rows, lax.axis_index("core"), axis=1, keepdims=False)
    width = own_slice.shape[1]
    cache = jnp.zeros((pages * PAGE, width), jnp.bfloat16).at[target].set(own_slice)
    return (layer_out, cache.reshape(pages, PAGE, width))


def solution(mesh):
    groups, tensors = mesh.devices.shape
    split = Mesh(mesh.devices.reshape(groups, tensors // 2, 2), ("group", "chip", "core"))
    tensor = ("chip", "core")
    placed = (
        P(("group",) + tensor, None),
        P("group"),
        P("group"),
        P("group", None),
        P(),
        P(),
        P("group", tensor),
        P("group", tensor),
        P("group", tensor),
        P(tensor, "group"),
        P("group", tensor),
        P("group", tensor),
        P(tensor, "group"),
    )
    return jax.shard_map(
        body,
        mesh=split,
        in_specs=placed,
        out_specs=(P(("group",) + tensor, None), P("group", None, tensor)),
        check_vma=False,
    )
```

```python
import functools

import jax
import jax.numpy as jnp
from jax import lax
from jax.experimental import pallas as pl
from jax.experimental.pallas import tpu as pltpu
from jax.sharding import Mesh
from jax.sharding import PartitionSpec as P

QH = 16
KVH = 8
HD = 128
PAGE = 128
MAXLEN = 512


rope_base = 1000000.0
norm_eps = 1e-06


def swap_cores(value):
    return lax.ppermute(value, "core", [(0, 1), (1, 0)])


def from_behind(block, axis, distance):
    devices = range(lax.axis_size(axis))
    route = [(i - distance, i) for i in devices if i - distance in devices]
    return lax.ppermute(block, axis, route)


def exchange_kernel(count, spread, spreads, swaps, *refs):
    source = refs[0]
    weights = refs[1] if (spreads or swaps) else None
    outs = refs[1 + (spreads or swaps) :]
    slots = outs[0]
    moved = outs[1] if (spreads or swaps) else None
    send_sems, recv_sems, local_sem = outs[-3:]
    me = lax.axis_index("chip")
    group = lax.axis_index("group")
    core = lax.axis_index("core")
    groups = lax.axis_size("group")
    mesh_ids = pl.DeviceIdType.MESH
    barrier = pltpu.get_barrier_semaphore()
    for shift in range(1, count):
        peer = lax.rem(me + shift, count)
        pl.semaphore_signal(barrier, inc=1, device_id=(group, peer, core), device_id_type=mesh_ids)
    greeted = count - 1
    if swaps:
        pl.semaphore_signal(barrier, inc=1, device_id=(group, me, 1 - core), device_id_type=mesh_ids)
        greeted += 1
    if spreads:
        for shift in range(1, groups):
            peer = lax.rem(group + shift, groups)
            pl.semaphore_signal(barrier, inc=1, device_id=(peer, me, core), device_id_type=mesh_ids)
        greeted += groups - 1
    pl.semaphore_wait(barrier, greeted)
    local = pltpu.make_async_copy(source.at[me] if spread else source, slots.at[me], local_sem.at[0])
    local.start()
    locals_ = [local]
    copies = []
    if swaps:
        swap = pltpu.make_async_remote_copy(
            src_ref=weights,
            dst_ref=moved,
            send_sem=send_sems.at[0],
            recv_sem=recv_sems.at[0],
            device_id=(group, me, 1 - core),
            device_id_type=mesh_ids,
        )
        swap.start()
        copies.append(swap)
    if spreads:
        own_weights = pltpu.make_async_copy(weights, moved.at[group], local_sem.at[1])
        own_weights.start()
        locals_.append(own_weights)
        for shift in range(1, groups):
            peer = lax.rem(group + shift, groups)
            copy = pltpu.make_async_remote_copy(
                src_ref=weights,
                dst_ref=moved.at[group],
                send_sem=send_sems.at[count + shift],
                recv_sem=recv_sems.at[count + shift],
                device_id=(peer, me, core),
                device_id_type=mesh_ids,
            )
            copy.start()
            copies.append(copy)
    for shift in range(1, count):
        peer = lax.rem(me + shift, count)
        copy = pltpu.make_async_remote_copy(
            src_ref=source.at[peer] if spread else source,
            dst_ref=slots.at[me],
            send_sem=send_sems.at[shift],
            recv_sem=recv_sems.at[shift],
            device_id=(group, peer, core),
            device_id_type=mesh_ids,
        )
        copy.start()
        copies.append(copy)
    for shift in range(1, count):
        sender = lax.rem(me + count - shift, count)
        pltpu.make_async_remote_copy(
            src_ref=slots.at[sender],
            dst_ref=slots.at[sender],
            send_sem=send_sems.at[shift],
            recv_sem=recv_sems.at[shift],
            device_id=(group, sender, core),
            device_id_type=mesh_ids,
        ).wait_recv()
    if swaps:
        swap.wait_recv()
    if spreads:
        for shift in range(1, groups):
            sender = lax.rem(group + groups - shift, groups)
            pltpu.make_async_remote_copy(
                src_ref=moved.at[sender],
                dst_ref=moved.at[sender],
                send_sem=send_sems.at[count + shift],
                recv_sem=recv_sems.at[count + shift],
                device_id=(sender, me, core),
                device_id_type=mesh_ids,
            ).wait_recv()
    for copy in copies:
        copy.wait_send()
    for copy in locals_:
        copy.wait()


def exchange(block, spread, tag, weights=None, spreads=False):
    count = lax.axis_size("chip")
    groups = lax.axis_size("group")
    rows, cols = block.shape[-2:]
    moved = count * rows * cols * block.dtype.itemsize
    out_shape = [jax.ShapeDtypeStruct((count, rows, cols), block.dtype)]
    operands = [block]
    swaps = weights is not None and not spreads
    if weights is not None:
        copies = groups if spreads else 1
        out_shape.append(jax.ShapeDtypeStruct((copies,) * spreads + weights.shape, weights.dtype))
        operands.append(weights)
        moved += copies * weights.size * weights.dtype.itemsize
    outs = pl.pallas_call(
        functools.partial(exchange_kernel, count, spread, spreads, swaps),
        out_shape=tuple(out_shape),
        in_specs=[pl.BlockSpec(memory_space=pl.ANY)] * len(operands),
        out_specs=tuple(pl.BlockSpec(memory_space=pl.ANY) for _ in out_shape),
        scratch_shapes=[
            pltpu.SemaphoreType.DMA((count + groups,)),
            pltpu.SemaphoreType.DMA((count + groups,)),
            pltpu.SemaphoreType.DMA((2,)),
        ],
        compiler_params=pltpu.CompilerParams(collective_id=tag, has_side_effects=True),
        cost_estimate=pl.CostEstimate(flops=0, bytes_accessed=2 * moved, transcendentals=0),
    )(*operands)
    return outs


def gather_chip(block, tag):
    outs = exchange(block, False, tag)
    return outs[0].reshape(-1, block.shape[1])


def gather_swap(block, tag, weights):
    outs = exchange(block, False, tag, weights)
    return outs[0].reshape(-1, block.shape[1]), outs[1]


def scatter_chip(partial, tag):
    count = lax.axis_size("chip")
    outs = exchange(partial.reshape(count, -1, partial.shape[1]), True, tag)
    return jnp.sum(outs[0].astype(jnp.float32), axis=0)


def mlp_kernel(count, ff, own_block, weights, rs_out, own_w, other_w, slots, partials, ag_send, ag_recv, rs_send, rs_recv, swap_sems, local_sems):
    me = lax.axis_index("chip")
    group = lax.axis_index("group")
    core = lax.axis_index("core")
    mesh_ids = pl.DeviceIdType.MESH
    barrier = pltpu.get_barrier_semaphore()
    for shift in range(1, count):
        peer = lax.rem(me + shift, count)
        pl.semaphore_signal(barrier, inc=1, device_id=(group, peer, core), device_id_type=mesh_ids)
    pl.semaphore_signal(barrier, inc=1, device_id=(group, me, 1 - core), device_id_type=mesh_ids)
    pl.semaphore_wait(barrier, count)
    load_w = pltpu.make_async_copy(weights, own_w, local_sems.at[0])
    load_w.start()
    load_x = pltpu.make_async_copy(own_block, slots.at[me], local_sems.at[1])
    load_x.start()
    swap = pltpu.make_async_remote_copy(
        src_ref=weights,
        dst_ref=other_w,
        send_sem=swap_sems.at[0],
        recv_sem=swap_sems.at[1],
        device_id=(group, me, 1 - core),
        device_id_type=mesh_ids,
    )
    swap.start()
    sends = [swap]
    for shift in range(1, count):
        peer = lax.rem(me + shift, count)
        copy = pltpu.make_async_remote_copy(
            src_ref=own_block,
            dst_ref=slots.at[me],
            send_sem=ag_send.at[shift],
            recv_sem=ag_recv.at[shift],
            device_id=(group, peer, core),
            device_id_type=mesh_ids,
        )
        copy.start()
        sends.append(copy)
    load_w.wait()
    swap.wait_recv()
    load_x.wait()
    outs = []
    for shift in range(count):
        sender = lax.rem(me + count - shift, count)
        if shift > 0:
            pltpu.make_async_remote_copy(
                src_ref=slots.at[sender],
                dst_ref=slots.at[sender],
                send_sem=ag_send.at[shift],
                recv_sem=ag_recv.at[shift],
                device_id=(group, sender, core),
                device_id_type=mesh_ids,
            ).wait_recv()
        rows = slots[sender]
        total = None
        for table in (own_w, other_w):
            gate = jnp.dot(rows, table[:, pl.ds(0, ff)], preferred_element_type=jnp.float32)
            up = jnp.dot(rows, table[:, pl.ds(ff, ff)], preferred_element_type=jnp.float32)
            act = (gate / (1.0 + jnp.exp(-gate)) * up).astype(jnp.bfloat16)
            down = lax.dot_general(
                act, table[:, pl.ds(2 * ff, ff)], (((1,), (1,)), ((), ())),
                preferred_element_type=jnp.float32,
            )
            total = down if total is None else total + down
        partials[shift] = total.astype(jnp.bfloat16)
        if shift == 0:
            back = pltpu.make_async_copy(partials.at[0], rs_out.at[me], local_sems.at[2])
        else:
            back = pltpu.make_async_remote_copy(
                src_ref=partials.at[shift],
                dst_ref=rs_out.at[me],
                send_sem=rs_send.at[shift],
                recv_sem=rs_recv.at[shift],
                device_id=(group, sender, core),
                device_id_type=mesh_ids,
            )
        back.start()
        outs.append(back)
    for shift in range(1, count):
        owner = lax.rem(me + shift, count)
        pltpu.make_async_remote_copy(
            src_ref=partials.at[shift],
            dst_ref=rs_out.at[owner],
            send_sem=rs_send.at[shift],
            recv_sem=rs_recv.at[shift],
            device_id=(group, owner, core),
            device_id_type=mesh_ids,
        ).wait_recv()
    outs[0].wait()
    for copy in outs[1:]:
        copy.wait_send()
    for copy in sends:
        copy.wait_send()


def fused_mlp(block, weights, tag):
    count = lax.axis_size("chip")
    rows, cols = block.shape
    ff = weights.shape[1] // 3
    flops = 2 * count * rows * cols * ff * 6
    return pl.pallas_call(
        functools.partial(mlp_kernel, count, ff),
        out_shape=jax.ShapeDtypeStruct((count, rows, cols), block.dtype),
        in_specs=[pl.BlockSpec(memory_space=pl.ANY)] * 2,
        out_specs=pl.BlockSpec(memory_space=pl.ANY),
        scratch_shapes=[
            pltpu.VMEM(weights.shape, weights.dtype),
            pltpu.VMEM(weights.shape, weights.dtype),
            pltpu.VMEM((count, rows, cols), block.dtype),
            pltpu.VMEM((count, rows, cols), block.dtype),
            pltpu.SemaphoreType.DMA((count,)),
            pltpu.SemaphoreType.DMA((count,)),
            pltpu.SemaphoreType.DMA((count,)),
            pltpu.SemaphoreType.DMA((count,)),
            pltpu.SemaphoreType.DMA((2,)),
            pltpu.SemaphoreType.DMA((3,)),
        ],
        compiler_params=pltpu.CompilerParams(
            collective_id=tag, has_side_effects=True, vmem_limit_bytes=60 * 1024 * 1024
        ),
        cost_estimate=pl.CostEstimate(
            flops=flops, bytes_accessed=4 * count * rows * cols * 2, transcendentals=count * rows * ff * 2
        ),
    )(block, weights)


def gather_group(block):
    count = lax.axis_size("group")
    pieces = [block]
    for shift in range(1, count):
        route = [(source, (source + shift) % count) for source in range(count)]
        pieces.append(lax.ppermute(block, "group", route))
    stacked = jnp.stack(pieces)
    order = (lax.axis_index("group") - jnp.arange(count)) % count
    return jnp.take(stacked, order, axis=0).reshape(count * block.shape[0], block.shape[1])


def rms_scale(values, gain):
    square = jnp.mean(values * values, axis=-1, keepdims=True)
    return (values * lax.rsqrt(square + norm_eps) * gain).astype(jnp.bfloat16)


def rotate(values, places):
    half_dim = values.shape[-1] // 2
    frequency = rope_base ** (-(jnp.arange(half_dim, dtype=jnp.float32) * 2.0 / values.shape[-1]))
    angle = places.astype(jnp.float32)[:, None] * frequency[None, :]
    cosine = jnp.cos(angle)[:, None, :]
    sine = jnp.sin(angle)[:, None, :]
    widened = values.astype(jnp.float32)
    first = widened[..., :half_dim]
    second = widened[..., half_dim:]
    return jnp.concatenate(
        [first * cosine - second * sine, second * cosine + first * sine], axis=-1
    ).astype(jnp.bfloat16)


def by_core(own_part, other_part):
    first = lax.axis_index("core") == 0
    return jnp.where(first, own_part, other_part), jnp.where(first, other_part, own_part)


def dot(acts, weight):
    return jnp.dot(acts, weight, preferred_element_type=jnp.float32)


def dot_t(acts, weight_t):
    return lax.dot_general(
        acts, weight_t, (((1,), (1,)), ((), ())), preferred_element_type=jnp.float32
    )


def core_rows(values, chips, rows_dev):
    blocks = values.reshape(chips, 2, rows_dev, *values.shape[1:])
    own = lax.dynamic_index_in_dim(blocks, lax.axis_index("core"), axis=1, keepdims=False)
    return own.reshape(chips * rows_dev, *values.shape[1:])


def body(
    hidden,
    request_of,
    positions,
    page_table,
    attn_gain,
    mlp_gain,
    wq,
    wk,
    wv,
    wo,
    w_gate,
    w_up,
    w_down,
):
    chips = lax.axis_size("chip")
    rows_dev = hidden.shape[0]
    tok_group = request_of.shape[0]
    bf = jnp.bfloat16
    residual = hidden.astype(jnp.float32)
    q_cols = wq.shape[1]
    kv_half = wk.shape[1]
    own_attn = jnp.concatenate([wq.astype(bf), wk.astype(bf), wv.astype(bf), wo.astype(bf).T], axis=1)
    own_attn = lax.all_gather(own_attn, "group", axis=0, tiled=True)
    normed = gather_chip(rms_scale(residual, attn_gain), 0)
    other_attn = swap_cores(own_attn)
    query_w = jnp.concatenate([own_attn[:, :q_cols], other_attn[:, :q_cols]], axis=1)
    out_w_t = jnp.concatenate(
        [own_attn[:, q_cols + 2 * kv_half :], other_attn[:, q_cols + 2 * kv_half :]], axis=1
    )
    key_lo, key_hi = by_core(own_attn[:, q_cols : q_cols + kv_half], other_attn[:, q_cols : q_cols + kv_half])
    value_lo, value_hi = by_core(
        own_attn[:, q_cols + kv_half : q_cols + 2 * kv_half],
        other_attn[:, q_cols + kv_half : q_cols + 2 * kv_half],
    )
    key_w = jnp.concatenate([key_lo, key_hi], axis=1)
    value_w = jnp.concatenate([value_lo, value_hi], axis=1)
    ff_cols = w_gate.shape[1]
    own_mlp = jnp.concatenate([w_gate.astype(bf), w_up.astype(bf), w_down.astype(bf).T], axis=1)
    own_mlp = lax.all_gather(own_mlp, "group", axis=0, tiled=True)
    half_pos = core_rows(positions, chips, rows_dev)
    half_req = core_rows(request_of, chips, rows_dev)
    heads = 2 * q_cols // HD
    queries = rotate(dot(normed, query_w).astype(bf).reshape(-1, heads, HD), half_pos)
    keys_half = rotate(dot(normed, key_w).astype(bf).reshape(-1, 1, HD), half_pos)
    values_half = dot(normed, value_w).astype(bf).reshape(-1, 1, HD)
    kv_own = jnp.stack([keys_half[:, 0], values_half[:, 0]], axis=1)
    kv_other = swap_cores(kv_own)
    kv_lo, kv_hi = by_core(kv_own, kv_other)
    kv_rows = jnp.stack(
        [kv_lo.reshape(chips, rows_dev, 2, HD), kv_hi.reshape(chips, rows_dev, 2, HD)], axis=1
    ).reshape(tok_group, 2, HD)
    earlier_rows = min(MAXLEN, tok_group)
    earlier = from_behind(kv_rows[tok_group - earlier_rows :], "group", 1)
    all_rows = jnp.concatenate([earlier, kv_rows], axis=0)
    all_keys = all_rows[:, 0]
    all_values = all_rows[:, 1]
    first_request = request_of[0]
    first_position = positions[0]
    same_local = (half_req[:, None] == request_of[None, :]) & (
        positions[None, :] <= half_pos[:, None]
    )
    same_earlier = (half_req[:, None] == first_request) & (
        jnp.arange(earlier_rows)[None, :] >= earlier_rows - first_position
    )
    visible = jnp.concatenate([same_earlier, same_local], axis=1)
    scores = jnp.einsum(
        "qhd,kd->hqk", queries, all_keys, preferred_element_type=jnp.float32
    ) * HD ** (-0.5)
    scores = jnp.where(visible[None], scores, -1e30)
    row_peak = jnp.max(scores, axis=-1, keepdims=True)
    probs = jnp.where(visible[None], jnp.exp(scores - row_peak), 0.0)
    total = jnp.sum(probs, axis=-1, keepdims=True)
    mixed_heads = jnp.einsum(
        "hqk,kd->qhd", probs.astype(bf), all_values, preferred_element_type=jnp.float32
    ) / jnp.transpose(total, (1, 0, 2))
    attended = mixed_heads.astype(bf).reshape(-1, heads * HD)
    attn_part = dot_t(attended, out_w_t)
    attn_sum = scatter_chip(attn_part.astype(bf), 1)
    mixed = residual + attn_sum
    partials = fused_mlp(rms_scale(mixed, mlp_gain), own_mlp, 2)
    layer_out = (mixed + jnp.sum(partials.astype(jnp.float32), axis=0)).astype(bf)
    pages = page_table.shape[1]
    changed = jnp.concatenate(
        [jnp.ones((1,), jnp.int32), (request_of[1:] != request_of[:-1]).astype(jnp.int32)]
    )
    opens = jnp.maximum(changed, (positions % PAGE == 0).astype(jnp.int32))
    logical = jnp.cumsum(opens) - 1
    chosen = jnp.sum(
        jnp.where(logical[:, None] == jnp.arange(pages)[None, :], page_table, 0), axis=1
    )
    target = chosen * PAGE + positions % PAGE
    own_slice = lax.dynamic_index_in_dim(kv_rows, lax.axis_index("core"), axis=1, keepdims=False)
    width = own_slice.shape[1]
    cache = jnp.zeros((pages * PAGE, width), jnp.bfloat16).at[target].set(own_slice)
    return (layer_out, cache.reshape(pages, PAGE, width))


def solution(mesh):
    groups, tensors = mesh.devices.shape
    split = Mesh(mesh.devices.reshape(groups, tensors // 2, 2), ("group", "chip", "core"))
    tensor = ("chip", "core")
    placed = (
        P(("group",) + tensor, None),
        P("group"),
        P("group"),
        P("group", None),
        P(),
        P(),
        P("group", tensor),
        P("group", tensor),
        P("group", tensor),
        P(tensor, "group"),
        P("group", tensor),
        P("group", tensor),
        P(tensor, "group"),
    )
    return jax.shard_map(
        body,
        mesh=split,
        in_specs=placed,
        out_specs=(P(("group",) + tensor, None), P("group", None, tensor)),
        check_vma=False,
    )
```

```python
import functools

import jax
import jax.numpy as jnp
from jax import lax
from jax.experimental import pallas as pl
from jax.experimental.pallas import tpu as pltpu
from jax.sharding import Mesh
from jax.sharding import PartitionSpec as P

QH = 16
KVH = 8
HD = 128
PAGE = 128
MAXLEN = 512


rope_base = 1000000.0
norm_eps = 1e-06


def swap_cores(value):
    return lax.ppermute(value, "core", [(0, 1), (1, 0)])


def from_behind(block, axis, distance):
    devices = range(lax.axis_size(axis))
    route = [(i - distance, i) for i in devices if i - distance in devices]
    return lax.ppermute(block, axis, route)


def exchange_kernel(count, spread, spreads, swaps, *refs):
    source = refs[0]
    weights = refs[1] if (spreads or swaps) else None
    outs = refs[1 + (spreads or swaps) :]
    slots = outs[0]
    moved = outs[1] if (spreads or swaps) else None
    send_sems, recv_sems, local_sem = outs[-3:]
    me = lax.axis_index("chip")
    group = lax.axis_index("group")
    core = lax.axis_index("core")
    groups = lax.axis_size("group")
    mesh_ids = pl.DeviceIdType.MESH
    barrier = pltpu.get_barrier_semaphore()
    for shift in range(1, count):
        peer = lax.rem(me + shift, count)
        pl.semaphore_signal(barrier, inc=1, device_id=(group, peer, core), device_id_type=mesh_ids)
    greeted = count - 1
    if swaps:
        pl.semaphore_signal(barrier, inc=1, device_id=(group, me, 1 - core), device_id_type=mesh_ids)
        greeted += 1
    if spreads:
        for shift in range(1, groups):
            peer = lax.rem(group + shift, groups)
            pl.semaphore_signal(barrier, inc=1, device_id=(peer, me, core), device_id_type=mesh_ids)
        greeted += groups - 1
    pl.semaphore_wait(barrier, greeted)
    local = pltpu.make_async_copy(source.at[me] if spread else source, slots.at[me], local_sem.at[0])
    local.start()
    locals_ = [local]
    copies = []
    if swaps:
        swap = pltpu.make_async_remote_copy(
            src_ref=weights,
            dst_ref=moved,
            send_sem=send_sems.at[0],
            recv_sem=recv_sems.at[0],
            device_id=(group, me, 1 - core),
            device_id_type=mesh_ids,
        )
        swap.start()
        copies.append(swap)
    if spreads:
        own_weights = pltpu.make_async_copy(weights, moved.at[group], local_sem.at[1])
        own_weights.start()
        locals_.append(own_weights)
        for shift in range(1, groups):
            peer = lax.rem(group + shift, groups)
            copy = pltpu.make_async_remote_copy(
                src_ref=weights,
                dst_ref=moved.at[group],
                send_sem=send_sems.at[count + shift],
                recv_sem=recv_sems.at[count + shift],
                device_id=(peer, me, core),
                device_id_type=mesh_ids,
            )
            copy.start()
            copies.append(copy)
    for shift in range(1, count):
        peer = lax.rem(me + shift, count)
        copy = pltpu.make_async_remote_copy(
            src_ref=source.at[peer] if spread else source,
            dst_ref=slots.at[me],
            send_sem=send_sems.at[shift],
            recv_sem=recv_sems.at[shift],
            device_id=(group, peer, core),
            device_id_type=mesh_ids,
        )
        copy.start()
        copies.append(copy)
    for shift in range(1, count):
        sender = lax.rem(me + count - shift, count)
        pltpu.make_async_remote_copy(
            src_ref=slots.at[sender],
            dst_ref=slots.at[sender],
            send_sem=send_sems.at[shift],
            recv_sem=recv_sems.at[shift],
            device_id=(group, sender, core),
            device_id_type=mesh_ids,
        ).wait_recv()
    if swaps:
        swap.wait_recv()
    if spreads:
        for shift in range(1, groups):
            sender = lax.rem(group + groups - shift, groups)
            pltpu.make_async_remote_copy(
                src_ref=moved.at[sender],
                dst_ref=moved.at[sender],
                send_sem=send_sems.at[count + shift],
                recv_sem=recv_sems.at[count + shift],
                device_id=(sender, me, core),
                device_id_type=mesh_ids,
            ).wait_recv()
    for copy in copies:
        copy.wait_send()
    for copy in locals_:
        copy.wait()


def exchange(block, spread, tag, weights=None, spreads=False):
    count = lax.axis_size("chip")
    groups = lax.axis_size("group")
    rows, cols = block.shape[-2:]
    moved = count * rows * cols * block.dtype.itemsize
    out_shape = [jax.ShapeDtypeStruct((count, rows, cols), block.dtype)]
    operands = [block]
    swaps = weights is not None and not spreads
    if weights is not None:
        copies = groups if spreads else 1
        out_shape.append(jax.ShapeDtypeStruct((copies,) * spreads + weights.shape, weights.dtype))
        operands.append(weights)
        moved += copies * weights.size * weights.dtype.itemsize
    outs = pl.pallas_call(
        functools.partial(exchange_kernel, count, spread, spreads, swaps),
        out_shape=tuple(out_shape),
        in_specs=[pl.BlockSpec(memory_space=pl.ANY)] * len(operands),
        out_specs=tuple(pl.BlockSpec(memory_space=pl.ANY) for _ in out_shape),
        scratch_shapes=[
            pltpu.SemaphoreType.DMA((count + groups,)),
            pltpu.SemaphoreType.DMA((count + groups,)),
            pltpu.SemaphoreType.DMA((2,)),
        ],
        compiler_params=pltpu.CompilerParams(collective_id=tag, has_side_effects=True),
        cost_estimate=pl.CostEstimate(flops=0, bytes_accessed=2 * moved, transcendentals=0),
    )(*operands)
    return outs


def gather_chip(block, tag):
    outs = exchange(block, False, tag)
    return outs[0].reshape(-1, block.shape[1])


def gather_swap(block, tag, weights):
    outs = exchange(block, False, tag, weights)
    return outs[0].reshape(-1, block.shape[1]), outs[1]


def scatter_chip(partial, tag):
    count = lax.axis_size("chip")
    outs = exchange(partial.reshape(count, -1, partial.shape[1]), True, tag)
    return jnp.sum(outs[0].astype(jnp.float32), axis=0)


def mlp_kernel(count, ff, own_block, weights, rs_out, own_w, other_w, slots, partials, ag_send, ag_recv, rs_send, rs_recv, swap_sems, local_sems):
    me = lax.axis_index("chip")
    group = lax.axis_index("group")
    core = lax.axis_index("core")
    mesh_ids = pl.DeviceIdType.MESH
    barrier = pltpu.get_barrier_semaphore()
    for shift in range(1, count):
        peer = lax.rem(me + shift, count)
        pl.semaphore_signal(barrier, inc=1, device_id=(group, peer, core), device_id_type=mesh_ids)
    pl.semaphore_signal(barrier, inc=1, device_id=(group, me, 1 - core), device_id_type=mesh_ids)
    pl.semaphore_wait(barrier, count)
    load_w = pltpu.make_async_copy(weights, own_w, local_sems.at[0])
    load_w.start()
    load_x = pltpu.make_async_copy(own_block, slots.at[me], local_sems.at[1])
    load_x.start()
    swap = pltpu.make_async_remote_copy(
        src_ref=weights,
        dst_ref=other_w,
        send_sem=swap_sems.at[0],
        recv_sem=swap_sems.at[1],
        device_id=(group, me, 1 - core),
        device_id_type=mesh_ids,
    )
    swap.start()
    sends = [swap]
    for shift in range(1, count):
        peer = lax.rem(me + shift, count)
        copy = pltpu.make_async_remote_copy(
            src_ref=own_block,
            dst_ref=slots.at[me],
            send_sem=ag_send.at[shift],
            recv_sem=ag_recv.at[shift],
            device_id=(group, peer, core),
            device_id_type=mesh_ids,
        )
        copy.start()
        sends.append(copy)
    load_w.wait()
    swap.wait_recv()
    load_x.wait()
    outs = []
    for shift in range(count):
        sender = lax.rem(me + count - shift, count)
        if shift > 0:
            pltpu.make_async_remote_copy(
                src_ref=slots.at[sender],
                dst_ref=slots.at[sender],
                send_sem=ag_send.at[shift],
                recv_sem=ag_recv.at[shift],
                device_id=(group, sender, core),
                device_id_type=mesh_ids,
            ).wait_recv()
        rows = slots[sender]
        total = None
        for table in (own_w, other_w):
            gate = jnp.dot(rows, table[:, pl.ds(0, ff)], preferred_element_type=jnp.float32)
            up = jnp.dot(rows, table[:, pl.ds(ff, ff)], preferred_element_type=jnp.float32)
            act = (gate / (1.0 + jnp.exp(-gate)) * up).astype(jnp.bfloat16)
            down = lax.dot_general(
                act, table[:, pl.ds(2 * ff, ff)], (((1,), (1,)), ((), ())),
                preferred_element_type=jnp.float32,
            )
            total = down if total is None else total + down
        partials[shift] = total.astype(jnp.bfloat16)
        if shift == 0:
            back = pltpu.make_async_copy(partials.at[0], rs_out.at[me], local_sems.at[2])
        else:
            back = pltpu.make_async_remote_copy(
                src_ref=partials.at[shift],
                dst_ref=rs_out.at[me],
                send_sem=rs_send.at[shift],
                recv_sem=rs_recv.at[shift],
                device_id=(group, sender, core),
                device_id_type=mesh_ids,
            )
        back.start()
        outs.append(back)
    for shift in range(1, count):
        owner = lax.rem(me + shift, count)
        pltpu.make_async_remote_copy(
            src_ref=partials.at[shift],
            dst_ref=rs_out.at[owner],
            send_sem=rs_send.at[shift],
            recv_sem=rs_recv.at[shift],
            device_id=(group, owner, core),
            device_id_type=mesh_ids,
        ).wait_recv()
    outs[0].wait()
    for copy in outs[1:]:
        copy.wait_send()
    for copy in sends:
        copy.wait_send()


def fused_mlp(block, weights, tag):
    count = lax.axis_size("chip")
    rows, cols = block.shape
    ff = weights.shape[1] // 3
    flops = 2 * count * rows * cols * ff * 6
    return pl.pallas_call(
        functools.partial(mlp_kernel, count, ff),
        out_shape=jax.ShapeDtypeStruct((count, rows, cols), block.dtype),
        in_specs=[pl.BlockSpec(memory_space=pl.ANY)] * 2,
        out_specs=pl.BlockSpec(memory_space=pl.ANY),
        scratch_shapes=[
            pltpu.VMEM(weights.shape, weights.dtype),
            pltpu.VMEM(weights.shape, weights.dtype),
            pltpu.VMEM((count, rows, cols), block.dtype),
            pltpu.VMEM((count, rows, cols), block.dtype),
            pltpu.SemaphoreType.DMA((count,)),
            pltpu.SemaphoreType.DMA((count,)),
            pltpu.SemaphoreType.DMA((count,)),
            pltpu.SemaphoreType.DMA((count,)),
            pltpu.SemaphoreType.DMA((2,)),
            pltpu.SemaphoreType.DMA((3,)),
        ],
        compiler_params=pltpu.CompilerParams(
            collective_id=tag, has_side_effects=True, vmem_limit_bytes=60 * 1024 * 1024
        ),
        cost_estimate=pl.CostEstimate(
            flops=flops, bytes_accessed=4 * count * rows * cols * 2, transcendentals=count * rows * ff * 2
        ),
    )(block, weights)


def attend_kernel(count, heads, queries, keys, values, out_w_t, query_req, query_pos, key_req, key_pos, rs_out, partials, rs_send, rs_recv, local_sem):
    me = lax.axis_index("chip")
    group = lax.axis_index("group")
    core = lax.axis_index("core")
    mesh_ids = pl.DeviceIdType.MESH
    rows = rs_out.shape[1]
    barrier = pltpu.get_barrier_semaphore()
    for shift in range(1, count):
        peer = lax.rem(me + shift, count)
        pl.semaphore_signal(barrier, inc=1, device_id=(group, peer, core), device_id_type=mesh_ids)
    pl.semaphore_wait(barrier, count - 1)
    key_block = keys[...]
    value_block = values[...]
    visible_req = key_req[...]
    visible_pos = key_pos[...]
    sends = []
    for step in range(count):
        shift = (step + 1) % count
        peer = lax.rem(me + shift, count)
        start = pl.multiple_of(peer * rows, 8)
        own_req = query_req[pl.ds(start, rows), :]
        own_pos = query_pos[pl.ds(start, rows), :]
        visible = (own_req == visible_req) & (visible_pos <= own_pos)
        mixed = []
        for head in range(heads):
            q = queries[pl.ds(start, rows), pl.ds(head * HD, HD)]
            scores = lax.dot_general(
                q, key_block, (((1,), (1,)), ((), ())), preferred_element_type=jnp.float32
            ) * HD ** (-0.5)
            scores = jnp.where(visible, scores, -1e30)
            peak = jnp.max(scores, axis=1, keepdims=True)
            probs = jnp.where(visible, jnp.exp(scores - peak), 0.0)
            total = jnp.sum(probs, axis=1, keepdims=True)
            head_out = jnp.dot(probs.astype(jnp.bfloat16), value_block, preferred_element_type=jnp.float32)
            mixed.append((head_out / total).astype(jnp.bfloat16))
        attended = jnp.concatenate(mixed, axis=1)
        partial = lax.dot_general(
            attended, out_w_t[...], (((1,), (1,)), ((), ())), preferred_element_type=jnp.float32
        )
        partials[shift] = partial.astype(jnp.bfloat16)
        if shift == 0:
            back = pltpu.make_async_copy(partials.at[0], rs_out.at[me], local_sem)
        else:
            back = pltpu.make_async_remote_copy(
                src_ref=partials.at[shift],
                dst_ref=rs_out.at[me],
                send_sem=rs_send.at[shift],
                recv_sem=rs_recv.at[shift],
                device_id=(group, peer, core),
                device_id_type=mesh_ids,
            )
        back.start()
        sends.append((shift, back))
    for shift in range(1, count):
        source = lax.rem(me + count - shift, count)
        pltpu.make_async_remote_copy(
            src_ref=partials.at[shift],
            dst_ref=rs_out.at[source],
            send_sem=rs_send.at[shift],
            recv_sem=rs_recv.at[shift],
            device_id=(group, source, core),
            device_id_type=mesh_ids,
        ).wait_recv()
    for shift, copy in sends:
        if shift == 0:
            copy.wait()
        else:
            copy.wait_send()


def fused_attention(queries, keys, values, out_w_t, query_req, query_pos, key_req, key_pos, tag):
    count = lax.axis_size("chip")
    rows = queries.shape[0] // count
    cols = out_w_t.shape[0]
    heads = queries.shape[1] // HD
    vmem = pl.BlockSpec(memory_space=pltpu.VMEM)
    flops = 2 * queries.shape[0] * keys.shape[0] * HD * 2 * heads + 2 * queries.shape[0] * queries.shape[1] * cols
    return pl.pallas_call(
        functools.partial(attend_kernel, count, heads),
        out_shape=jax.ShapeDtypeStruct((count, rows, cols), jnp.bfloat16),
        in_specs=[vmem] * 8,
        out_specs=pl.BlockSpec(memory_space=pl.ANY),
        scratch_shapes=[
            pltpu.VMEM((count, rows, cols), jnp.bfloat16),
            pltpu.SemaphoreType.DMA((count,)),
            pltpu.SemaphoreType.DMA((count,)),
            pltpu.SemaphoreType.DMA(()),
        ],
        compiler_params=pltpu.CompilerParams(
            collective_id=tag, has_side_effects=True, vmem_limit_bytes=48 * 1024 * 1024
        ),
        cost_estimate=pl.CostEstimate(
            flops=flops, bytes_accessed=2 * count * rows * cols * 2, transcendentals=queries.shape[0] * keys.shape[0] * heads
        ),
    )(queries, keys, values, out_w_t, query_req, query_pos, key_req, key_pos)


def gather_group(block):
    count = lax.axis_size("group")
    pieces = [block]
    for shift in range(1, count):
        route = [(source, (source + shift) % count) for source in range(count)]
        pieces.append(lax.ppermute(block, "group", route))
    stacked = jnp.stack(pieces)
    order = (lax.axis_index("group") - jnp.arange(count)) % count
    return jnp.take(stacked, order, axis=0).reshape(count * block.shape[0], block.shape[1])


def rms_scale(values, gain):
    square = jnp.mean(values * values, axis=-1, keepdims=True)
    return (values * lax.rsqrt(square + norm_eps) * gain).astype(jnp.bfloat16)


def rotate(values, places):
    half_dim = values.shape[-1] // 2
    frequency = rope_base ** (-(jnp.arange(half_dim, dtype=jnp.float32) * 2.0 / values.shape[-1]))
    angle = places.astype(jnp.float32)[:, None] * frequency[None, :]
    cosine = jnp.cos(angle)[:, None, :]
    sine = jnp.sin(angle)[:, None, :]
    widened = values.astype(jnp.float32)
    first = widened[..., :half_dim]
    second = widened[..., half_dim:]
    return jnp.concatenate(
        [first * cosine - second * sine, second * cosine + first * sine], axis=-1
    ).astype(jnp.bfloat16)


def by_core(own_part, other_part):
    first = lax.axis_index("core") == 0
    return jnp.where(first, own_part, other_part), jnp.where(first, other_part, own_part)


def dot(acts, weight):
    return jnp.dot(acts, weight, preferred_element_type=jnp.float32)


def dot_t(acts, weight_t):
    return lax.dot_general(
        acts, weight_t, (((1,), (1,)), ((), ())), preferred_element_type=jnp.float32
    )


def core_rows(values, chips, rows_dev):
    blocks = values.reshape(chips, 2, rows_dev, *values.shape[1:])
    own = lax.dynamic_index_in_dim(blocks, lax.axis_index("core"), axis=1, keepdims=False)
    return own.reshape(chips * rows_dev, *values.shape[1:])


def body(
    hidden,
    request_of,
    positions,
    page_table,
    attn_gain,
    mlp_gain,
    wq,
    wk,
    wv,
    wo,
    w_gate,
    w_up,
    w_down,
):
    chips = lax.axis_size("chip")
    rows_dev = hidden.shape[0]
    tok_group = request_of.shape[0]
    bf = jnp.bfloat16
    residual = hidden.astype(jnp.float32)
    q_cols = wq.shape[1]
    kv_half = wk.shape[1]
    own_attn = jnp.concatenate([wq.astype(bf), wk.astype(bf), wv.astype(bf), wo.astype(bf).T], axis=1)
    own_attn = lax.all_gather(own_attn, "group", axis=0, tiled=True)
    normed = gather_chip(rms_scale(residual, attn_gain), 0)
    other_attn = swap_cores(own_attn)
    query_w = jnp.concatenate([own_attn[:, :q_cols], other_attn[:, :q_cols]], axis=1)
    out_w_t = jnp.concatenate(
        [own_attn[:, q_cols + 2 * kv_half :], other_attn[:, q_cols + 2 * kv_half :]], axis=1
    )
    key_lo, key_hi = by_core(own_attn[:, q_cols : q_cols + kv_half], other_attn[:, q_cols : q_cols + kv_half])
    value_lo, value_hi = by_core(
        own_attn[:, q_cols + kv_half : q_cols + 2 * kv_half],
        other_attn[:, q_cols + kv_half : q_cols + 2 * kv_half],
    )
    key_w = jnp.concatenate([key_lo, key_hi], axis=1)
    value_w = jnp.concatenate([value_lo, value_hi], axis=1)
    ff_cols = w_gate.shape[1]
    own_mlp = jnp.concatenate([w_gate.astype(bf), w_up.astype(bf), w_down.astype(bf).T], axis=1)
    own_mlp = lax.all_gather(own_mlp, "group", axis=0, tiled=True)
    half_pos = core_rows(positions, chips, rows_dev)
    half_req = core_rows(request_of, chips, rows_dev)
    heads = 2 * q_cols // HD
    queries = rotate(dot(normed, query_w).astype(bf).reshape(-1, heads, HD), half_pos)
    keys_half = rotate(dot(normed, key_w).astype(bf).reshape(-1, 1, HD), half_pos)
    values_half = dot(normed, value_w).astype(bf).reshape(-1, 1, HD)
    kv_own = jnp.stack([keys_half[:, 0], values_half[:, 0]], axis=1)
    kv_other = swap_cores(kv_own)
    kv_lo, kv_hi = by_core(kv_own, kv_other)
    kv_rows = jnp.stack(
        [kv_lo.reshape(chips, rows_dev, 2, HD), kv_hi.reshape(chips, rows_dev, 2, HD)], axis=1
    ).reshape(tok_group, 2, HD)
    earlier_rows = min(MAXLEN, tok_group)
    earlier = from_behind(kv_rows[tok_group - earlier_rows :], "group", 1)
    all_rows = jnp.concatenate([earlier, kv_rows], axis=0)
    first_request = request_of[0]
    first_position = positions[0]
    earlier_req = jnp.where(
        jnp.arange(earlier_rows) >= earlier_rows - first_position, first_request, -1
    ).astype(jnp.int32)
    key_req = jnp.concatenate([earlier_req, request_of])[None, :]
    key_pos = jnp.concatenate([jnp.full((earlier_rows,), -1, jnp.int32), positions])[None, :]
    slots = fused_attention(
        queries.reshape(-1, heads * HD),
        all_rows[:, 0],
        all_rows[:, 1],
        out_w_t,
        half_req[:, None],
        half_pos[:, None],
        key_req,
        key_pos,
        1,
    )
    attn_sum = jnp.sum(slots.astype(jnp.float32), axis=0)
    mixed = residual + attn_sum
    partials = fused_mlp(rms_scale(mixed, mlp_gain), own_mlp, 2)
    layer_out = (mixed + jnp.sum(partials.astype(jnp.float32), axis=0)).astype(bf)
    pages = page_table.shape[1]
    changed = jnp.concatenate(
        [jnp.ones((1,), jnp.int32), (request_of[1:] != request_of[:-1]).astype(jnp.int32)]
    )
    opens = jnp.maximum(changed, (positions % PAGE == 0).astype(jnp.int32))
    logical = jnp.cumsum(opens) - 1
    chosen = jnp.sum(
        jnp.where(logical[:, None] == jnp.arange(pages)[None, :], page_table, 0), axis=1
    )
    target = chosen * PAGE + positions % PAGE
    own_slice = lax.dynamic_index_in_dim(kv_rows, lax.axis_index("core"), axis=1, keepdims=False)
    width = own_slice.shape[1]
    cache = jnp.zeros((pages * PAGE, width), jnp.bfloat16).at[target].set(own_slice)
    return (layer_out, cache.reshape(pages, PAGE, width))


def solution(mesh):
    groups, tensors = mesh.devices.shape
    split = Mesh(mesh.devices.reshape(groups, tensors // 2, 2), ("group", "chip", "core"))
    tensor = ("chip", "core")
    placed = (
        P(("group",) + tensor, None),
        P("group"),
        P("group"),
        P("group", None),
        P(),
        P(),
        P("group", tensor),
        P("group", tensor),
        P("group", tensor),
        P(tensor, "group"),
        P("group", tensor),
        P("group", tensor),
        P(tensor, "group"),
    )
    return jax.shard_map(
        body,
        mesh=split,
        in_specs=placed,
        out_specs=(P(("group",) + tensor, None), P("group", None, tensor)),
        check_vma=False,
    )
```

```python
import functools

import jax
import jax.numpy as jnp
from jax import lax
from jax.experimental import pallas as pl
from jax.experimental.pallas import tpu as pltpu
from jax.sharding import Mesh
from jax.sharding import PartitionSpec as P

QH = 16
KVH = 8
HD = 128
PAGE = 128
MAXLEN = 512


rope_base = 1000000.0
norm_eps = 1e-06


def swap_cores(value):
    return lax.ppermute(value, "core", [(0, 1), (1, 0)])


def from_behind(block, axis, distance):
    devices = range(lax.axis_size(axis))
    route = [(i - distance, i) for i in devices if i - distance in devices]
    return lax.ppermute(block, axis, route)


def exchange_kernel(count, spread, spreads, swaps, *refs):
    source = refs[0]
    weights = refs[1] if (spreads or swaps) else None
    outs = refs[1 + (spreads or swaps) :]
    slots = outs[0]
    moved = outs[1] if (spreads or swaps) else None
    send_sems, recv_sems, local_sem = outs[-3:]
    me = lax.axis_index("chip")
    group = lax.axis_index("group")
    core = lax.axis_index("core")
    groups = lax.axis_size("group")
    mesh_ids = pl.DeviceIdType.MESH
    barrier = pltpu.get_barrier_semaphore()
    for shift in range(1, count):
        peer = lax.rem(me + shift, count)
        pl.semaphore_signal(barrier, inc=1, device_id=(group, peer, core), device_id_type=mesh_ids)
    greeted = count - 1
    if swaps:
        pl.semaphore_signal(barrier, inc=1, device_id=(group, me, 1 - core), device_id_type=mesh_ids)
        greeted += 1
    if spreads:
        for shift in range(1, groups):
            peer = lax.rem(group + shift, groups)
            pl.semaphore_signal(barrier, inc=1, device_id=(peer, me, core), device_id_type=mesh_ids)
        greeted += groups - 1
    pl.semaphore_wait(barrier, greeted)
    local = pltpu.make_async_copy(source.at[me] if spread else source, slots.at[me], local_sem.at[0])
    local.start()
    locals_ = [local]
    copies = []
    if swaps:
        swap = pltpu.make_async_remote_copy(
            src_ref=weights,
            dst_ref=moved,
            send_sem=send_sems.at[0],
            recv_sem=recv_sems.at[0],
            device_id=(group, me, 1 - core),
            device_id_type=mesh_ids,
        )
        swap.start()
        copies.append(swap)
    if spreads:
        own_weights = pltpu.make_async_copy(weights, moved.at[group], local_sem.at[1])
        own_weights.start()
        locals_.append(own_weights)
        for shift in range(1, groups):
            peer = lax.rem(group + shift, groups)
            copy = pltpu.make_async_remote_copy(
                src_ref=weights,
                dst_ref=moved.at[group],
                send_sem=send_sems.at[count + shift],
                recv_sem=recv_sems.at[count + shift],
                device_id=(peer, me, core),
                device_id_type=mesh_ids,
            )
            copy.start()
            copies.append(copy)
    for shift in range(1, count):
        peer = lax.rem(me + shift, count)
        copy = pltpu.make_async_remote_copy(
            src_ref=source.at[peer] if spread else source,
            dst_ref=slots.at[me],
            send_sem=send_sems.at[shift],
            recv_sem=recv_sems.at[shift],
            device_id=(group, peer, core),
            device_id_type=mesh_ids,
        )
        copy.start()
        copies.append(copy)
    for shift in range(1, count):
        sender = lax.rem(me + count - shift, count)
        pltpu.make_async_remote_copy(
            src_ref=slots.at[sender],
            dst_ref=slots.at[sender],
            send_sem=send_sems.at[shift],
            recv_sem=recv_sems.at[shift],
            device_id=(group, sender, core),
            device_id_type=mesh_ids,
        ).wait_recv()
    if swaps:
        swap.wait_recv()
    if spreads:
        for shift in range(1, groups):
            sender = lax.rem(group + groups - shift, groups)
            pltpu.make_async_remote_copy(
                src_ref=moved.at[sender],
                dst_ref=moved.at[sender],
                send_sem=send_sems.at[count + shift],
                recv_sem=recv_sems.at[count + shift],
                device_id=(sender, me, core),
                device_id_type=mesh_ids,
            ).wait_recv()
    for copy in copies:
        copy.wait_send()
    for copy in locals_:
        copy.wait()


def exchange(block, spread, tag, weights=None, spreads=False):
    count = lax.axis_size("chip")
    groups = lax.axis_size("group")
    rows, cols = block.shape[-2:]
    moved = count * rows * cols * block.dtype.itemsize
    out_shape = [jax.ShapeDtypeStruct((count, rows, cols), block.dtype)]
    operands = [block]
    swaps = weights is not None and not spreads
    if weights is not None:
        copies = groups if spreads else 1
        out_shape.append(jax.ShapeDtypeStruct((copies,) * spreads + weights.shape, weights.dtype))
        operands.append(weights)
        moved += copies * weights.size * weights.dtype.itemsize
    outs = pl.pallas_call(
        functools.partial(exchange_kernel, count, spread, spreads, swaps),
        out_shape=tuple(out_shape),
        in_specs=[pl.BlockSpec(memory_space=pl.ANY)] * len(operands),
        out_specs=tuple(pl.BlockSpec(memory_space=pl.ANY) for _ in out_shape),
        scratch_shapes=[
            pltpu.SemaphoreType.DMA((count + groups,)),
            pltpu.SemaphoreType.DMA((count + groups,)),
            pltpu.SemaphoreType.DMA((2,)),
        ],
        compiler_params=pltpu.CompilerParams(collective_id=tag, has_side_effects=True),
        cost_estimate=pl.CostEstimate(flops=0, bytes_accessed=2 * moved, transcendentals=0),
    )(*operands)
    return outs


def gather_chip(block, tag):
    outs = exchange(block, False, tag)
    return outs[0].reshape(-1, block.shape[1])


def gather_swap(block, tag, weights):
    outs = exchange(block, False, tag, weights)
    return outs[0].reshape(-1, block.shape[1]), outs[1]


def scatter_chip(partial, tag):
    count = lax.axis_size("chip")
    outs = exchange(partial.reshape(count, -1, partial.shape[1]), True, tag)
    return jnp.sum(outs[0].astype(jnp.float32), axis=0)


def mlp_kernel(count, ff, own_block, weights, rs_out, own_w, other_w, slots, partials, ag_send, ag_recv, rs_send, rs_recv, swap_sems, local_sems):
    me = lax.axis_index("chip")
    group = lax.axis_index("group")
    core = lax.axis_index("core")
    mesh_ids = pl.DeviceIdType.MESH
    barrier = pltpu.get_barrier_semaphore()
    for shift in range(1, count):
        peer = lax.rem(me + shift, count)
        pl.semaphore_signal(barrier, inc=1, device_id=(group, peer, core), device_id_type=mesh_ids)
    pl.semaphore_signal(barrier, inc=1, device_id=(group, me, 1 - core), device_id_type=mesh_ids)
    pl.semaphore_wait(barrier, count)
    load_w = pltpu.make_async_copy(weights, own_w, local_sems.at[0])
    load_w.start()
    load_x = pltpu.make_async_copy(own_block, slots.at[me], local_sems.at[1])
    load_x.start()
    swap = pltpu.make_async_remote_copy(
        src_ref=weights,
        dst_ref=other_w,
        send_sem=swap_sems.at[0],
        recv_sem=swap_sems.at[1],
        device_id=(group, me, 1 - core),
        device_id_type=mesh_ids,
    )
    swap.start()
    sends = [swap]
    for shift in range(1, count):
        peer = lax.rem(me + shift, count)
        copy = pltpu.make_async_remote_copy(
            src_ref=own_block,
            dst_ref=slots.at[me],
            send_sem=ag_send.at[shift],
            recv_sem=ag_recv.at[shift],
            device_id=(group, peer, core),
            device_id_type=mesh_ids,
        )
        copy.start()
        sends.append(copy)
    load_w.wait()
    swap.wait_recv()
    load_x.wait()
    outs = []
    for shift in range(count):
        sender = lax.rem(me + count - shift, count)
        if shift > 0:
            pltpu.make_async_remote_copy(
                src_ref=slots.at[sender],
                dst_ref=slots.at[sender],
                send_sem=ag_send.at[shift],
                recv_sem=ag_recv.at[shift],
                device_id=(group, sender, core),
                device_id_type=mesh_ids,
            ).wait_recv()
        rows = slots[sender]
        total = None
        for table in (own_w, other_w):
            gate = jnp.dot(rows, table[:, pl.ds(0, ff)], preferred_element_type=jnp.float32)
            up = jnp.dot(rows, table[:, pl.ds(ff, ff)], preferred_element_type=jnp.float32)
            act = (gate / (1.0 + jnp.exp(-gate)) * up).astype(jnp.bfloat16)
            down = lax.dot_general(
                act, table[:, pl.ds(2 * ff, ff)], (((1,), (1,)), ((), ())),
                preferred_element_type=jnp.float32,
            )
            total = down if total is None else total + down
        partials[shift] = total.astype(jnp.bfloat16)
        if shift == 0:
            back = pltpu.make_async_copy(partials.at[0], rs_out.at[me], local_sems.at[2])
        else:
            back = pltpu.make_async_remote_copy(
                src_ref=partials.at[shift],
                dst_ref=rs_out.at[me],
                send_sem=rs_send.at[shift],
                recv_sem=rs_recv.at[shift],
                device_id=(group, sender, core),
                device_id_type=mesh_ids,
            )
        back.start()
        outs.append(back)
    for shift in range(1, count):
        owner = lax.rem(me + shift, count)
        pltpu.make_async_remote_copy(
            src_ref=partials.at[shift],
            dst_ref=rs_out.at[owner],
            send_sem=rs_send.at[shift],
            recv_sem=rs_recv.at[shift],
            device_id=(group, owner, core),
            device_id_type=mesh_ids,
        ).wait_recv()
    outs[0].wait()
    for copy in outs[1:]:
        copy.wait_send()
    for copy in sends:
        copy.wait_send()


def fused_mlp(block, weights, tag):
    count = lax.axis_size("chip")
    rows, cols = block.shape
    ff = weights.shape[1] // 3
    flops = 2 * count * rows * cols * ff * 6
    return pl.pallas_call(
        functools.partial(mlp_kernel, count, ff),
        out_shape=jax.ShapeDtypeStruct((count, rows, cols), block.dtype),
        in_specs=[pl.BlockSpec(memory_space=pl.ANY)] * 2,
        out_specs=pl.BlockSpec(memory_space=pl.ANY),
        scratch_shapes=[
            pltpu.VMEM(weights.shape, weights.dtype),
            pltpu.VMEM(weights.shape, weights.dtype),
            pltpu.VMEM((count, rows, cols), block.dtype),
            pltpu.VMEM((count, rows, cols), block.dtype),
            pltpu.SemaphoreType.DMA((count,)),
            pltpu.SemaphoreType.DMA((count,)),
            pltpu.SemaphoreType.DMA((count,)),
            pltpu.SemaphoreType.DMA((count,)),
            pltpu.SemaphoreType.DMA((2,)),
            pltpu.SemaphoreType.DMA((3,)),
        ],
        compiler_params=pltpu.CompilerParams(
            collective_id=tag, has_side_effects=True, vmem_limit_bytes=60 * 1024 * 1024
        ),
        cost_estimate=pl.CostEstimate(
            flops=flops, bytes_accessed=4 * count * rows * cols * 2, transcendentals=count * rows * ff * 2
        ),
    )(block, weights)


def attend_kernel(count, heads, queries, keys, values, out_w_t, query_req, query_pos, key_req, key_pos, rs_out, partials, rs_send, rs_recv, local_sem):
    me = lax.axis_index("chip")
    group = lax.axis_index("group")
    core = lax.axis_index("core")
    mesh_ids = pl.DeviceIdType.MESH
    rows = rs_out.shape[1]
    barrier = pltpu.get_barrier_semaphore()
    for shift in range(1, count):
        peer = lax.rem(me + shift, count)
        pl.semaphore_signal(barrier, inc=1, device_id=(group, peer, core), device_id_type=mesh_ids)
    pl.semaphore_wait(barrier, count - 1)
    key_block = keys[...]
    value_block = values[...]
    visible_req = key_req[...]
    visible_pos = key_pos[...]
    sends = []
    for step in range(count):
        shift = (step + 1) % count
        peer = lax.rem(me + shift, count)
        start = pl.multiple_of(peer * rows, 8)
        own_req = query_req[pl.ds(start, rows), :]
        own_pos = query_pos[pl.ds(start, rows), :]
        visible = (own_req == visible_req) & (visible_pos <= own_pos)
        mixed = []
        for head in range(heads):
            q = queries[pl.ds(start, rows), pl.ds(head * HD, HD)]
            scores = lax.dot_general(
                q, key_block, (((1,), (1,)), ((), ())), preferred_element_type=jnp.float32
            ) * HD ** (-0.5)
            scores = jnp.where(visible, scores, -1e30)
            peak = jnp.max(scores, axis=1, keepdims=True)
            probs = jnp.where(visible, jnp.exp(scores - peak), 0.0)
            total = jnp.sum(probs, axis=1, keepdims=True)
            head_out = jnp.dot(probs.astype(jnp.bfloat16), value_block, preferred_element_type=jnp.float32)
            mixed.append((head_out / total).astype(jnp.bfloat16))
        attended = jnp.concatenate(mixed, axis=1)
        partial = lax.dot_general(
            attended, out_w_t[...], (((1,), (1,)), ((), ())), preferred_element_type=jnp.float32
        )
        partials[shift] = partial.astype(jnp.bfloat16)
        if shift == 0:
            back = pltpu.make_async_copy(partials.at[0], rs_out.at[me], local_sem)
        else:
            back = pltpu.make_async_remote_copy(
                src_ref=partials.at[shift],
                dst_ref=rs_out.at[me],
                send_sem=rs_send.at[shift],
                recv_sem=rs_recv.at[shift],
                device_id=(group, peer, core),
                device_id_type=mesh_ids,
            )
        back.start()
        sends.append((shift, back))
    for shift in range(1, count):
        source = lax.rem(me + count - shift, count)
        pltpu.make_async_remote_copy(
            src_ref=partials.at[shift],
            dst_ref=rs_out.at[source],
            send_sem=rs_send.at[shift],
            recv_sem=rs_recv.at[shift],
            device_id=(group, source, core),
            device_id_type=mesh_ids,
        ).wait_recv()
    for shift, copy in sends:
        if shift == 0:
            copy.wait()
        else:
            copy.wait_send()


def fused_attention(queries, keys, values, out_w_t, query_req, query_pos, key_req, key_pos, tag):
    count = lax.axis_size("chip")
    rows = queries.shape[0] // count
    cols = out_w_t.shape[0]
    heads = queries.shape[1] // HD
    vmem = pl.BlockSpec(memory_space=pltpu.VMEM)
    flops = 2 * queries.shape[0] * keys.shape[0] * HD * 2 * heads + 2 * queries.shape[0] * queries.shape[1] * cols
    return pl.pallas_call(
        functools.partial(attend_kernel, count, heads),
        out_shape=jax.ShapeDtypeStruct((count, rows, cols), jnp.bfloat16),
        in_specs=[vmem] * 8,
        out_specs=pl.BlockSpec(memory_space=pl.ANY),
        scratch_shapes=[
            pltpu.VMEM((count, rows, cols), jnp.bfloat16),
            pltpu.SemaphoreType.DMA((count,)),
            pltpu.SemaphoreType.DMA((count,)),
            pltpu.SemaphoreType.DMA(()),
        ],
        compiler_params=pltpu.CompilerParams(
            collective_id=tag, has_side_effects=True, vmem_limit_bytes=48 * 1024 * 1024
        ),
        cost_estimate=pl.CostEstimate(
            flops=0, bytes_accessed=2 * count * rows * cols * 2, transcendentals=0
        ),
    )(queries, keys, values, out_w_t, query_req, query_pos, key_req, key_pos)


def gather_group(block):
    count = lax.axis_size("group")
    pieces = [block]
    for shift in range(1, count):
        route = [(source, (source + shift) % count) for source in range(count)]
        pieces.append(lax.ppermute(block, "group", route))
    stacked = jnp.stack(pieces)
    order = (lax.axis_index("group") - jnp.arange(count)) % count
    return jnp.take(stacked, order, axis=0).reshape(count * block.shape[0], block.shape[1])


def rms_scale(values, gain):
    square = jnp.mean(values * values, axis=-1, keepdims=True)
    return (values * lax.rsqrt(square + norm_eps) * gain).astype(jnp.bfloat16)


def rotate(values, places):
    half_dim = values.shape[-1] // 2
    frequency = rope_base ** (-(jnp.arange(half_dim, dtype=jnp.float32) * 2.0 / values.shape[-1]))
    angle = places.astype(jnp.float32)[:, None] * frequency[None, :]
    cosine = jnp.cos(angle)[:, None, :]
    sine = jnp.sin(angle)[:, None, :]
    widened = values.astype(jnp.float32)
    first = widened[..., :half_dim]
    second = widened[..., half_dim:]
    return jnp.concatenate(
        [first * cosine - second * sine, second * cosine + first * sine], axis=-1
    ).astype(jnp.bfloat16)


def by_core(own_part, other_part):
    first = lax.axis_index("core") == 0
    return jnp.where(first, own_part, other_part), jnp.where(first, other_part, own_part)


def dot(acts, weight):
    return jnp.dot(acts, weight, preferred_element_type=jnp.float32)


def dot_t(acts, weight_t):
    return lax.dot_general(
        acts, weight_t, (((1,), (1,)), ((), ())), preferred_element_type=jnp.float32
    )


def core_rows(values, chips, rows_dev):
    blocks = values.reshape(chips, 2, rows_dev, *values.shape[1:])
    own = lax.dynamic_index_in_dim(blocks, lax.axis_index("core"), axis=1, keepdims=False)
    return own.reshape(chips * rows_dev, *values.shape[1:])


def body(
    hidden,
    request_of,
    positions,
    page_table,
    attn_gain,
    mlp_gain,
    wq,
    wk,
    wv,
    wo,
    w_gate,
    w_up,
    w_down,
):
    chips = lax.axis_size("chip")
    rows_dev = hidden.shape[0]
    tok_group = request_of.shape[0]
    bf = jnp.bfloat16
    residual = hidden.astype(jnp.float32)
    q_cols = wq.shape[1]
    kv_half = wk.shape[1]
    own_attn = jnp.concatenate([wq.astype(bf), wk.astype(bf), wv.astype(bf), wo.astype(bf).T], axis=1)
    own_attn = lax.all_gather(own_attn, "group", axis=0, tiled=True)
    normed = gather_chip(rms_scale(residual, attn_gain), 0)
    normed, own_attn = lax.optimization_barrier((normed, own_attn))
    other_attn = swap_cores(own_attn)
    query_w = jnp.concatenate([own_attn[:, :q_cols], other_attn[:, :q_cols]], axis=1)
    out_w_t = jnp.concatenate(
        [own_attn[:, q_cols + 2 * kv_half :], other_attn[:, q_cols + 2 * kv_half :]], axis=1
    )
    key_lo, key_hi = by_core(own_attn[:, q_cols : q_cols + kv_half], other_attn[:, q_cols : q_cols + kv_half])
    value_lo, value_hi = by_core(
        own_attn[:, q_cols + kv_half : q_cols + 2 * kv_half],
        other_attn[:, q_cols + kv_half : q_cols + 2 * kv_half],
    )
    key_w = jnp.concatenate([key_lo, key_hi], axis=1)
    value_w = jnp.concatenate([value_lo, value_hi], axis=1)
    ff_cols = w_gate.shape[1]
    own_mlp = jnp.concatenate([w_gate.astype(bf), w_up.astype(bf), w_down.astype(bf).T], axis=1)
    own_mlp = lax.all_gather(own_mlp, "group", axis=0, tiled=True)
    half_pos = core_rows(positions, chips, rows_dev)
    half_req = core_rows(request_of, chips, rows_dev)
    heads = 2 * q_cols // HD
    queries = rotate(dot(normed, query_w).astype(bf).reshape(-1, heads, HD), half_pos)
    keys_half = rotate(dot(normed, key_w).astype(bf).reshape(-1, 1, HD), half_pos)
    values_half = dot(normed, value_w).astype(bf).reshape(-1, 1, HD)
    kv_own = jnp.stack([keys_half[:, 0], values_half[:, 0]], axis=1)
    kv_other = swap_cores(kv_own)
    kv_lo, kv_hi = by_core(kv_own, kv_other)
    kv_rows = jnp.stack(
        [kv_lo.reshape(chips, rows_dev, 2, HD), kv_hi.reshape(chips, rows_dev, 2, HD)], axis=1
    ).reshape(tok_group, 2, HD)
    earlier_rows = min(MAXLEN, tok_group)
    earlier = from_behind(kv_rows[tok_group - earlier_rows :], "group", 1)
    all_rows = jnp.concatenate([earlier, kv_rows], axis=0)
    first_request = request_of[0]
    first_position = positions[0]
    earlier_req = jnp.where(
        jnp.arange(earlier_rows) >= earlier_rows - first_position, first_request, -1
    ).astype(jnp.int32)
    key_req = jnp.concatenate([earlier_req, request_of])[None, :]
    key_pos = jnp.concatenate([jnp.full((earlier_rows,), -1, jnp.int32), positions])[None, :]
    slots = fused_attention(
        queries.reshape(-1, heads * HD),
        all_rows[:, 0],
        all_rows[:, 1],
        out_w_t,
        half_req[:, None],
        half_pos[:, None],
        key_req,
        key_pos,
        1,
    )
    attn_sum = jnp.sum(slots.astype(jnp.float32), axis=0)
    mixed = residual + attn_sum
    partials = fused_mlp(rms_scale(mixed, mlp_gain), own_mlp, 2)
    layer_out = (mixed + jnp.sum(partials.astype(jnp.float32), axis=0)).astype(bf)
    pages = page_table.shape[1]
    changed = jnp.concatenate(
        [jnp.ones((1,), jnp.int32), (request_of[1:] != request_of[:-1]).astype(jnp.int32)]
    )
    opens = jnp.maximum(changed, (positions % PAGE == 0).astype(jnp.int32))
    logical = jnp.cumsum(opens) - 1
    chosen = jnp.sum(
        jnp.where(logical[:, None] == jnp.arange(pages)[None, :], page_table, 0), axis=1
    )
    target = chosen * PAGE + positions % PAGE
    own_slice = lax.dynamic_index_in_dim(kv_rows, lax.axis_index("core"), axis=1, keepdims=False)
    width = own_slice.shape[1]
    cache = jnp.zeros((pages * PAGE, width), jnp.bfloat16).at[target].set(own_slice)
    return (layer_out, cache.reshape(pages, PAGE, width))


def solution(mesh):
    groups, tensors = mesh.devices.shape
    split = Mesh(mesh.devices.reshape(groups, tensors // 2, 2), ("group", "chip", "core"))
    tensor = ("chip", "core")
    placed = (
        P(("group",) + tensor, None),
        P("group"),
        P("group"),
        P("group", None),
        P(),
        P(),
        P("group", tensor),
        P("group", tensor),
        P("group", tensor),
        P(tensor, "group"),
        P("group", tensor),
        P("group", tensor),
        P(tensor, "group"),
    )
    return jax.shard_map(
        body,
        mesh=split,
        in_specs=placed,
        out_specs=(P(("group",) + tensor, None), P("group", None, tensor)),
        check_vma=False,
    )
```

```python
import functools

import jax
import jax.numpy as jnp
from jax import lax
from jax.experimental import pallas as pl
from jax.experimental.pallas import tpu as pltpu
from jax.sharding import Mesh
from jax.sharding import PartitionSpec as P

QH = 16
KVH = 8
HD = 128
PAGE = 128
MAXLEN = 512


rope_base = 1000000.0
norm_eps = 1e-06


def swap_cores(value):
    return lax.ppermute(value, "core", [(0, 1), (1, 0)])


def from_behind(block, axis, distance):
    devices = range(lax.axis_size(axis))
    route = [(i - distance, i) for i in devices if i - distance in devices]
    return lax.ppermute(block, axis, route)


def exchange_kernel(count, spread, spreads, swaps, *refs):
    source = refs[0]
    weights = refs[1] if (spreads or swaps) else None
    outs = refs[1 + (spreads or swaps) :]
    slots = outs[0]
    moved = outs[1] if (spreads or swaps) else None
    send_sems, recv_sems, local_sem = outs[-3:]
    me = lax.axis_index("chip")
    group = lax.axis_index("group")
    core = lax.axis_index("core")
    groups = lax.axis_size("group")
    mesh_ids = pl.DeviceIdType.MESH
    barrier = pltpu.get_barrier_semaphore()
    for shift in range(1, count):
        peer = lax.rem(me + shift, count)
        pl.semaphore_signal(barrier, inc=1, device_id=(group, peer, core), device_id_type=mesh_ids)
    greeted = count - 1
    if swaps:
        pl.semaphore_signal(barrier, inc=1, device_id=(group, me, 1 - core), device_id_type=mesh_ids)
        greeted += 1
    if spreads:
        for shift in range(1, groups):
            peer = lax.rem(group + shift, groups)
            pl.semaphore_signal(barrier, inc=1, device_id=(peer, me, core), device_id_type=mesh_ids)
        greeted += groups - 1
    pl.semaphore_wait(barrier, greeted)
    local = pltpu.make_async_copy(source.at[me] if spread else source, slots.at[me], local_sem.at[0])
    local.start()
    locals_ = [local]
    copies = []
    if swaps:
        swap = pltpu.make_async_remote_copy(
            src_ref=weights,
            dst_ref=moved,
            send_sem=send_sems.at[0],
            recv_sem=recv_sems.at[0],
            device_id=(group, me, 1 - core),
            device_id_type=mesh_ids,
        )
        swap.start()
        copies.append(swap)
    if spreads:
        own_weights = pltpu.make_async_copy(weights, moved.at[group], local_sem.at[1])
        own_weights.start()
        locals_.append(own_weights)
        for shift in range(1, groups):
            peer = lax.rem(group + shift, groups)
            copy = pltpu.make_async_remote_copy(
                src_ref=weights,
                dst_ref=moved.at[group],
                send_sem=send_sems.at[count + shift],
                recv_sem=recv_sems.at[count + shift],
                device_id=(peer, me, core),
                device_id_type=mesh_ids,
            )
            copy.start()
            copies.append(copy)
    for shift in range(1, count):
        peer = lax.rem(me + shift, count)
        copy = pltpu.make_async_remote_copy(
            src_ref=source.at[peer] if spread else source,
            dst_ref=slots.at[me],
            send_sem=send_sems.at[shift],
            recv_sem=recv_sems.at[shift],
            device_id=(group, peer, core),
            device_id_type=mesh_ids,
        )
        copy.start()
        copies.append(copy)
    for shift in range(1, count):
        sender = lax.rem(me + count - shift, count)
        pltpu.make_async_remote_copy(
            src_ref=slots.at[sender],
            dst_ref=slots.at[sender],
            send_sem=send_sems.at[shift],
            recv_sem=recv_sems.at[shift],
            device_id=(group, sender, core),
            device_id_type=mesh_ids,
        ).wait_recv()
    if swaps:
        swap.wait_recv()
    if spreads:
        for shift in range(1, groups):
            sender = lax.rem(group + groups - shift, groups)
            pltpu.make_async_remote_copy(
                src_ref=moved.at[sender],
                dst_ref=moved.at[sender],
                send_sem=send_sems.at[count + shift],
                recv_sem=recv_sems.at[count + shift],
                device_id=(sender, me, core),
                device_id_type=mesh_ids,
            ).wait_recv()
    for copy in copies:
        copy.wait_send()
    for copy in locals_:
        copy.wait()


def exchange(block, spread, tag, weights=None, spreads=False):
    count = lax.axis_size("chip")
    groups = lax.axis_size("group")
    rows, cols = block.shape[-2:]
    moved = count * rows * cols * block.dtype.itemsize
    out_shape = [jax.ShapeDtypeStruct((count, rows, cols), block.dtype)]
    operands = [block]
    swaps = weights is not None and not spreads
    if weights is not None:
        copies = groups if spreads else 1
        out_shape.append(jax.ShapeDtypeStruct((copies,) * spreads + weights.shape, weights.dtype))
        operands.append(weights)
        moved += copies * weights.size * weights.dtype.itemsize
    outs = pl.pallas_call(
        functools.partial(exchange_kernel, count, spread, spreads, swaps),
        out_shape=tuple(out_shape),
        in_specs=[pl.BlockSpec(memory_space=pl.ANY)] * len(operands),
        out_specs=tuple(pl.BlockSpec(memory_space=pl.ANY) for _ in out_shape),
        scratch_shapes=[
            pltpu.SemaphoreType.DMA((count + groups,)),
            pltpu.SemaphoreType.DMA((count + groups,)),
            pltpu.SemaphoreType.DMA((2,)),
        ],
        compiler_params=pltpu.CompilerParams(collective_id=tag, has_side_effects=True),
        cost_estimate=pl.CostEstimate(flops=0, bytes_accessed=2 * moved, transcendentals=0),
    )(*operands)
    return outs


def gather_chip(block, tag):
    outs = exchange(block, False, tag)
    return outs[0].reshape(-1, block.shape[1])


def gather_swap(block, tag, weights):
    outs = exchange(block, False, tag, weights)
    return outs[0].reshape(-1, block.shape[1]), outs[1]


def scatter_chip(partial, tag, weights=None):
    count = lax.axis_size("chip")
    outs = exchange(partial.reshape(count, -1, partial.shape[1]), True, tag, weights)
    summed = jnp.sum(outs[0].astype(jnp.float32), axis=0)
    if weights is None:
        return summed
    return summed, outs[1]


def mlp_kernel(count, ff, own_block, weights, other_weights, rs_out, own_w, other_w, slots, partials, ag_send, ag_recv, rs_send, rs_recv, swap_sems, local_sems):
    me = lax.axis_index("chip")
    group = lax.axis_index("group")
    core = lax.axis_index("core")
    mesh_ids = pl.DeviceIdType.MESH
    barrier = pltpu.get_barrier_semaphore()
    for shift in range(1, count):
        peer = lax.rem(me + shift, count)
        pl.semaphore_signal(barrier, inc=1, device_id=(group, peer, core), device_id_type=mesh_ids)
    pl.semaphore_wait(barrier, count - 1)
    load_w = pltpu.make_async_copy(weights, own_w, local_sems.at[0])
    load_w.start()
    load_x = pltpu.make_async_copy(own_block, slots.at[me], local_sems.at[1])
    load_x.start()
    load_other = pltpu.make_async_copy(other_weights, other_w, swap_sems.at[0])
    load_other.start()
    sends = []
    for shift in range(1, count):
        peer = lax.rem(me + shift, count)
        copy = pltpu.make_async_remote_copy(
            src_ref=own_block,
            dst_ref=slots.at[me],
            send_sem=ag_send.at[shift],
            recv_sem=ag_recv.at[shift],
            device_id=(group, peer, core),
            device_id_type=mesh_ids,
        )
        copy.start()
        sends.append(copy)
    load_w.wait()
    load_other.wait()
    load_x.wait()
    outs = []
    for shift in range(count):
        sender = lax.rem(me + count - shift, count)
        if shift > 0:
            pltpu.make_async_remote_copy(
                src_ref=slots.at[sender],
                dst_ref=slots.at[sender],
                send_sem=ag_send.at[shift],
                recv_sem=ag_recv.at[shift],
                device_id=(group, sender, core),
                device_id_type=mesh_ids,
            ).wait_recv()
        rows = slots[sender]
        total = None
        for table in (own_w, other_w):
            gate = jnp.dot(rows, table[:, pl.ds(0, ff)], preferred_element_type=jnp.float32)
            up = jnp.dot(rows, table[:, pl.ds(ff, ff)], preferred_element_type=jnp.float32)
            act = (gate / (1.0 + jnp.exp(-gate)) * up).astype(jnp.bfloat16)
            down = lax.dot_general(
                act, table[:, pl.ds(2 * ff, ff)], (((1,), (1,)), ((), ())),
                preferred_element_type=jnp.float32,
            )
            total = down if total is None else total + down
        partials[shift] = total.astype(jnp.bfloat16)
        if shift == 0:
            back = pltpu.make_async_copy(partials.at[0], rs_out.at[me], local_sems.at[2])
        else:
            back = pltpu.make_async_remote_copy(
                src_ref=partials.at[shift],
                dst_ref=rs_out.at[me],
                send_sem=rs_send.at[shift],
                recv_sem=rs_recv.at[shift],
                device_id=(group, sender, core),
                device_id_type=mesh_ids,
            )
        back.start()
        outs.append(back)
    for shift in range(1, count):
        owner = lax.rem(me + shift, count)
        pltpu.make_async_remote_copy(
            src_ref=partials.at[shift],
            dst_ref=rs_out.at[owner],
            send_sem=rs_send.at[shift],
            recv_sem=rs_recv.at[shift],
            device_id=(group, owner, core),
            device_id_type=mesh_ids,
        ).wait_recv()
    outs[0].wait()
    for copy in outs[1:]:
        copy.wait_send()
    for copy in sends:
        copy.wait_send()


def fused_mlp(block, weights, other_weights, tag):
    count = lax.axis_size("chip")
    rows, cols = block.shape
    ff = weights.shape[1] // 3
    flops = 2 * count * rows * cols * ff * 6
    return pl.pallas_call(
        functools.partial(mlp_kernel, count, ff),
        out_shape=jax.ShapeDtypeStruct((count, rows, cols), block.dtype),
        in_specs=[pl.BlockSpec(memory_space=pl.ANY)] * 3,
        out_specs=pl.BlockSpec(memory_space=pl.ANY),
        scratch_shapes=[
            pltpu.VMEM(weights.shape, weights.dtype),
            pltpu.VMEM(weights.shape, weights.dtype),
            pltpu.VMEM((count, rows, cols), block.dtype),
            pltpu.VMEM((count, rows, cols), block.dtype),
            pltpu.SemaphoreType.DMA((count,)),
            pltpu.SemaphoreType.DMA((count,)),
            pltpu.SemaphoreType.DMA((count,)),
            pltpu.SemaphoreType.DMA((count,)),
            pltpu.SemaphoreType.DMA((2,)),
            pltpu.SemaphoreType.DMA((3,)),
        ],
        compiler_params=pltpu.CompilerParams(
            collective_id=tag, has_side_effects=True, vmem_limit_bytes=60 * 1024 * 1024
        ),
        cost_estimate=pl.CostEstimate(
            flops=flops, bytes_accessed=4 * count * rows * cols * 2, transcendentals=count * rows * ff * 2
        ),
    )(block, weights, other_weights)


def gather_group(block):
    count = lax.axis_size("group")
    pieces = [block]
    for shift in range(1, count):
        route = [(source, (source + shift) % count) for source in range(count)]
        pieces.append(lax.ppermute(block, "group", route))
    stacked = jnp.stack(pieces)
    order = (lax.axis_index("group") - jnp.arange(count)) % count
    return jnp.take(stacked, order, axis=0).reshape(count * block.shape[0], block.shape[1])


def rms_scale(values, gain):
    square = jnp.mean(values * values, axis=-1, keepdims=True)
    return (values * lax.rsqrt(square + norm_eps) * gain).astype(jnp.bfloat16)


def rotate(values, places):
    half_dim = values.shape[-1] // 2
    frequency = rope_base ** (-(jnp.arange(half_dim, dtype=jnp.float32) * 2.0 / values.shape[-1]))
    angle = places.astype(jnp.float32)[:, None] * frequency[None, :]
    cosine = jnp.cos(angle)[:, None, :]
    sine = jnp.sin(angle)[:, None, :]
    widened = values.astype(jnp.float32)
    first = widened[..., :half_dim]
    second = widened[..., half_dim:]
    return jnp.concatenate(
        [first * cosine - second * sine, second * cosine + first * sine], axis=-1
    ).astype(jnp.bfloat16)


def by_core(own_part, other_part):
    first = lax.axis_index("core") == 0
    return jnp.where(first, own_part, other_part), jnp.where(first, other_part, own_part)


def dot(acts, weight):
    return jnp.dot(acts, weight, preferred_element_type=jnp.float32)


def dot_t(acts, weight_t):
    return lax.dot_general(
        acts, weight_t, (((1,), (1,)), ((), ())), preferred_element_type=jnp.float32
    )


def core_rows(values, chips, rows_dev):
    blocks = values.reshape(chips, 2, rows_dev, *values.shape[1:])
    own = lax.dynamic_index_in_dim(blocks, lax.axis_index("core"), axis=1, keepdims=False)
    return own.reshape(chips * rows_dev, *values.shape[1:])


def body(
    hidden,
    request_of,
    positions,
    page_table,
    attn_gain,
    mlp_gain,
    wq,
    wk,
    wv,
    wo,
    w_gate,
    w_up,
    w_down,
):
    chips = lax.axis_size("chip")
    rows_dev = hidden.shape[0]
    tok_group = request_of.shape[0]
    bf = jnp.bfloat16
    residual = hidden.astype(jnp.float32)
    q_cols = wq.shape[1]
    kv_half = wk.shape[1]
    own_attn = jnp.concatenate([wq.astype(bf), wk.astype(bf), wv.astype(bf), wo.astype(bf).T], axis=1)
    own_attn = lax.all_gather(own_attn, "group", axis=0, tiled=True)
    normed = gather_chip(rms_scale(residual, attn_gain), 0)
    other_attn = swap_cores(own_attn)
    query_w = jnp.concatenate([own_attn[:, :q_cols], other_attn[:, :q_cols]], axis=1)
    out_w_t = jnp.concatenate(
        [own_attn[:, q_cols + 2 * kv_half :], other_attn[:, q_cols + 2 * kv_half :]], axis=1
    )
    key_lo, key_hi = by_core(own_attn[:, q_cols : q_cols + kv_half], other_attn[:, q_cols : q_cols + kv_half])
    value_lo, value_hi = by_core(
        own_attn[:, q_cols + kv_half : q_cols + 2 * kv_half],
        other_attn[:, q_cols + kv_half : q_cols + 2 * kv_half],
    )
    key_w = jnp.concatenate([key_lo, key_hi], axis=1)
    value_w = jnp.concatenate([value_lo, value_hi], axis=1)
    ff_cols = w_gate.shape[1]
    own_mlp = jnp.concatenate([w_gate.astype(bf), w_up.astype(bf), w_down.astype(bf).T], axis=1)
    own_mlp = lax.all_gather(own_mlp, "group", axis=0, tiled=True)
    half_pos = core_rows(positions, chips, rows_dev)
    half_req = core_rows(request_of, chips, rows_dev)
    heads = 2 * q_cols // HD
    queries = rotate(dot(normed, query_w).astype(bf).reshape(-1, heads, HD), half_pos)
    keys_half = rotate(dot(normed, key_w).astype(bf).reshape(-1, 1, HD), half_pos)
    values_half = dot(normed, value_w).astype(bf).reshape(-1, 1, HD)
    kv_own = jnp.stack([keys_half[:, 0], values_half[:, 0]], axis=1)
    kv_other = swap_cores(kv_own)
    kv_lo, kv_hi = by_core(kv_own, kv_other)
    kv_rows = jnp.stack(
        [kv_lo.reshape(chips, rows_dev, 2, HD), kv_hi.reshape(chips, rows_dev, 2, HD)], axis=1
    ).reshape(tok_group, 2, HD)
    earlier_rows = min(MAXLEN, tok_group)
    earlier = from_behind(kv_rows[tok_group - earlier_rows :], "group", 1)
    all_rows = jnp.concatenate([earlier, kv_rows], axis=0)
    all_keys = all_rows[:, 0]
    all_values = all_rows[:, 1]
    first_request = request_of[0]
    first_position = positions[0]
    same_local = (half_req[:, None] == request_of[None, :]) & (
        positions[None, :] <= half_pos[:, None]
    )
    same_earlier = (half_req[:, None] == first_request) & (
        jnp.arange(earlier_rows)[None, :] >= earlier_rows - first_position
    )
    visible = jnp.concatenate([same_earlier, same_local], axis=1)
    scores = jnp.einsum(
        "qhd,kd->hqk", queries, all_keys, preferred_element_type=jnp.float32
    ) * HD ** (-0.5)
    scores = jnp.where(visible[None], scores, -1e30)
    row_peak = jnp.max(scores, axis=-1, keepdims=True)
    probs = jnp.where(visible[None], jnp.exp(scores - row_peak), 0.0)
    total = jnp.sum(probs, axis=-1, keepdims=True)
    mixed_heads = jnp.einsum(
        "hqk,kd->qhd", probs.astype(bf), all_values, preferred_element_type=jnp.float32
    ) / jnp.transpose(total, (1, 0, 2))
    attended = mixed_heads.astype(bf).reshape(-1, heads * HD)
    attn_part = dot_t(attended, out_w_t)
    attn_sum, other_mlp = scatter_chip(attn_part.astype(bf), 1, own_mlp)
    mixed = residual + attn_sum
    partials = fused_mlp(rms_scale(mixed, mlp_gain), own_mlp, other_mlp, 2)
    layer_out = (mixed + jnp.sum(partials.astype(jnp.float32), axis=0)).astype(bf)
    pages = page_table.shape[1]
    changed = jnp.concatenate(
        [jnp.ones((1,), jnp.int32), (request_of[1:] != request_of[:-1]).astype(jnp.int32)]
    )
    opens = jnp.maximum(changed, (positions % PAGE == 0).astype(jnp.int32))
    logical = jnp.cumsum(opens) - 1
    chosen = jnp.sum(
        jnp.where(logical[:, None] == jnp.arange(pages)[None, :], page_table, 0), axis=1
    )
    target = chosen * PAGE + positions % PAGE
    own_slice = lax.dynamic_index_in_dim(kv_rows, lax.axis_index("core"), axis=1, keepdims=False)
    width = own_slice.shape[1]
    cache = jnp.zeros((pages * PAGE, width), jnp.bfloat16).at[target].set(own_slice)
    return (layer_out, cache.reshape(pages, PAGE, width))


def solution(mesh):
    groups, tensors = mesh.devices.shape
    split = Mesh(mesh.devices.reshape(groups, tensors // 2, 2), ("group", "chip", "core"))
    tensor = ("chip", "core")
    placed = (
        P(("group",) + tensor, None),
        P("group"),
        P("group"),
        P("group", None),
        P(),
        P(),
        P("group", tensor),
        P("group", tensor),
        P("group", tensor),
        P(tensor, "group"),
        P("group", tensor),
        P("group", tensor),
        P(tensor, "group"),
    )
    return jax.shard_map(
        body,
        mesh=split,
        in_specs=placed,
        out_specs=(P(("group",) + tensor, None), P("group", None, tensor)),
        check_vma=False,
    )
```

```python
import functools

import jax
import jax.numpy as jnp
from jax import lax
from jax.experimental import pallas as pl
from jax.experimental.pallas import tpu as pltpu
from jax.sharding import Mesh
from jax.sharding import PartitionSpec as P

QH = 16
KVH = 8
HD = 128
PAGE = 128
MAXLEN = 512


rope_base = 1000000.0
norm_eps = 1e-06


def swap_cores(value):
    return lax.ppermute(value, "core", [(0, 1), (1, 0)])


def from_behind(block, axis, distance):
    devices = range(lax.axis_size(axis))
    route = [(i - distance, i) for i in devices if i - distance in devices]
    return lax.ppermute(block, axis, route)


def exchange_kernel(count, spread, spreads, swaps, *refs):
    source = refs[0]
    weights = refs[1] if (spreads or swaps) else None
    outs = refs[1 + (spreads or swaps) :]
    slots = outs[0]
    moved = outs[1] if (spreads or swaps) else None
    send_sems, recv_sems, local_sem = outs[-3:]
    me = lax.axis_index("chip")
    group = lax.axis_index("group")
    core = lax.axis_index("core")
    groups = lax.axis_size("group")
    mesh_ids = pl.DeviceIdType.MESH
    barrier = pltpu.get_barrier_semaphore()
    for shift in range(1, count):
        peer = lax.rem(me + shift, count)
        pl.semaphore_signal(barrier, inc=1, device_id=(group, peer, core), device_id_type=mesh_ids)
    greeted = count - 1
    if swaps:
        pl.semaphore_signal(barrier, inc=1, device_id=(group, me, 1 - core), device_id_type=mesh_ids)
        greeted += 1
    if spreads:
        for shift in range(1, groups):
            peer = lax.rem(group + shift, groups)
            pl.semaphore_signal(barrier, inc=1, device_id=(peer, me, core), device_id_type=mesh_ids)
        greeted += groups - 1
    pl.semaphore_wait(barrier, greeted)
    local = pltpu.make_async_copy(source.at[me] if spread else source, slots.at[me], local_sem.at[0])
    local.start()
    locals_ = [local]
    copies = []
    if swaps:
        swap = pltpu.make_async_remote_copy(
            src_ref=weights,
            dst_ref=moved,
            send_sem=send_sems.at[0],
            recv_sem=recv_sems.at[0],
            device_id=(group, me, 1 - core),
            device_id_type=mesh_ids,
        )
        swap.start()
        copies.append(swap)
    if spreads:
        own_weights = pltpu.make_async_copy(weights, moved.at[group], local_sem.at[1])
        own_weights.start()
        locals_.append(own_weights)
        for shift in range(1, groups):
            peer = lax.rem(group + shift, groups)
            copy = pltpu.make_async_remote_copy(
                src_ref=weights,
                dst_ref=moved.at[group],
                send_sem=send_sems.at[count + shift],
                recv_sem=recv_sems.at[count + shift],
                device_id=(peer, me, core),
                device_id_type=mesh_ids,
            )
            copy.start()
            copies.append(copy)
    for shift in range(1, count):
        peer = lax.rem(me + shift, count)
        copy = pltpu.make_async_remote_copy(
            src_ref=source.at[peer] if spread else source,
            dst_ref=slots.at[me],
            send_sem=send_sems.at[shift],
            recv_sem=recv_sems.at[shift],
            device_id=(group, peer, core),
            device_id_type=mesh_ids,
        )
        copy.start()
        copies.append(copy)
    for shift in range(1, count):
        sender = lax.rem(me + count - shift, count)
        pltpu.make_async_remote_copy(
            src_ref=slots.at[sender],
            dst_ref=slots.at[sender],
            send_sem=send_sems.at[shift],
            recv_sem=recv_sems.at[shift],
            device_id=(group, sender, core),
            device_id_type=mesh_ids,
        ).wait_recv()
    if swaps:
        swap.wait_recv()
    if spreads:
        for shift in range(1, groups):
            sender = lax.rem(group + groups - shift, groups)
            pltpu.make_async_remote_copy(
                src_ref=moved.at[sender],
                dst_ref=moved.at[sender],
                send_sem=send_sems.at[count + shift],
                recv_sem=recv_sems.at[count + shift],
                device_id=(sender, me, core),
                device_id_type=mesh_ids,
            ).wait_recv()
    for copy in copies:
        copy.wait_send()
    for copy in locals_:
        copy.wait()


def exchange(block, spread, tag, weights=None, spreads=False):
    count = lax.axis_size("chip")
    groups = lax.axis_size("group")
    rows, cols = block.shape[-2:]
    moved = count * rows * cols * block.dtype.itemsize
    out_shape = [jax.ShapeDtypeStruct((count, rows, cols), block.dtype)]
    operands = [block]
    swaps = weights is not None and not spreads
    if weights is not None:
        copies = groups if spreads else 1
        out_shape.append(jax.ShapeDtypeStruct((copies,) * spreads + weights.shape, weights.dtype))
        operands.append(weights)
        moved += copies * weights.size * weights.dtype.itemsize
    outs = pl.pallas_call(
        functools.partial(exchange_kernel, count, spread, spreads, swaps),
        out_shape=tuple(out_shape),
        in_specs=[pl.BlockSpec(memory_space=pl.ANY)] * len(operands),
        out_specs=tuple(pl.BlockSpec(memory_space=pl.ANY) for _ in out_shape),
        scratch_shapes=[
            pltpu.SemaphoreType.DMA((count + groups,)),
            pltpu.SemaphoreType.DMA((count + groups,)),
            pltpu.SemaphoreType.DMA((2,)),
        ],
        compiler_params=pltpu.CompilerParams(collective_id=tag, has_side_effects=True),
        cost_estimate=pl.CostEstimate(flops=0, bytes_accessed=2 * moved, transcendentals=0),
    )(*operands)
    return outs


def gather_chip(block, tag):
    outs = exchange(block, False, tag)
    return outs[0].reshape(-1, block.shape[1])


def gather_swap(block, tag, weights):
    outs = exchange(block, False, tag, weights)
    return outs[0].reshape(-1, block.shape[1]), outs[1]


def scatter_chip(partial, tag):
    count = lax.axis_size("chip")
    outs = exchange(partial.reshape(count, -1, partial.shape[1]), True, tag)
    return jnp.sum(outs[0].astype(jnp.float32), axis=0)


def mlp_kernel(count, ff, own_block, weights, rs_out, own_w, other_w, slots, partials, ag_send, ag_recv, rs_send, rs_recv, swap_sems, local_sems):
    me = lax.axis_index("chip")
    group = lax.axis_index("group")
    core = lax.axis_index("core")
    mesh_ids = pl.DeviceIdType.MESH
    barrier = pltpu.get_barrier_semaphore()
    for shift in range(1, count):
        peer = lax.rem(me + shift, count)
        pl.semaphore_signal(barrier, inc=1, device_id=(group, peer, core), device_id_type=mesh_ids)
    pl.semaphore_signal(barrier, inc=1, device_id=(group, me, 1 - core), device_id_type=mesh_ids)
    pl.semaphore_wait(barrier, count)
    load_w = pltpu.make_async_copy(weights, own_w, local_sems.at[0])
    load_w.start()
    load_x = pltpu.make_async_copy(own_block, slots.at[me], local_sems.at[1])
    load_x.start()
    swap = pltpu.make_async_remote_copy(
        src_ref=weights,
        dst_ref=other_w,
        send_sem=swap_sems.at[0],
        recv_sem=swap_sems.at[1],
        device_id=(group, me, 1 - core),
        device_id_type=mesh_ids,
    )
    swap.start()
    sends = [swap]
    for shift in range(1, count):
        peer = lax.rem(me + shift, count)
        copy = pltpu.make_async_remote_copy(
            src_ref=own_block,
            dst_ref=slots.at[me],
            send_sem=ag_send.at[shift],
            recv_sem=ag_recv.at[shift],
            device_id=(group, peer, core),
            device_id_type=mesh_ids,
        )
        copy.start()
        sends.append(copy)
    load_w.wait()
    swap.wait_recv()
    load_x.wait()
    outs = []
    for shift in range(count):
        sender = lax.rem(me + count - shift, count)
        if shift > 0:
            pltpu.make_async_remote_copy(
                src_ref=slots.at[sender],
                dst_ref=slots.at[sender],
                send_sem=ag_send.at[shift],
                recv_sem=ag_recv.at[shift],
                device_id=(group, sender, core),
                device_id_type=mesh_ids,
            ).wait_recv()
        rows = slots[sender]
        total = None
        for table in (own_w, other_w):
            gate = jnp.dot(rows, table[:, pl.ds(0, ff)], preferred_element_type=jnp.float32)
            up = jnp.dot(rows, table[:, pl.ds(ff, ff)], preferred_element_type=jnp.float32)
            act = (gate / (1.0 + jnp.exp(-gate)) * up).astype(jnp.bfloat16)
            down = lax.dot_general(
                act, table[:, pl.ds(2 * ff, ff)], (((1,), (1,)), ((), ())),
                preferred_element_type=jnp.float32,
            )
            total = down if total is None else total + down
        partials[shift] = total.astype(jnp.bfloat16)
        if shift == 0:
            back = pltpu.make_async_copy(partials.at[0], rs_out.at[me], local_sems.at[2])
        else:
            back = pltpu.make_async_remote_copy(
                src_ref=partials.at[shift],
                dst_ref=rs_out.at[me],
                send_sem=rs_send.at[shift],
                recv_sem=rs_recv.at[shift],
                device_id=(group, sender, core),
                device_id_type=mesh_ids,
            )
        back.start()
        outs.append(back)
    for shift in range(1, count):
        owner = lax.rem(me + shift, count)
        pltpu.make_async_remote_copy(
            src_ref=partials.at[shift],
            dst_ref=rs_out.at[owner],
            send_sem=rs_send.at[shift],
            recv_sem=rs_recv.at[shift],
            device_id=(group, owner, core),
            device_id_type=mesh_ids,
        ).wait_recv()
    outs[0].wait()
    for copy in outs[1:]:
        copy.wait_send()
    for copy in sends:
        copy.wait_send()


def fused_mlp(block, weights, tag):
    count = lax.axis_size("chip")
    rows, cols = block.shape
    ff = weights.shape[1] // 3
    flops = 2 * count * rows * cols * ff * 6
    return pl.pallas_call(
        functools.partial(mlp_kernel, count, ff),
        out_shape=jax.ShapeDtypeStruct((count, rows, cols), block.dtype),
        in_specs=[pl.BlockSpec(memory_space=pl.ANY)] * 2,
        out_specs=pl.BlockSpec(memory_space=pl.ANY),
        scratch_shapes=[
            pltpu.VMEM(weights.shape, weights.dtype),
            pltpu.VMEM(weights.shape, weights.dtype),
            pltpu.VMEM((count, rows, cols), block.dtype),
            pltpu.VMEM((count, rows, cols), block.dtype),
            pltpu.SemaphoreType.DMA((count,)),
            pltpu.SemaphoreType.DMA((count,)),
            pltpu.SemaphoreType.DMA((count,)),
            pltpu.SemaphoreType.DMA((count,)),
            pltpu.SemaphoreType.DMA((2,)),
            pltpu.SemaphoreType.DMA((3,)),
        ],
        compiler_params=pltpu.CompilerParams(
            collective_id=tag, has_side_effects=True, vmem_limit_bytes=60 * 1024 * 1024
        ),
        cost_estimate=pl.CostEstimate(
            flops=flops, bytes_accessed=4 * count * rows * cols * 2, transcendentals=count * rows * ff * 2
        ),
    )(block, weights)


def gather_group(block):
    count = lax.axis_size("group")
    pieces = [block]
    for shift in range(1, count):
        route = [(source, (source + shift) % count) for source in range(count)]
        pieces.append(lax.ppermute(block, "group", route))
    stacked = jnp.stack(pieces)
    order = (lax.axis_index("group") - jnp.arange(count)) % count
    return jnp.take(stacked, order, axis=0).reshape(count * block.shape[0], block.shape[1])


def rms_scale(values, gain):
    square = jnp.mean(values * values, axis=-1, keepdims=True)
    return (values * lax.rsqrt(square + norm_eps) * gain).astype(jnp.bfloat16)


def rotate(values, places):
    half_dim = values.shape[-1] // 2
    frequency = rope_base ** (-(jnp.arange(half_dim, dtype=jnp.float32) * 2.0 / values.shape[-1]))
    angle = places.astype(jnp.float32)[:, None] * frequency[None, :]
    cosine = jnp.cos(angle)[:, None, :]
    sine = jnp.sin(angle)[:, None, :]
    widened = values.astype(jnp.float32)
    first = widened[..., :half_dim]
    second = widened[..., half_dim:]
    return jnp.concatenate(
        [first * cosine - second * sine, second * cosine + first * sine], axis=-1
    ).astype(jnp.bfloat16)


def by_core(own_part, other_part):
    first = lax.axis_index("core") == 0
    return jnp.where(first, own_part, other_part), jnp.where(first, other_part, own_part)


def dot(acts, weight):
    return jnp.dot(acts, weight, preferred_element_type=jnp.float32)


def dot_t(acts, weight_t):
    return lax.dot_general(
        acts, weight_t, (((1,), (1,)), ((), ())), preferred_element_type=jnp.float32
    )


def core_rows(values, chips, rows_dev):
    blocks = values.reshape(chips, 2, rows_dev, *values.shape[1:])
    own = lax.dynamic_index_in_dim(blocks, lax.axis_index("core"), axis=1, keepdims=False)
    return own.reshape(chips * rows_dev, *values.shape[1:])


def body(
    hidden,
    request_of,
    positions,
    page_table,
    attn_gain,
    mlp_gain,
    wq,
    wk,
    wv,
    wo,
    w_gate,
    w_up,
    w_down,
):
    chips = lax.axis_size("chip")
    rows_dev = hidden.shape[0]
    tok_group = request_of.shape[0]
    bf = jnp.bfloat16
    residual = hidden.astype(jnp.float32)
    q_cols = wq.shape[1]
    kv_half = wk.shape[1]
    own_attn = jnp.concatenate([wq.astype(bf), wk.astype(bf), wv.astype(bf), wo.astype(bf).T], axis=1)
    own_attn = lax.all_gather(own_attn, "group", axis=0, tiled=True)
    normed = gather_chip(rms_scale(residual, attn_gain), 0)
    other_attn = swap_cores(own_attn)
    query_w = jnp.concatenate([own_attn[:, :q_cols], other_attn[:, :q_cols]], axis=1)
    out_w_t = jnp.concatenate(
        [own_attn[:, q_cols + 2 * kv_half :], other_attn[:, q_cols + 2 * kv_half :]], axis=1
    )
    key_lo, key_hi = by_core(own_attn[:, q_cols : q_cols + kv_half], other_attn[:, q_cols : q_cols + kv_half])
    value_lo, value_hi = by_core(
        own_attn[:, q_cols + kv_half : q_cols + 2 * kv_half],
        other_attn[:, q_cols + kv_half : q_cols + 2 * kv_half],
    )
    key_w = jnp.concatenate([key_lo, key_hi], axis=1)
    value_w = jnp.concatenate([value_lo, value_hi], axis=1)
    ff_cols = w_gate.shape[1]
    own_mlp = jnp.concatenate([w_gate.astype(bf), w_up.astype(bf), w_down.astype(bf).T], axis=1)
    own_mlp = lax.all_gather(own_mlp, "group", axis=0, tiled=True)
    half_pos = core_rows(positions, chips, rows_dev)
    half_req = core_rows(request_of, chips, rows_dev)
    heads = 2 * q_cols // HD
    queries = rotate(dot(normed, query_w).astype(bf).reshape(-1, heads, HD), half_pos)
    keys_half = rotate(dot(normed, key_w).astype(bf).reshape(-1, 1, HD), half_pos)
    values_half = dot(normed, value_w).astype(bf).reshape(-1, 1, HD)
    kv_own = jnp.stack([keys_half[:, 0], values_half[:, 0]], axis=1)
    kv_other = swap_cores(kv_own)
    kv_lo, kv_hi = by_core(kv_own, kv_other)
    kv_rows = jnp.stack(
        [kv_lo.reshape(chips, rows_dev, 2, HD), kv_hi.reshape(chips, rows_dev, 2, HD)], axis=1
    ).reshape(tok_group, 2, HD)
    earlier_rows = min(MAXLEN, tok_group)
    earlier = from_behind(kv_rows[tok_group - earlier_rows :], "group", 1)
    all_rows = jnp.concatenate([earlier, kv_rows], axis=0)
    all_keys = all_rows[:, 0]
    all_values = all_rows[:, 1]
    first_request = request_of[0]
    first_position = positions[0]
    same_local = (half_req[:, None] == request_of[None, :]) & (
        positions[None, :] <= half_pos[:, None]
    )
    same_earlier = (half_req[:, None] == first_request) & (
        jnp.arange(earlier_rows)[None, :] >= earlier_rows - first_position
    )
    visible = jnp.concatenate([same_earlier, same_local], axis=1)
    scores = jnp.einsum(
        "qhd,kd->hqk", queries, all_keys, preferred_element_type=jnp.float32
    ) * HD ** (-0.5)
    scores = jnp.where(visible[None], scores, -1e30)
    row_peak = jnp.max(scores, axis=-1, keepdims=True)
    probs = jnp.where(visible[None], jnp.exp(scores - row_peak), 0.0)
    total = jnp.sum(probs, axis=-1, keepdims=True)
    mixed_heads = jnp.einsum(
        "hqk,kd->qhd", probs.astype(bf), all_values, preferred_element_type=jnp.float32
    ) / jnp.transpose(total, (1, 0, 2))
    attended = mixed_heads.astype(bf).reshape(-1, heads * HD)
    attn_part = dot_t(attended, out_w_t)
    attn_sum = scatter_chip(attn_part.astype(bf), 1)
    mixed = residual + attn_sum
    partials = fused_mlp(rms_scale(mixed, mlp_gain), own_mlp, 2)
    layer_out = (mixed + jnp.sum(partials.astype(jnp.float32), axis=0)).astype(bf)
    pages = page_table.shape[1]
    changed = jnp.concatenate(
        [jnp.ones((1,), jnp.int32), (request_of[1:] != request_of[:-1]).astype(jnp.int32)]
    )
    opens = jnp.maximum(changed, (positions % PAGE == 0).astype(jnp.int32))
    logical = jnp.cumsum(opens) - 1
    chosen = jnp.sum(
        jnp.where(logical[:, None] == jnp.arange(pages)[None, :], page_table, 0), axis=1
    )
    target = chosen * PAGE + positions % PAGE
    own_slice = lax.dynamic_index_in_dim(kv_rows, lax.axis_index("core"), axis=1, keepdims=False)
    width = own_slice.shape[1]
    source_row = jnp.full((pages * PAGE,), tok_group, jnp.int32).at[target].set(
        jnp.arange(tok_group, dtype=jnp.int32)
    )
    padded = jnp.concatenate([own_slice, jnp.zeros((1, width), own_slice.dtype)], axis=0)
    cache = jnp.take(padded, source_row, axis=0)
    return (layer_out, cache.reshape(pages, PAGE, width))


def solution(mesh):
    groups, tensors = mesh.devices.shape
    split = Mesh(mesh.devices.reshape(groups, tensors // 2, 2), ("group", "chip", "core"))
    tensor = ("chip", "core")
    placed = (
        P(("group",) + tensor, None),
        P("group"),
        P("group"),
        P("group", None),
        P(),
        P(),
        P("group", tensor),
        P("group", tensor),
        P("group", tensor),
        P(tensor, "group"),
        P("group", tensor),
        P("group", tensor),
        P(tensor, "group"),
    )
    return jax.shard_map(
        body,
        mesh=split,
        in_specs=placed,
        out_specs=(P(("group",) + tensor, None), P("group", None, tensor)),
        check_vma=False,
    )
```

```python
import functools

import jax
import jax.numpy as jnp
from jax import lax
from jax.experimental import pallas as pl
from jax.experimental.pallas import tpu as pltpu
from jax.sharding import Mesh
from jax.sharding import PartitionSpec as P

QH = 16
KVH = 8
HD = 128
PAGE = 128
MAXLEN = 512
SWAP_PARTS = 4


rope_base = 1000000.0
norm_eps = 1e-06


def swap_cores(value):
    return lax.ppermute(value, "core", [(0, 1), (1, 0)])


def from_behind(block, axis, distance):
    devices = range(lax.axis_size(axis))
    route = [(i - distance, i) for i in devices if i - distance in devices]
    return lax.ppermute(block, axis, route)


def exchange_kernel(count, spread, spreads, swaps, *refs):
    source = refs[0]
    weights = refs[1] if (spreads or swaps) else None
    outs = refs[1 + (spreads or swaps) :]
    slots = outs[0]
    moved = outs[1] if (spreads or swaps) else None
    send_sems, recv_sems, local_sem = outs[-3:]
    me = lax.axis_index("chip")
    group = lax.axis_index("group")
    core = lax.axis_index("core")
    groups = lax.axis_size("group")
    mesh_ids = pl.DeviceIdType.MESH
    barrier = pltpu.get_barrier_semaphore()
    for shift in range(1, count):
        peer = lax.rem(me + shift, count)
        pl.semaphore_signal(barrier, inc=1, device_id=(group, peer, core), device_id_type=mesh_ids)
    greeted = count - 1
    if swaps:
        pl.semaphore_signal(barrier, inc=1, device_id=(group, me, 1 - core), device_id_type=mesh_ids)
        greeted += 1
    if spreads:
        for shift in range(1, groups):
            peer = lax.rem(group + shift, groups)
            pl.semaphore_signal(barrier, inc=1, device_id=(peer, me, core), device_id_type=mesh_ids)
        greeted += groups - 1
    pl.semaphore_wait(barrier, greeted)
    local = pltpu.make_async_copy(source.at[me] if spread else source, slots.at[me], local_sem.at[0])
    local.start()
    locals_ = [local]
    copies = []
    if swaps:
        swap = pltpu.make_async_remote_copy(
            src_ref=weights,
            dst_ref=moved,
            send_sem=send_sems.at[0],
            recv_sem=recv_sems.at[0],
            device_id=(group, me, 1 - core),
            device_id_type=mesh_ids,
        )
        swap.start()
        copies.append(swap)
    if spreads:
        own_weights = pltpu.make_async_copy(weights, moved.at[group], local_sem.at[1])
        own_weights.start()
        locals_.append(own_weights)
        for shift in range(1, groups):
            peer = lax.rem(group + shift, groups)
            copy = pltpu.make_async_remote_copy(
                src_ref=weights,
                dst_ref=moved.at[group],
                send_sem=send_sems.at[count + shift],
                recv_sem=recv_sems.at[count + shift],
                device_id=(peer, me, core),
                device_id_type=mesh_ids,
            )
            copy.start()
            copies.append(copy)
    for shift in range(1, count):
        peer = lax.rem(me + shift, count)
        copy = pltpu.make_async_remote_copy(
            src_ref=source.at[peer] if spread else source,
            dst_ref=slots.at[me],
            send_sem=send_sems.at[shift],
            recv_sem=recv_sems.at[shift],
            device_id=(group, peer, core),
            device_id_type=mesh_ids,
        )
        copy.start()
        copies.append(copy)
    for shift in range(1, count):
        sender = lax.rem(me + count - shift, count)
        pltpu.make_async_remote_copy(
            src_ref=slots.at[sender],
            dst_ref=slots.at[sender],
            send_sem=send_sems.at[shift],
            recv_sem=recv_sems.at[shift],
            device_id=(group, sender, core),
            device_id_type=mesh_ids,
        ).wait_recv()
    if swaps:
        swap.wait_recv()
    if spreads:
        for shift in range(1, groups):
            sender = lax.rem(group + groups - shift, groups)
            pltpu.make_async_remote_copy(
                src_ref=moved.at[sender],
                dst_ref=moved.at[sender],
                send_sem=send_sems.at[count + shift],
                recv_sem=recv_sems.at[count + shift],
                device_id=(sender, me, core),
                device_id_type=mesh_ids,
            ).wait_recv()
    for copy in copies:
        copy.wait_send()
    for copy in locals_:
        copy.wait()


def exchange(block, spread, tag, weights=None, spreads=False):
    count = lax.axis_size("chip")
    groups = lax.axis_size("group")
    rows, cols = block.shape[-2:]
    moved = count * rows * cols * block.dtype.itemsize
    out_shape = [jax.ShapeDtypeStruct((count, rows, cols), block.dtype)]
    operands = [block]
    swaps = weights is not None and not spreads
    if weights is not None:
        copies = groups if spreads else 1
        out_shape.append(jax.ShapeDtypeStruct((copies,) * spreads + weights.shape, weights.dtype))
        operands.append(weights)
        moved += copies * weights.size * weights.dtype.itemsize
    outs = pl.pallas_call(
        functools.partial(exchange_kernel, count, spread, spreads, swaps),
        out_shape=tuple(out_shape),
        in_specs=[pl.BlockSpec(memory_space=pl.ANY)] * len(operands),
        out_specs=tuple(pl.BlockSpec(memory_space=pl.ANY) for _ in out_shape),
        scratch_shapes=[
            pltpu.SemaphoreType.DMA((count + groups,)),
            pltpu.SemaphoreType.DMA((count + groups,)),
            pltpu.SemaphoreType.DMA((2,)),
        ],
        compiler_params=pltpu.CompilerParams(collective_id=tag, has_side_effects=True),
        cost_estimate=pl.CostEstimate(flops=0, bytes_accessed=2 * moved, transcendentals=0),
    )(*operands)
    return outs


def gather_chip(block, tag):
    outs = exchange(block, False, tag)
    return outs[0].reshape(-1, block.shape[1])


def gather_swap(block, tag, weights):
    outs = exchange(block, False, tag, weights)
    return outs[0].reshape(-1, block.shape[1]), outs[1]


def scatter_chip(partial, tag):
    count = lax.axis_size("chip")
    outs = exchange(partial.reshape(count, -1, partial.shape[1]), True, tag)
    return jnp.sum(outs[0].astype(jnp.float32), axis=0)


def mlp_kernel(count, ff, own_block, weights, rs_out, own_w, other_w, slots, partials, ag_send, ag_recv, rs_send, rs_recv, swap_sems, local_sems):
    me = lax.axis_index("chip")
    group = lax.axis_index("group")
    core = lax.axis_index("core")
    mesh_ids = pl.DeviceIdType.MESH
    barrier = pltpu.get_barrier_semaphore()
    for shift in range(1, count):
        peer = lax.rem(me + shift, count)
        pl.semaphore_signal(barrier, inc=1, device_id=(group, peer, core), device_id_type=mesh_ids)
    pl.semaphore_signal(barrier, inc=1, device_id=(group, me, 1 - core), device_id_type=mesh_ids)
    pl.semaphore_wait(barrier, count)
    load_w = pltpu.make_async_copy(weights, own_w, local_sems.at[0])
    load_w.start()
    load_x = pltpu.make_async_copy(own_block, slots.at[me], local_sems.at[1])
    load_x.start()
    parts = SWAP_PARTS
    depth = weights.shape[0] // parts
    swaps = []
    for part in range(parts):
        rows_part = pl.ds(part * depth, depth)
        swap = pltpu.make_async_remote_copy(
            src_ref=weights.at[rows_part],
            dst_ref=other_w.at[rows_part],
            send_sem=swap_sems.at[part],
            recv_sem=swap_sems.at[parts + part],
            device_id=(group, me, 1 - core),
            device_id_type=mesh_ids,
        )
        swap.start()
        swaps.append(swap)
    sends = list(swaps)
    for shift in range(1, count):
        peer = lax.rem(me + shift, count)
        copy = pltpu.make_async_remote_copy(
            src_ref=own_block,
            dst_ref=slots.at[me],
            send_sem=ag_send.at[shift],
            recv_sem=ag_recv.at[shift],
            device_id=(group, peer, core),
            device_id_type=mesh_ids,
        )
        copy.start()
        sends.append(copy)
    load_w.wait()
    for swap in swaps:
        swap.wait_recv()
    load_x.wait()
    outs = []
    for shift in range(count):
        sender = lax.rem(me + count - shift, count)
        if shift > 0:
            pltpu.make_async_remote_copy(
                src_ref=slots.at[sender],
                dst_ref=slots.at[sender],
                send_sem=ag_send.at[shift],
                recv_sem=ag_recv.at[shift],
                device_id=(group, sender, core),
                device_id_type=mesh_ids,
            ).wait_recv()
        rows = slots[sender]
        total = None
        for table in (own_w, other_w):
            gate = jnp.dot(rows, table[:, pl.ds(0, ff)], preferred_element_type=jnp.float32)
            up = jnp.dot(rows, table[:, pl.ds(ff, ff)], preferred_element_type=jnp.float32)
            act = (gate / (1.0 + jnp.exp(-gate)) * up).astype(jnp.bfloat16)
            down = lax.dot_general(
                act, table[:, pl.ds(2 * ff, ff)], (((1,), (1,)), ((), ())),
                preferred_element_type=jnp.float32,
            )
            total = down if total is None else total + down
        partials[shift] = total.astype(jnp.bfloat16)
        if shift == 0:
            back = pltpu.make_async_copy(partials.at[0], rs_out.at[me], local_sems.at[2])
        else:
            back = pltpu.make_async_remote_copy(
                src_ref=partials.at[shift],
                dst_ref=rs_out.at[me],
                send_sem=rs_send.at[shift],
                recv_sem=rs_recv.at[shift],
                device_id=(group, sender, core),
                device_id_type=mesh_ids,
            )
        back.start()
        outs.append(back)
    for shift in range(1, count):
        owner = lax.rem(me + shift, count)
        pltpu.make_async_remote_copy(
            src_ref=partials.at[shift],
            dst_ref=rs_out.at[owner],
            send_sem=rs_send.at[shift],
            recv_sem=rs_recv.at[shift],
            device_id=(group, owner, core),
            device_id_type=mesh_ids,
        ).wait_recv()
    outs[0].wait()
    for copy in outs[1:]:
        copy.wait_send()
    for copy in sends:
        copy.wait_send()


def fused_mlp(block, weights, tag):
    count = lax.axis_size("chip")
    rows, cols = block.shape
    ff = weights.shape[1] // 3
    flops = 2 * count * rows * cols * ff * 6
    return pl.pallas_call(
        functools.partial(mlp_kernel, count, ff),
        out_shape=jax.ShapeDtypeStruct((count, rows, cols), block.dtype),
        in_specs=[pl.BlockSpec(memory_space=pl.ANY)] * 2,
        out_specs=pl.BlockSpec(memory_space=pl.ANY),
        scratch_shapes=[
            pltpu.VMEM(weights.shape, weights.dtype),
            pltpu.VMEM(weights.shape, weights.dtype),
            pltpu.VMEM((count, rows, cols), block.dtype),
            pltpu.VMEM((count, rows, cols), block.dtype),
            pltpu.SemaphoreType.DMA((count,)),
            pltpu.SemaphoreType.DMA((count,)),
            pltpu.SemaphoreType.DMA((count,)),
            pltpu.SemaphoreType.DMA((count,)),
            pltpu.SemaphoreType.DMA((2 * SWAP_PARTS,)),
            pltpu.SemaphoreType.DMA((3,)),
        ],
        compiler_params=pltpu.CompilerParams(
            collective_id=tag, has_side_effects=True, vmem_limit_bytes=60 * 1024 * 1024
        ),
        cost_estimate=pl.CostEstimate(
            flops=flops, bytes_accessed=4 * count * rows * cols * 2, transcendentals=count * rows * ff * 2
        ),
    )(block, weights)


def gather_group(block):
    count = lax.axis_size("group")
    pieces = [block]
    for shift in range(1, count):
        route = [(source, (source + shift) % count) for source in range(count)]
        pieces.append(lax.ppermute(block, "group", route))
    stacked = jnp.stack(pieces)
    order = (lax.axis_index("group") - jnp.arange(count)) % count
    return jnp.take(stacked, order, axis=0).reshape(count * block.shape[0], block.shape[1])


def rms_scale(values, gain):
    square = jnp.mean(values * values, axis=-1, keepdims=True)
    return (values * lax.rsqrt(square + norm_eps) * gain).astype(jnp.bfloat16)


def rotate(values, places):
    half_dim = values.shape[-1] // 2
    frequency = rope_base ** (-(jnp.arange(half_dim, dtype=jnp.float32) * 2.0 / values.shape[-1]))
    angle = places.astype(jnp.float32)[:, None] * frequency[None, :]
    cosine = jnp.cos(angle)[:, None, :]
    sine = jnp.sin(angle)[:, None, :]
    widened = values.astype(jnp.float32)
    first = widened[..., :half_dim]
    second = widened[..., half_dim:]
    return jnp.concatenate(
        [first * cosine - second * sine, second * cosine + first * sine], axis=-1
    ).astype(jnp.bfloat16)


def by_core(own_part, other_part):
    first = lax.axis_index("core") == 0
    return jnp.where(first, own_part, other_part), jnp.where(first, other_part, own_part)


def dot(acts, weight):
    return jnp.dot(acts, weight, preferred_element_type=jnp.float32)


def dot_t(acts, weight_t):
    return lax.dot_general(
        acts, weight_t, (((1,), (1,)), ((), ())), preferred_element_type=jnp.float32
    )


def core_rows(values, chips, rows_dev):
    blocks = values.reshape(chips, 2, rows_dev, *values.shape[1:])
    own = lax.dynamic_index_in_dim(blocks, lax.axis_index("core"), axis=1, keepdims=False)
    return own.reshape(chips * rows_dev, *values.shape[1:])


def body(
    hidden,
    request_of,
    positions,
    page_table,
    attn_gain,
    mlp_gain,
    wq,
    wk,
    wv,
    wo,
    w_gate,
    w_up,
    w_down,
):
    chips = lax.axis_size("chip")
    rows_dev = hidden.shape[0]
    tok_group = request_of.shape[0]
    bf = jnp.bfloat16
    residual = hidden.astype(jnp.float32)
    q_cols = wq.shape[1]
    kv_half = wk.shape[1]
    own_attn = jnp.concatenate([wq.astype(bf), wk.astype(bf), wv.astype(bf), wo.astype(bf).T], axis=1)
    own_attn = lax.all_gather(own_attn, "group", axis=0, tiled=True)
    normed = gather_chip(rms_scale(residual, attn_gain), 0)
    other_attn = swap_cores(own_attn)
    query_w = jnp.concatenate([own_attn[:, :q_cols], other_attn[:, :q_cols]], axis=1)
    out_w_t = jnp.concatenate(
        [own_attn[:, q_cols + 2 * kv_half :], other_attn[:, q_cols + 2 * kv_half :]], axis=1
    )
    key_lo, key_hi = by_core(own_attn[:, q_cols : q_cols + kv_half], other_attn[:, q_cols : q_cols + kv_half])
    value_lo, value_hi = by_core(
        own_attn[:, q_cols + kv_half : q_cols + 2 * kv_half],
        other_attn[:, q_cols + kv_half : q_cols + 2 * kv_half],
    )
    key_w = jnp.concatenate([key_lo, key_hi], axis=1)
    value_w = jnp.concatenate([value_lo, value_hi], axis=1)
    ff_cols = w_gate.shape[1]
    own_mlp = jnp.concatenate([w_gate.astype(bf), w_up.astype(bf), w_down.astype(bf).T], axis=1)
    own_mlp = lax.all_gather(own_mlp, "group", axis=0, tiled=True)
    half_pos = core_rows(positions, chips, rows_dev)
    half_req = core_rows(request_of, chips, rows_dev)
    heads = 2 * q_cols // HD
    queries = rotate(dot(normed, query_w).astype(bf).reshape(-1, heads, HD), half_pos)
    keys_half = rotate(dot(normed, key_w).astype(bf).reshape(-1, 1, HD), half_pos)
    values_half = dot(normed, value_w).astype(bf).reshape(-1, 1, HD)
    kv_own = jnp.stack([keys_half[:, 0], values_half[:, 0]], axis=1)
    kv_other = swap_cores(kv_own)
    kv_lo, kv_hi = by_core(kv_own, kv_other)
    kv_rows = jnp.stack(
        [kv_lo.reshape(chips, rows_dev, 2, HD), kv_hi.reshape(chips, rows_dev, 2, HD)], axis=1
    ).reshape(tok_group, 2, HD)
    earlier_rows = min(MAXLEN, tok_group)
    earlier = from_behind(kv_rows[tok_group - earlier_rows :], "group", 1)
    all_rows = jnp.concatenate([earlier, kv_rows], axis=0)
    all_keys = all_rows[:, 0]
    all_values = all_rows[:, 1]
    first_request = request_of[0]
    first_position = positions[0]
    same_local = (half_req[:, None] == request_of[None, :]) & (
        positions[None, :] <= half_pos[:, None]
    )
    same_earlier = (half_req[:, None] == first_request) & (
        jnp.arange(earlier_rows)[None, :] >= earlier_rows - first_position
    )
    visible = jnp.concatenate([same_earlier, same_local], axis=1)
    scores = jnp.einsum(
        "qhd,kd->hqk", queries, all_keys, preferred_element_type=jnp.float32
    ) * HD ** (-0.5)
    scores = jnp.where(visible[None], scores, -1e30)
    row_peak = jnp.max(scores, axis=-1, keepdims=True)
    probs = jnp.where(visible[None], jnp.exp(scores - row_peak), 0.0)
    total = jnp.sum(probs, axis=-1, keepdims=True)
    mixed_heads = jnp.einsum(
        "hqk,kd->qhd", probs.astype(bf), all_values, preferred_element_type=jnp.float32
    ) / jnp.transpose(total, (1, 0, 2))
    attended = mixed_heads.astype(bf).reshape(-1, heads * HD)
    attn_part = dot_t(attended, out_w_t)
    attn_sum = scatter_chip(attn_part.astype(bf), 1)
    mixed = residual + attn_sum
    partials = fused_mlp(rms_scale(mixed, mlp_gain), own_mlp, 2)
    layer_out = (mixed + jnp.sum(partials.astype(jnp.float32), axis=0)).astype(bf)
    pages = page_table.shape[1]
    changed = jnp.concatenate(
        [jnp.ones((1,), jnp.int32), (request_of[1:] != request_of[:-1]).astype(jnp.int32)]
    )
    opens = jnp.maximum(changed, (positions % PAGE == 0).astype(jnp.int32))
    logical = jnp.cumsum(opens) - 1
    chosen = jnp.sum(
        jnp.where(logical[:, None] == jnp.arange(pages)[None, :], page_table, 0), axis=1
    )
    target = chosen * PAGE + positions % PAGE
    own_slice = lax.dynamic_index_in_dim(kv_rows, lax.axis_index("core"), axis=1, keepdims=False)
    width = own_slice.shape[1]
    cache = jnp.zeros((pages * PAGE, width), jnp.bfloat16).at[target].set(own_slice)
    return (layer_out, cache.reshape(pages, PAGE, width))


def solution(mesh):
    groups, tensors = mesh.devices.shape
    split = Mesh(mesh.devices.reshape(groups, tensors // 2, 2), ("group", "chip", "core"))
    tensor = ("chip", "core")
    placed = (
        P(("group",) + tensor, None),
        P("group"),
        P("group"),
        P("group", None),
        P(),
        P(),
        P("group", tensor),
        P("group", tensor),
        P("group", tensor),
        P(tensor, "group"),
        P("group", tensor),
        P("group", tensor),
        P(tensor, "group"),
    )
    return jax.shard_map(
        body,
        mesh=split,
        in_specs=placed,
        out_specs=(P(("group",) + tensor, None), P("group", None, tensor)),
        check_vma=False,
    )
```

```python
import functools

import jax
import jax.numpy as jnp
from jax import lax
from jax.experimental import pallas as pl
from jax.experimental.pallas import tpu as pltpu
from jax.sharding import Mesh
from jax.sharding import PartitionSpec as P

QH = 16
KVH = 8
HD = 128
PAGE = 128
MAXLEN = 512
FAR_FIRST = (4, 2, 6, 3, 5, 1, 7)


rope_base = 1000000.0
norm_eps = 1e-06


def swap_cores(value):
    return lax.ppermute(value, "core", [(0, 1), (1, 0)])


def from_behind(block, axis, distance):
    devices = range(lax.axis_size(axis))
    route = [(i - distance, i) for i in devices if i - distance in devices]
    return lax.ppermute(block, axis, route)


def send_order(count):
    if sorted(FAR_FIRST) == list(range(1, count)):
        return FAR_FIRST
    return tuple(range(1, count))


def exchange_kernel(count, spread, spreads, swaps, *refs):
    source = refs[0]
    weights = refs[1] if (spreads or swaps) else None
    outs = refs[1 + (spreads or swaps) :]
    slots = outs[0]
    moved = outs[1] if (spreads or swaps) else None
    send_sems, recv_sems, local_sem = outs[-3:]
    me = lax.axis_index("chip")
    group = lax.axis_index("group")
    core = lax.axis_index("core")
    groups = lax.axis_size("group")
    mesh_ids = pl.DeviceIdType.MESH
    barrier = pltpu.get_barrier_semaphore()
    for shift in range(1, count):
        peer = lax.rem(me + shift, count)
        pl.semaphore_signal(barrier, inc=1, device_id=(group, peer, core), device_id_type=mesh_ids)
    greeted = count - 1
    if swaps:
        pl.semaphore_signal(barrier, inc=1, device_id=(group, me, 1 - core), device_id_type=mesh_ids)
        greeted += 1
    if spreads:
        for shift in range(1, groups):
            peer = lax.rem(group + shift, groups)
            pl.semaphore_signal(barrier, inc=1, device_id=(peer, me, core), device_id_type=mesh_ids)
        greeted += groups - 1
    pl.semaphore_wait(barrier, greeted)
    local = pltpu.make_async_copy(source.at[me] if spread else source, slots.at[me], local_sem.at[0])
    local.start()
    locals_ = [local]
    copies = []
    if swaps:
        swap = pltpu.make_async_remote_copy(
            src_ref=weights,
            dst_ref=moved,
            send_sem=send_sems.at[0],
            recv_sem=recv_sems.at[0],
            device_id=(group, me, 1 - core),
            device_id_type=mesh_ids,
        )
        swap.start()
        copies.append(swap)
    if spreads:
        own_weights = pltpu.make_async_copy(weights, moved.at[group], local_sem.at[1])
        own_weights.start()
        locals_.append(own_weights)
        for shift in range(1, groups):
            peer = lax.rem(group + shift, groups)
            copy = pltpu.make_async_remote_copy(
                src_ref=weights,
                dst_ref=moved.at[group],
                send_sem=send_sems.at[count + shift],
                recv_sem=recv_sems.at[count + shift],
                device_id=(peer, me, core),
                device_id_type=mesh_ids,
            )
            copy.start()
            copies.append(copy)
    for shift in send_order(count):
        peer = lax.rem(me + shift, count)
        copy = pltpu.make_async_remote_copy(
            src_ref=source.at[peer] if spread else source,
            dst_ref=slots.at[me],
            send_sem=send_sems.at[shift],
            recv_sem=recv_sems.at[shift],
            device_id=(group, peer, core),
            device_id_type=mesh_ids,
        )
        copy.start()
        copies.append(copy)
    for shift in range(1, count):
        sender = lax.rem(me + count - shift, count)
        pltpu.make_async_remote_copy(
            src_ref=slots.at[sender],
            dst_ref=slots.at[sender],
            send_sem=send_sems.at[shift],
            recv_sem=recv_sems.at[shift],
            device_id=(group, sender, core),
            device_id_type=mesh_ids,
        ).wait_recv()
    if swaps:
        swap.wait_recv()
    if spreads:
        for shift in range(1, groups):
            sender = lax.rem(group + groups - shift, groups)
            pltpu.make_async_remote_copy(
                src_ref=moved.at[sender],
                dst_ref=moved.at[sender],
                send_sem=send_sems.at[count + shift],
                recv_sem=recv_sems.at[count + shift],
                device_id=(sender, me, core),
                device_id_type=mesh_ids,
            ).wait_recv()
    for copy in copies:
        copy.wait_send()
    for copy in locals_:
        copy.wait()


def exchange(block, spread, tag, weights=None, spreads=False):
    count = lax.axis_size("chip")
    groups = lax.axis_size("group")
    rows, cols = block.shape[-2:]
    moved = count * rows * cols * block.dtype.itemsize
    out_shape = [jax.ShapeDtypeStruct((count, rows, cols), block.dtype)]
    operands = [block]
    swaps = weights is not None and not spreads
    if weights is not None:
        copies = groups if spreads else 1
        out_shape.append(jax.ShapeDtypeStruct((copies,) * spreads + weights.shape, weights.dtype))
        operands.append(weights)
        moved += copies * weights.size * weights.dtype.itemsize
    outs = pl.pallas_call(
        functools.partial(exchange_kernel, count, spread, spreads, swaps),
        out_shape=tuple(out_shape),
        in_specs=[pl.BlockSpec(memory_space=pl.ANY)] * len(operands),
        out_specs=tuple(pl.BlockSpec(memory_space=pl.ANY) for _ in out_shape),
        scratch_shapes=[
            pltpu.SemaphoreType.DMA((count + groups,)),
            pltpu.SemaphoreType.DMA((count + groups,)),
            pltpu.SemaphoreType.DMA((2,)),
        ],
        compiler_params=pltpu.CompilerParams(collective_id=tag, has_side_effects=True),
        cost_estimate=pl.CostEstimate(flops=0, bytes_accessed=2 * moved, transcendentals=0),
    )(*operands)
    return outs


def gather_chip(block, tag):
    outs = exchange(block, False, tag)
    return outs[0].reshape(-1, block.shape[1])


def gather_swap(block, tag, weights):
    outs = exchange(block, False, tag, weights)
    return outs[0].reshape(-1, block.shape[1]), outs[1]


def scatter_chip(partial, tag):
    count = lax.axis_size("chip")
    outs = exchange(partial.reshape(count, -1, partial.shape[1]), True, tag)
    return jnp.sum(outs[0].astype(jnp.float32), axis=0)


def mlp_kernel(count, ff, own_block, weights, rs_out, own_w, other_w, slots, partials, ag_send, ag_recv, rs_send, rs_recv, swap_sems, local_sems):
    me = lax.axis_index("chip")
    group = lax.axis_index("group")
    core = lax.axis_index("core")
    mesh_ids = pl.DeviceIdType.MESH
    barrier = pltpu.get_barrier_semaphore()
    for shift in range(1, count):
        peer = lax.rem(me + shift, count)
        pl.semaphore_signal(barrier, inc=1, device_id=(group, peer, core), device_id_type=mesh_ids)
    pl.semaphore_signal(barrier, inc=1, device_id=(group, me, 1 - core), device_id_type=mesh_ids)
    pl.semaphore_wait(barrier, count)
    load_w = pltpu.make_async_copy(weights, own_w, local_sems.at[0])
    load_w.start()
    load_x = pltpu.make_async_copy(own_block, slots.at[me], local_sems.at[1])
    load_x.start()
    swap = pltpu.make_async_remote_copy(
        src_ref=weights,
        dst_ref=other_w,
        send_sem=swap_sems.at[0],
        recv_sem=swap_sems.at[1],
        device_id=(group, me, 1 - core),
        device_id_type=mesh_ids,
    )
    swap.start()
    sends = [swap]
    for shift in send_order(count):
        peer = lax.rem(me + shift, count)
        copy = pltpu.make_async_remote_copy(
            src_ref=own_block,
            dst_ref=slots.at[me],
            send_sem=ag_send.at[shift],
            recv_sem=ag_recv.at[shift],
            device_id=(group, peer, core),
            device_id_type=mesh_ids,
        )
        copy.start()
        sends.append(copy)
    load_w.wait()
    swap.wait_recv()
    load_x.wait()
    outs = []
    for shift in range(count):
        sender = lax.rem(me + count - shift, count)
        if shift > 0:
            pltpu.make_async_remote_copy(
                src_ref=slots.at[sender],
                dst_ref=slots.at[sender],
                send_sem=ag_send.at[shift],
                recv_sem=ag_recv.at[shift],
                device_id=(group, sender, core),
                device_id_type=mesh_ids,
            ).wait_recv()
        rows = slots[sender]
        total = None
        for table in (own_w, other_w):
            gate = jnp.dot(rows, table[:, pl.ds(0, ff)], preferred_element_type=jnp.float32)
            up = jnp.dot(rows, table[:, pl.ds(ff, ff)], preferred_element_type=jnp.float32)
            act = (gate / (1.0 + jnp.exp(-gate)) * up).astype(jnp.bfloat16)
            down = lax.dot_general(
                act, table[:, pl.ds(2 * ff, ff)], (((1,), (1,)), ((), ())),
                preferred_element_type=jnp.float32,
            )
            total = down if total is None else total + down
        partials[shift] = total.astype(jnp.bfloat16)
        if shift == 0:
            back = pltpu.make_async_copy(partials.at[0], rs_out.at[me], local_sems.at[2])
        else:
            back = pltpu.make_async_remote_copy(
                src_ref=partials.at[shift],
                dst_ref=rs_out.at[me],
                send_sem=rs_send.at[shift],
                recv_sem=rs_recv.at[shift],
                device_id=(group, sender, core),
                device_id_type=mesh_ids,
            )
        back.start()
        outs.append(back)
    for shift in range(1, count):
        owner = lax.rem(me + shift, count)
        pltpu.make_async_remote_copy(
            src_ref=partials.at[shift],
            dst_ref=rs_out.at[owner],
            send_sem=rs_send.at[shift],
            recv_sem=rs_recv.at[shift],
            device_id=(group, owner, core),
            device_id_type=mesh_ids,
        ).wait_recv()
    outs[0].wait()
    for copy in outs[1:]:
        copy.wait_send()
    for copy in sends:
        copy.wait_send()


def fused_mlp(block, weights, tag):
    count = lax.axis_size("chip")
    rows, cols = block.shape
    ff = weights.shape[1] // 3
    flops = 2 * count * rows * cols * ff * 6
    return pl.pallas_call(
        functools.partial(mlp_kernel, count, ff),
        out_shape=jax.ShapeDtypeStruct((count, rows, cols), block.dtype),
        in_specs=[pl.BlockSpec(memory_space=pl.ANY)] * 2,
        out_specs=pl.BlockSpec(memory_space=pl.ANY),
        scratch_shapes=[
            pltpu.VMEM(weights.shape, weights.dtype),
            pltpu.VMEM(weights.shape, weights.dtype),
            pltpu.VMEM((count, rows, cols), block.dtype),
            pltpu.VMEM((count, rows, cols), block.dtype),
            pltpu.SemaphoreType.DMA((count,)),
            pltpu.SemaphoreType.DMA((count,)),
            pltpu.SemaphoreType.DMA((count,)),
            pltpu.SemaphoreType.DMA((count,)),
            pltpu.SemaphoreType.DMA((2,)),
            pltpu.SemaphoreType.DMA((3,)),
        ],
        compiler_params=pltpu.CompilerParams(
            collective_id=tag, has_side_effects=True, vmem_limit_bytes=60 * 1024 * 1024
        ),
        cost_estimate=pl.CostEstimate(
            flops=flops, bytes_accessed=4 * count * rows * cols * 2, transcendentals=count * rows * ff * 2
        ),
    )(block, weights)


def gather_group(block):
    count = lax.axis_size("group")
    pieces = [block]
    for shift in range(1, count):
        route = [(source, (source + shift) % count) for source in range(count)]
        pieces.append(lax.ppermute(block, "group", route))
    stacked = jnp.stack(pieces)
    order = (lax.axis_index("group") - jnp.arange(count)) % count
    return jnp.take(stacked, order, axis=0).reshape(count * block.shape[0], block.shape[1])


def rms_scale(values, gain):
    square = jnp.mean(values * values, axis=-1, keepdims=True)
    return (values * lax.rsqrt(square + norm_eps) * gain).astype(jnp.bfloat16)


def rotate(values, places):
    half_dim = values.shape[-1] // 2
    frequency = rope_base ** (-(jnp.arange(half_dim, dtype=jnp.float32) * 2.0 / values.shape[-1]))
    angle = places.astype(jnp.float32)[:, None] * frequency[None, :]
    cosine = jnp.cos(angle)[:, None, :]
    sine = jnp.sin(angle)[:, None, :]
    widened = values.astype(jnp.float32)
    first = widened[..., :half_dim]
    second = widened[..., half_dim:]
    return jnp.concatenate(
        [first * cosine - second * sine, second * cosine + first * sine], axis=-1
    ).astype(jnp.bfloat16)


def by_core(own_part, other_part):
    first = lax.axis_index("core") == 0
    return jnp.where(first, own_part, other_part), jnp.where(first, other_part, own_part)


def dot(acts, weight):
    return jnp.dot(acts, weight, preferred_element_type=jnp.float32)


def dot_t(acts, weight_t):
    return lax.dot_general(
        acts, weight_t, (((1,), (1,)), ((), ())), preferred_element_type=jnp.float32
    )


def core_rows(values, chips, rows_dev):
    blocks = values.reshape(chips, 2, rows_dev, *values.shape[1:])
    own = lax.dynamic_index_in_dim(blocks, lax.axis_index("core"), axis=1, keepdims=False)
    return own.reshape(chips * rows_dev, *values.shape[1:])


def body(
    hidden,
    request_of,
    positions,
    page_table,
    attn_gain,
    mlp_gain,
    wq,
    wk,
    wv,
    wo,
    w_gate,
    w_up,
    w_down,
):
    chips = lax.axis_size("chip")
    rows_dev = hidden.shape[0]
    tok_group = request_of.shape[0]
    bf = jnp.bfloat16
    residual = hidden.astype(jnp.float32)
    q_cols = wq.shape[1]
    kv_half = wk.shape[1]
    own_attn = jnp.concatenate([wq.astype(bf), wk.astype(bf), wv.astype(bf), wo.astype(bf).T], axis=1)
    own_attn = lax.all_gather(own_attn, "group", axis=0, tiled=True)
    normed = gather_chip(rms_scale(residual, attn_gain), 0)
    other_attn = swap_cores(own_attn)
    query_w = jnp.concatenate([own_attn[:, :q_cols], other_attn[:, :q_cols]], axis=1)
    out_w_t = jnp.concatenate(
        [own_attn[:, q_cols + 2 * kv_half :], other_attn[:, q_cols + 2 * kv_half :]], axis=1
    )
    key_lo, key_hi = by_core(own_attn[:, q_cols : q_cols + kv_half], other_attn[:, q_cols : q_cols + kv_half])
    value_lo, value_hi = by_core(
        own_attn[:, q_cols + kv_half : q_cols + 2 * kv_half],
        other_attn[:, q_cols + kv_half : q_cols + 2 * kv_half],
    )
    key_w = jnp.concatenate([key_lo, key_hi], axis=1)
    value_w = jnp.concatenate([value_lo, value_hi], axis=1)
    ff_cols = w_gate.shape[1]
    own_mlp = jnp.concatenate([w_gate.astype(bf), w_up.astype(bf), w_down.astype(bf).T], axis=1)
    own_mlp = lax.all_gather(own_mlp, "group", axis=0, tiled=True)
    half_pos = core_rows(positions, chips, rows_dev)
    half_req = core_rows(request_of, chips, rows_dev)
    heads = 2 * q_cols // HD
    queries = rotate(dot(normed, query_w).astype(bf).reshape(-1, heads, HD), half_pos)
    keys_half = rotate(dot(normed, key_w).astype(bf).reshape(-1, 1, HD), half_pos)
    values_half = dot(normed, value_w).astype(bf).reshape(-1, 1, HD)
    kv_own = jnp.stack([keys_half[:, 0], values_half[:, 0]], axis=1)
    kv_other = swap_cores(kv_own)
    kv_lo, kv_hi = by_core(kv_own, kv_other)
    kv_rows = jnp.stack(
        [kv_lo.reshape(chips, rows_dev, 2, HD), kv_hi.reshape(chips, rows_dev, 2, HD)], axis=1
    ).reshape(tok_group, 2, HD)
    earlier_rows = min(MAXLEN, tok_group)
    earlier = from_behind(kv_rows[tok_group - earlier_rows :], "group", 1)
    all_rows = jnp.concatenate([earlier, kv_rows], axis=0)
    all_keys = all_rows[:, 0]
    all_values = all_rows[:, 1]
    first_request = request_of[0]
    first_position = positions[0]
    same_local = (half_req[:, None] == request_of[None, :]) & (
        positions[None, :] <= half_pos[:, None]
    )
    same_earlier = (half_req[:, None] == first_request) & (
        jnp.arange(earlier_rows)[None, :] >= earlier_rows - first_position
    )
    visible = jnp.concatenate([same_earlier, same_local], axis=1)
    scores = jnp.einsum(
        "qhd,kd->hqk", queries, all_keys, preferred_element_type=jnp.float32
    ) * HD ** (-0.5)
    scores = jnp.where(visible[None], scores, -1e30)
    row_peak = jnp.max(scores, axis=-1, keepdims=True)
    probs = jnp.where(visible[None], jnp.exp(scores - row_peak), 0.0)
    total = jnp.sum(probs, axis=-1, keepdims=True)
    mixed_heads = jnp.einsum(
        "hqk,kd->qhd", probs.astype(bf), all_values, preferred_element_type=jnp.float32
    ) / jnp.transpose(total, (1, 0, 2))
    attended = mixed_heads.astype(bf).reshape(-1, heads * HD)
    attn_part = dot_t(attended, out_w_t)
    attn_sum = scatter_chip(attn_part.astype(bf), 1)
    mixed = residual + attn_sum
    partials = fused_mlp(rms_scale(mixed, mlp_gain), own_mlp, 2)
    layer_out = (mixed + jnp.sum(partials.astype(jnp.float32), axis=0)).astype(bf)
    pages = page_table.shape[1]
    changed = jnp.concatenate(
        [jnp.ones((1,), jnp.int32), (request_of[1:] != request_of[:-1]).astype(jnp.int32)]
    )
    opens = jnp.maximum(changed, (positions % PAGE == 0).astype(jnp.int32))
    logical = jnp.cumsum(opens) - 1
    chosen = jnp.sum(
        jnp.where(logical[:, None] == jnp.arange(pages)[None, :], page_table, 0), axis=1
    )
    target = chosen * PAGE + positions % PAGE
    own_slice = lax.dynamic_index_in_dim(kv_rows, lax.axis_index("core"), axis=1, keepdims=False)
    width = own_slice.shape[1]
    cache = jnp.zeros((pages * PAGE, width), jnp.bfloat16).at[target].set(own_slice)
    return (layer_out, cache.reshape(pages, PAGE, width))


def solution(mesh):
    groups, tensors = mesh.devices.shape
    split = Mesh(mesh.devices.reshape(groups, tensors // 2, 2), ("group", "chip", "core"))
    tensor = ("chip", "core")
    placed = (
        P(("group",) + tensor, None),
        P("group"),
        P("group"),
        P("group", None),
        P(),
        P(),
        P("group", tensor),
        P("group", tensor),
        P("group", tensor),
        P(tensor, "group"),
        P("group", tensor),
        P("group", tensor),
        P(tensor, "group"),
    )
    return jax.shard_map(
        body,
        mesh=split,
        in_specs=placed,
        out_specs=(P(("group",) + tensor, None), P("group", None, tensor)),
        check_vma=False,
    )
```

```python
import functools

import jax
import jax.numpy as jnp
from jax import lax
from jax.experimental import pallas as pl
from jax.experimental.pallas import tpu as pltpu
from jax.sharding import Mesh
from jax.sharding import PartitionSpec as P

QH = 16
KVH = 8
HD = 128
PAGE = 128
MAXLEN = 512
FAR_FIRST = (4, 2, 6, 3, 5, 1, 7)


rope_base = 1000000.0
norm_eps = 1e-06


def swap_cores(value):
    return lax.ppermute(value, "core", [(0, 1), (1, 0)])


def from_behind(block, axis, distance):
    devices = range(lax.axis_size(axis))
    route = [(i - distance, i) for i in devices if i - distance in devices]
    return lax.ppermute(block, axis, route)


def send_order(count):
    if sorted(FAR_FIRST) == list(range(1, count)):
        return FAR_FIRST
    return tuple(range(1, count))


def exchange_kernel(count, spread, spreads, swaps, *refs):
    source = refs[0]
    weights = refs[1] if (spreads or swaps) else None
    outs = refs[1 + (spreads or swaps) :]
    slots = outs[0]
    moved = outs[1] if (spreads or swaps) else None
    send_sems, recv_sems, local_sem = outs[-3:]
    me = lax.axis_index("chip")
    group = lax.axis_index("group")
    core = lax.axis_index("core")
    groups = lax.axis_size("group")
    mesh_ids = pl.DeviceIdType.MESH
    barrier = pltpu.get_barrier_semaphore()
    for shift in range(1, count):
        peer = lax.rem(me + shift, count)
        pl.semaphore_signal(barrier, inc=1, device_id=(group, peer, core), device_id_type=mesh_ids)
    greeted = count - 1
    if swaps:
        pl.semaphore_signal(barrier, inc=1, device_id=(group, me, 1 - core), device_id_type=mesh_ids)
        greeted += 1
    if spreads:
        for shift in range(1, groups):
            peer = lax.rem(group + shift, groups)
            pl.semaphore_signal(barrier, inc=1, device_id=(peer, me, core), device_id_type=mesh_ids)
        greeted += groups - 1
    pl.semaphore_wait(barrier, greeted)
    local = pltpu.make_async_copy(source.at[me] if spread else source, slots.at[me], local_sem.at[0])
    local.start()
    locals_ = [local]
    copies = []
    if swaps:
        swap = pltpu.make_async_remote_copy(
            src_ref=weights,
            dst_ref=moved,
            send_sem=send_sems.at[0],
            recv_sem=recv_sems.at[0],
            device_id=(group, me, 1 - core),
            device_id_type=mesh_ids,
        )
        swap.start()
        copies.append(swap)
    if spreads:
        own_weights = pltpu.make_async_copy(weights, moved.at[group], local_sem.at[1])
        own_weights.start()
        locals_.append(own_weights)
        for shift in range(1, groups):
            peer = lax.rem(group + shift, groups)
            copy = pltpu.make_async_remote_copy(
                src_ref=weights,
                dst_ref=moved.at[group],
                send_sem=send_sems.at[count + shift],
                recv_sem=recv_sems.at[count + shift],
                device_id=(peer, me, core),
                device_id_type=mesh_ids,
            )
            copy.start()
            copies.append(copy)
    for shift in send_order(count):
        peer = lax.rem(me + shift, count)
        copy = pltpu.make_async_remote_copy(
            src_ref=source.at[peer] if spread else source,
            dst_ref=slots.at[me],
            send_sem=send_sems.at[shift],
            recv_sem=recv_sems.at[shift],
            device_id=(group, peer, core),
            device_id_type=mesh_ids,
        )
        copy.start()
        copies.append(copy)
    for shift in range(1, count):
        sender = lax.rem(me + count - shift, count)
        pltpu.make_async_remote_copy(
            src_ref=slots.at[sender],
            dst_ref=slots.at[sender],
            send_sem=send_sems.at[shift],
            recv_sem=recv_sems.at[shift],
            device_id=(group, sender, core),
            device_id_type=mesh_ids,
        ).wait_recv()
    if swaps:
        swap.wait_recv()
    if spreads:
        for shift in range(1, groups):
            sender = lax.rem(group + groups - shift, groups)
            pltpu.make_async_remote_copy(
                src_ref=moved.at[sender],
                dst_ref=moved.at[sender],
                send_sem=send_sems.at[count + shift],
                recv_sem=recv_sems.at[count + shift],
                device_id=(sender, me, core),
                device_id_type=mesh_ids,
            ).wait_recv()
    for copy in copies:
        copy.wait_send()
    for copy in locals_:
        copy.wait()


def exchange(block, spread, tag, weights=None, spreads=False):
    count = lax.axis_size("chip")
    groups = lax.axis_size("group")
    rows, cols = block.shape[-2:]
    moved = count * rows * cols * block.dtype.itemsize
    out_shape = [jax.ShapeDtypeStruct((count, rows, cols), block.dtype)]
    operands = [block]
    swaps = weights is not None and not spreads
    if weights is not None:
        copies = groups if spreads else 1
        out_shape.append(jax.ShapeDtypeStruct((copies,) * spreads + weights.shape, weights.dtype))
        operands.append(weights)
        moved += copies * weights.size * weights.dtype.itemsize
    outs = pl.pallas_call(
        functools.partial(exchange_kernel, count, spread, spreads, swaps),
        out_shape=tuple(out_shape),
        in_specs=[pl.BlockSpec(memory_space=pl.ANY)] * len(operands),
        out_specs=tuple(pl.BlockSpec(memory_space=pl.ANY) for _ in out_shape),
        scratch_shapes=[
            pltpu.SemaphoreType.DMA((count + groups,)),
            pltpu.SemaphoreType.DMA((count + groups,)),
            pltpu.SemaphoreType.DMA((2,)),
        ],
        compiler_params=pltpu.CompilerParams(collective_id=tag, has_side_effects=True),
        cost_estimate=pl.CostEstimate(flops=0, bytes_accessed=2 * moved, transcendentals=0),
    )(*operands)
    return outs


def gather_chip(block, tag):
    outs = exchange(block, False, tag)
    return outs[0].reshape(-1, block.shape[1])


def gather_swap(block, tag, weights):
    outs = exchange(block, False, tag, weights)
    return outs[0].reshape(-1, block.shape[1]), outs[1]


def scatter_chip(partial, tag):
    count = lax.axis_size("chip")
    outs = exchange(partial.reshape(count, -1, partial.shape[1]), True, tag)
    return jnp.sum(outs[0].astype(jnp.float32), axis=0)


def mlp_kernel(count, ff, own_block, weights, rs_out, own_w, other_w, slots, partials, ag_send, ag_recv, rs_send, rs_recv, swap_sems, local_sems):
    me = lax.axis_index("chip")
    group = lax.axis_index("group")
    core = lax.axis_index("core")
    mesh_ids = pl.DeviceIdType.MESH
    barrier = pltpu.get_barrier_semaphore()
    for shift in range(1, count):
        peer = lax.rem(me + shift, count)
        pl.semaphore_signal(barrier, inc=1, device_id=(group, peer, core), device_id_type=mesh_ids)
    pl.semaphore_signal(barrier, inc=1, device_id=(group, me, 1 - core), device_id_type=mesh_ids)
    pl.semaphore_wait(barrier, count)
    load_w = pltpu.make_async_copy(weights, own_w, local_sems.at[0])
    load_w.start()
    load_x = pltpu.make_async_copy(own_block, slots.at[me], local_sems.at[1])
    load_x.start()
    swap = pltpu.make_async_remote_copy(
        src_ref=weights,
        dst_ref=other_w,
        send_sem=swap_sems.at[0],
        recv_sem=swap_sems.at[1],
        device_id=(group, me, 1 - core),
        device_id_type=mesh_ids,
    )
    swap.start()
    sends = [swap]
    for shift in send_order(count):
        peer = lax.rem(me + shift, count)
        copy = pltpu.make_async_remote_copy(
            src_ref=own_block,
            dst_ref=slots.at[me],
            send_sem=ag_send.at[shift],
            recv_sem=ag_recv.at[shift],
            device_id=(group, peer, core),
            device_id_type=mesh_ids,
        )
        copy.start()
        sends.append(copy)
    load_w.wait()
    swap.wait_recv()
    load_x.wait()
    outs = []
    for shift in (0,) + send_order(count):
        sender = lax.rem(me + count - shift, count)
        if shift > 0:
            pltpu.make_async_remote_copy(
                src_ref=slots.at[sender],
                dst_ref=slots.at[sender],
                send_sem=ag_send.at[shift],
                recv_sem=ag_recv.at[shift],
                device_id=(group, sender, core),
                device_id_type=mesh_ids,
            ).wait_recv()
        rows = slots[sender]
        total = None
        for table in (own_w, other_w):
            gate = jnp.dot(rows, table[:, pl.ds(0, ff)], preferred_element_type=jnp.float32)
            up = jnp.dot(rows, table[:, pl.ds(ff, ff)], preferred_element_type=jnp.float32)
            act = (gate / (1.0 + jnp.exp(-gate)) * up).astype(jnp.bfloat16)
            down = lax.dot_general(
                act, table[:, pl.ds(2 * ff, ff)], (((1,), (1,)), ((), ())),
                preferred_element_type=jnp.float32,
            )
            total = down if total is None else total + down
        partials[shift] = total.astype(jnp.bfloat16)
        if shift == 0:
            back = pltpu.make_async_copy(partials.at[0], rs_out.at[me], local_sems.at[2])
        else:
            back = pltpu.make_async_remote_copy(
                src_ref=partials.at[shift],
                dst_ref=rs_out.at[me],
                send_sem=rs_send.at[shift],
                recv_sem=rs_recv.at[shift],
                device_id=(group, sender, core),
                device_id_type=mesh_ids,
            )
        back.start()
        outs.append(back)
    for shift in range(1, count):
        owner = lax.rem(me + shift, count)
        pltpu.make_async_remote_copy(
            src_ref=partials.at[shift],
            dst_ref=rs_out.at[owner],
            send_sem=rs_send.at[shift],
            recv_sem=rs_recv.at[shift],
            device_id=(group, owner, core),
            device_id_type=mesh_ids,
        ).wait_recv()
    outs[0].wait()
    for copy in outs[1:]:
        copy.wait_send()
    for copy in sends:
        copy.wait_send()


def fused_mlp(block, weights, tag):
    count = lax.axis_size("chip")
    rows, cols = block.shape
    ff = weights.shape[1] // 3
    flops = 2 * count * rows * cols * ff * 6
    return pl.pallas_call(
        functools.partial(mlp_kernel, count, ff),
        out_shape=jax.ShapeDtypeStruct((count, rows, cols), block.dtype),
        in_specs=[pl.BlockSpec(memory_space=pl.ANY)] * 2,
        out_specs=pl.BlockSpec(memory_space=pl.ANY),
        scratch_shapes=[
            pltpu.VMEM(weights.shape, weights.dtype),
            pltpu.VMEM(weights.shape, weights.dtype),
            pltpu.VMEM((count, rows, cols), block.dtype),
            pltpu.VMEM((count, rows, cols), block.dtype),
            pltpu.SemaphoreType.DMA((count,)),
            pltpu.SemaphoreType.DMA((count,)),
            pltpu.SemaphoreType.DMA((count,)),
            pltpu.SemaphoreType.DMA((count,)),
            pltpu.SemaphoreType.DMA((2,)),
            pltpu.SemaphoreType.DMA((3,)),
        ],
        compiler_params=pltpu.CompilerParams(
            collective_id=tag, has_side_effects=True, vmem_limit_bytes=60 * 1024 * 1024
        ),
        cost_estimate=pl.CostEstimate(
            flops=flops, bytes_accessed=4 * count * rows * cols * 2, transcendentals=count * rows * ff * 2
        ),
    )(block, weights)


def gather_group(block):
    count = lax.axis_size("group")
    pieces = [block]
    for shift in range(1, count):
        route = [(source, (source + shift) % count) for source in range(count)]
        pieces.append(lax.ppermute(block, "group", route))
    stacked = jnp.stack(pieces)
    order = (lax.axis_index("group") - jnp.arange(count)) % count
    return jnp.take(stacked, order, axis=0).reshape(count * block.shape[0], block.shape[1])


def rms_scale(values, gain):
    square = jnp.mean(values * values, axis=-1, keepdims=True)
    return (values * lax.rsqrt(square + norm_eps) * gain).astype(jnp.bfloat16)


def rotate(values, places):
    half_dim = values.shape[-1] // 2
    frequency = rope_base ** (-(jnp.arange(half_dim, dtype=jnp.float32) * 2.0 / values.shape[-1]))
    angle = places.astype(jnp.float32)[:, None] * frequency[None, :]
    cosine = jnp.cos(angle)[:, None, :]
    sine = jnp.sin(angle)[:, None, :]
    widened = values.astype(jnp.float32)
    first = widened[..., :half_dim]
    second = widened[..., half_dim:]
    return jnp.concatenate(
        [first * cosine - second * sine, second * cosine + first * sine], axis=-1
    ).astype(jnp.bfloat16)


def by_core(own_part, other_part):
    first = lax.axis_index("core") == 0
    return jnp.where(first, own_part, other_part), jnp.where(first, other_part, own_part)


def dot(acts, weight):
    return jnp.dot(acts, weight, preferred_element_type=jnp.float32)


def dot_t(acts, weight_t):
    return lax.dot_general(
        acts, weight_t, (((1,), (1,)), ((), ())), preferred_element_type=jnp.float32
    )


def core_rows(values, chips, rows_dev):
    blocks = values.reshape(chips, 2, rows_dev, *values.shape[1:])
    own = lax.dynamic_index_in_dim(blocks, lax.axis_index("core"), axis=1, keepdims=False)
    return own.reshape(chips * rows_dev, *values.shape[1:])


def body(
    hidden,
    request_of,
    positions,
    page_table,
    attn_gain,
    mlp_gain,
    wq,
    wk,
    wv,
    wo,
    w_gate,
    w_up,
    w_down,
):
    chips = lax.axis_size("chip")
    rows_dev = hidden.shape[0]
    tok_group = request_of.shape[0]
    bf = jnp.bfloat16
    residual = hidden.astype(jnp.float32)
    q_cols = wq.shape[1]
    kv_half = wk.shape[1]
    own_attn = jnp.concatenate([wq.astype(bf), wk.astype(bf), wv.astype(bf), wo.astype(bf).T], axis=1)
    own_attn = lax.all_gather(own_attn, "group", axis=0, tiled=True)
    normed = gather_chip(rms_scale(residual, attn_gain), 0)
    other_attn = swap_cores(own_attn)
    query_w = jnp.concatenate([own_attn[:, :q_cols], other_attn[:, :q_cols]], axis=1)
    out_w_t = jnp.concatenate(
        [own_attn[:, q_cols + 2 * kv_half :], other_attn[:, q_cols + 2 * kv_half :]], axis=1
    )
    key_lo, key_hi = by_core(own_attn[:, q_cols : q_cols + kv_half], other_attn[:, q_cols : q_cols + kv_half])
    value_lo, value_hi = by_core(
        own_attn[:, q_cols + kv_half : q_cols + 2 * kv_half],
        other_attn[:, q_cols + kv_half : q_cols + 2 * kv_half],
    )
    key_w = jnp.concatenate([key_lo, key_hi], axis=1)
    value_w = jnp.concatenate([value_lo, value_hi], axis=1)
    ff_cols = w_gate.shape[1]
    own_mlp = jnp.concatenate([w_gate.astype(bf), w_up.astype(bf), w_down.astype(bf).T], axis=1)
    own_mlp = lax.all_gather(own_mlp, "group", axis=0, tiled=True)
    half_pos = core_rows(positions, chips, rows_dev)
    half_req = core_rows(request_of, chips, rows_dev)
    heads = 2 * q_cols // HD
    queries = rotate(dot(normed, query_w).astype(bf).reshape(-1, heads, HD), half_pos)
    keys_half = rotate(dot(normed, key_w).astype(bf).reshape(-1, 1, HD), half_pos)
    values_half = dot(normed, value_w).astype(bf).reshape(-1, 1, HD)
    kv_own = jnp.stack([keys_half[:, 0], values_half[:, 0]], axis=1)
    kv_other = swap_cores(kv_own)
    kv_lo, kv_hi = by_core(kv_own, kv_other)
    kv_rows = jnp.stack(
        [kv_lo.reshape(chips, rows_dev, 2, HD), kv_hi.reshape(chips, rows_dev, 2, HD)], axis=1
    ).reshape(tok_group, 2, HD)
    earlier_rows = min(MAXLEN, tok_group)
    earlier = from_behind(kv_rows[tok_group - earlier_rows :], "group", 1)
    all_rows = jnp.concatenate([earlier, kv_rows], axis=0)
    all_keys = all_rows[:, 0]
    all_values = all_rows[:, 1]
    first_request = request_of[0]
    first_position = positions[0]
    same_local = (half_req[:, None] == request_of[None, :]) & (
        positions[None, :] <= half_pos[:, None]
    )
    same_earlier = (half_req[:, None] == first_request) & (
        jnp.arange(earlier_rows)[None, :] >= earlier_rows - first_position
    )
    visible = jnp.concatenate([same_earlier, same_local], axis=1)
    scores = jnp.einsum(
        "qhd,kd->hqk", queries, all_keys, preferred_element_type=jnp.float32
    ) * HD ** (-0.5)
    scores = jnp.where(visible[None], scores, -1e30)
    row_peak = jnp.max(scores, axis=-1, keepdims=True)
    probs = jnp.where(visible[None], jnp.exp(scores - row_peak), 0.0)
    total = jnp.sum(probs, axis=-1, keepdims=True)
    mixed_heads = jnp.einsum(
        "hqk,kd->qhd", probs.astype(bf), all_values, preferred_element_type=jnp.float32
    ) / jnp.transpose(total, (1, 0, 2))
    attended = mixed_heads.astype(bf).reshape(-1, heads * HD)
    attn_part = dot_t(attended, out_w_t)
    attn_sum = scatter_chip(attn_part.astype(bf), 1)
    mixed = residual + attn_sum
    partials = fused_mlp(rms_scale(mixed, mlp_gain), own_mlp, 2)
    layer_out = (mixed + jnp.sum(partials.astype(jnp.float32), axis=0)).astype(bf)
    pages = page_table.shape[1]
    changed = jnp.concatenate(
        [jnp.ones((1,), jnp.int32), (request_of[1:] != request_of[:-1]).astype(jnp.int32)]
    )
    opens = jnp.maximum(changed, (positions % PAGE == 0).astype(jnp.int32))
    logical = jnp.cumsum(opens) - 1
    chosen = jnp.sum(
        jnp.where(logical[:, None] == jnp.arange(pages)[None, :], page_table, 0), axis=1
    )
    target = chosen * PAGE + positions % PAGE
    own_slice = lax.dynamic_index_in_dim(kv_rows, lax.axis_index("core"), axis=1, keepdims=False)
    width = own_slice.shape[1]
    cache = jnp.zeros((pages * PAGE, width), jnp.bfloat16).at[target].set(own_slice)
    return (layer_out, cache.reshape(pages, PAGE, width))


def solution(mesh):
    groups, tensors = mesh.devices.shape
    split = Mesh(mesh.devices.reshape(groups, tensors // 2, 2), ("group", "chip", "core"))
    tensor = ("chip", "core")
    placed = (
        P(("group",) + tensor, None),
        P("group"),
        P("group"),
        P("group", None),
        P(),
        P(),
        P("group", tensor),
        P("group", tensor),
        P("group", tensor),
        P(tensor, "group"),
        P("group", tensor),
        P("group", tensor),
        P(tensor, "group"),
    )
    return jax.shard_map(
        body,
        mesh=split,
        in_specs=placed,
        out_specs=(P(("group",) + tensor, None), P("group", None, tensor)),
        check_vma=False,
    )
```

```python
import functools

import jax
import jax.numpy as jnp
from jax import lax
from jax.experimental import pallas as pl
from jax.experimental.pallas import tpu as pltpu
from jax.sharding import Mesh
from jax.sharding import PartitionSpec as P

QH = 16
KVH = 8
HD = 128
PAGE = 128
MAXLEN = 512
FAR_FIRST = (4, 2, 6, 3, 5, 1, 7)


rope_base = 1000000.0
norm_eps = 1e-06


def swap_cores(value):
    return lax.ppermute(value, "core", [(0, 1), (1, 0)])


def from_behind(block, axis, distance):
    devices = range(lax.axis_size(axis))
    route = [(i - distance, i) for i in devices if i - distance in devices]
    return lax.ppermute(block, axis, route)


def send_order(count):
    if sorted(FAR_FIRST) == list(range(1, count)):
        return FAR_FIRST
    return tuple(range(1, count))


def exchange_kernel(count, spread, spreads, swaps, *refs):
    source = refs[0]
    weights = refs[1] if (spreads or swaps) else None
    outs = refs[1 + (spreads or swaps) :]
    slots = outs[0]
    moved = outs[1] if (spreads or swaps) else None
    send_sems, recv_sems, local_sem = outs[-3:]
    me = lax.axis_index("chip")
    group = lax.axis_index("group")
    core = lax.axis_index("core")
    groups = lax.axis_size("group")
    mesh_ids = pl.DeviceIdType.MESH
    barrier = pltpu.get_barrier_semaphore()
    for shift in range(1, count):
        peer = lax.rem(me + shift, count)
        pl.semaphore_signal(barrier, inc=1, device_id=(group, peer, core), device_id_type=mesh_ids)
    greeted = count - 1
    if swaps:
        pl.semaphore_signal(barrier, inc=1, device_id=(group, me, 1 - core), device_id_type=mesh_ids)
        greeted += 1
    if spreads:
        for shift in range(1, groups):
            peer = lax.rem(group + shift, groups)
            pl.semaphore_signal(barrier, inc=1, device_id=(peer, me, core), device_id_type=mesh_ids)
        greeted += groups - 1
    pl.semaphore_wait(barrier, greeted)
    locals_ = []
    copies = []
    if swaps:
        swap = pltpu.make_async_remote_copy(
            src_ref=weights,
            dst_ref=moved,
            send_sem=send_sems.at[0],
            recv_sem=recv_sems.at[0],
            device_id=(group, me, 1 - core),
            device_id_type=mesh_ids,
        )
        swap.start()
        copies.append(swap)
    if spreads:
        own_weights = pltpu.make_async_copy(weights, moved.at[group], local_sem.at[1])
        own_weights.start()
        locals_.append(own_weights)
        for shift in range(1, groups):
            peer = lax.rem(group + shift, groups)
            copy = pltpu.make_async_remote_copy(
                src_ref=weights,
                dst_ref=moved.at[group],
                send_sem=send_sems.at[count + shift],
                recv_sem=recv_sems.at[count + shift],
                device_id=(peer, me, core),
                device_id_type=mesh_ids,
            )
            copy.start()
            copies.append(copy)
    for shift in send_order(count):
        peer = lax.rem(me + shift, count)
        copy = pltpu.make_async_remote_copy(
            src_ref=source.at[peer] if spread else source,
            dst_ref=slots.at[me],
            send_sem=send_sems.at[shift],
            recv_sem=recv_sems.at[shift],
            device_id=(group, peer, core),
            device_id_type=mesh_ids,
        )
        copy.start()
        copies.append(copy)
    local = pltpu.make_async_copy(source.at[me] if spread else source, slots.at[me], local_sem.at[0])
    local.start()
    locals_.append(local)
    for shift in range(1, count):
        sender = lax.rem(me + count - shift, count)
        pltpu.make_async_remote_copy(
            src_ref=slots.at[sender],
            dst_ref=slots.at[sender],
            send_sem=send_sems.at[shift],
            recv_sem=recv_sems.at[shift],
            device_id=(group, sender, core),
            device_id_type=mesh_ids,
        ).wait_recv()
    if swaps:
        swap.wait_recv()
    if spreads:
        for shift in range(1, groups):
            sender = lax.rem(group + groups - shift, groups)
            pltpu.make_async_remote_copy(
                src_ref=moved.at[sender],
                dst_ref=moved.at[sender],
                send_sem=send_sems.at[count + shift],
                recv_sem=recv_sems.at[count + shift],
                device_id=(sender, me, core),
                device_id_type=mesh_ids,
            ).wait_recv()
    for copy in copies:
        copy.wait_send()
    for copy in locals_:
        copy.wait()


def exchange(block, spread, tag, weights=None, spreads=False):
    count = lax.axis_size("chip")
    groups = lax.axis_size("group")
    rows, cols = block.shape[-2:]
    moved = count * rows * cols * block.dtype.itemsize
    out_shape = [jax.ShapeDtypeStruct((count, rows, cols), block.dtype)]
    operands = [block]
    swaps = weights is not None and not spreads
    if weights is not None:
        copies = groups if spreads else 1
        out_shape.append(jax.ShapeDtypeStruct((copies,) * spreads + weights.shape, weights.dtype))
        operands.append(weights)
        moved += copies * weights.size * weights.dtype.itemsize
    outs = pl.pallas_call(
        functools.partial(exchange_kernel, count, spread, spreads, swaps),
        out_shape=tuple(out_shape),
        in_specs=[pl.BlockSpec(memory_space=pl.ANY)] * len(operands),
        out_specs=tuple(pl.BlockSpec(memory_space=pl.ANY) for _ in out_shape),
        scratch_shapes=[
            pltpu.SemaphoreType.DMA((count + groups,)),
            pltpu.SemaphoreType.DMA((count + groups,)),
            pltpu.SemaphoreType.DMA((2,)),
        ],
        compiler_params=pltpu.CompilerParams(collective_id=tag, has_side_effects=True),
        cost_estimate=pl.CostEstimate(flops=0, bytes_accessed=2 * moved, transcendentals=0),
    )(*operands)
    return outs


def gather_chip(block, tag):
    outs = exchange(block, False, tag)
    return outs[0].reshape(-1, block.shape[1])


def gather_swap(block, tag, weights):
    outs = exchange(block, False, tag, weights)
    return outs[0].reshape(-1, block.shape[1]), outs[1]


def scatter_chip(partial, tag):
    count = lax.axis_size("chip")
    outs = exchange(partial.reshape(count, -1, partial.shape[1]), True, tag)
    return jnp.sum(outs[0].astype(jnp.float32), axis=0)


def mlp_kernel(count, ff, own_block, weights, rs_out, own_w, other_w, slots, partials, ag_send, ag_recv, rs_send, rs_recv, swap_sems, local_sems):
    me = lax.axis_index("chip")
    group = lax.axis_index("group")
    core = lax.axis_index("core")
    mesh_ids = pl.DeviceIdType.MESH
    barrier = pltpu.get_barrier_semaphore()
    for shift in range(1, count):
        peer = lax.rem(me + shift, count)
        pl.semaphore_signal(barrier, inc=1, device_id=(group, peer, core), device_id_type=mesh_ids)
    pl.semaphore_signal(barrier, inc=1, device_id=(group, me, 1 - core), device_id_type=mesh_ids)
    pl.semaphore_wait(barrier, count)
    load_w = pltpu.make_async_copy(weights, own_w, local_sems.at[0])
    load_w.start()
    load_x = pltpu.make_async_copy(own_block, slots.at[me], local_sems.at[1])
    load_x.start()
    swap = pltpu.make_async_remote_copy(
        src_ref=weights,
        dst_ref=other_w,
        send_sem=swap_sems.at[0],
        recv_sem=swap_sems.at[1],
        device_id=(group, me, 1 - core),
        device_id_type=mesh_ids,
    )
    swap.start()
    sends = [swap]
    for shift in send_order(count):
        peer = lax.rem(me + shift, count)
        copy = pltpu.make_async_remote_copy(
            src_ref=own_block,
            dst_ref=slots.at[me],
            send_sem=ag_send.at[shift],
            recv_sem=ag_recv.at[shift],
            device_id=(group, peer, core),
            device_id_type=mesh_ids,
        )
        copy.start()
        sends.append(copy)
    load_w.wait()
    swap.wait_recv()
    load_x.wait()
    outs = []
    for shift in (0,) + send_order(count):
        sender = lax.rem(me + count - shift, count)
        if shift > 0:
            pltpu.make_async_remote_copy(
                src_ref=slots.at[sender],
                dst_ref=slots.at[sender],
                send_sem=ag_send.at[shift],
                recv_sem=ag_recv.at[shift],
                device_id=(group, sender, core),
                device_id_type=mesh_ids,
            ).wait_recv()
        rows = slots[sender]
        total = None
        for table in (own_w, other_w):
            gate = jnp.dot(rows, table[:, pl.ds(0, ff)], preferred_element_type=jnp.float32)
            up = jnp.dot(rows, table[:, pl.ds(ff, ff)], preferred_element_type=jnp.float32)
            act = (gate / (1.0 + jnp.exp(-gate)) * up).astype(jnp.bfloat16)
            down = lax.dot_general(
                act, table[:, pl.ds(2 * ff, ff)], (((1,), (1,)), ((), ())),
                preferred_element_type=jnp.float32,
            )
            total = down if total is None else total + down
        partials[shift] = total.astype(jnp.bfloat16)
        if shift == 0:
            back = pltpu.make_async_copy(partials.at[0], rs_out.at[me], local_sems.at[2])
        else:
            back = pltpu.make_async_remote_copy(
                src_ref=partials.at[shift],
                dst_ref=rs_out.at[me],
                send_sem=rs_send.at[shift],
                recv_sem=rs_recv.at[shift],
                device_id=(group, sender, core),
                device_id_type=mesh_ids,
            )
        back.start()
        outs.append(back)
    for shift in range(1, count):
        owner = lax.rem(me + shift, count)
        pltpu.make_async_remote_copy(
            src_ref=partials.at[shift],
            dst_ref=rs_out.at[owner],
            send_sem=rs_send.at[shift],
            recv_sem=rs_recv.at[shift],
            device_id=(group, owner, core),
            device_id_type=mesh_ids,
        ).wait_recv()
    outs[0].wait()
    for copy in outs[1:]:
        copy.wait_send()
    for copy in sends:
        copy.wait_send()


def fused_mlp(block, weights, tag):
    count = lax.axis_size("chip")
    rows, cols = block.shape
    ff = weights.shape[1] // 3
    flops = 2 * count * rows * cols * ff * 6
    return pl.pallas_call(
        functools.partial(mlp_kernel, count, ff),
        out_shape=jax.ShapeDtypeStruct((count, rows, cols), block.dtype),
        in_specs=[pl.BlockSpec(memory_space=pl.ANY)] * 2,
        out_specs=pl.BlockSpec(memory_space=pl.ANY),
        scratch_shapes=[
            pltpu.VMEM(weights.shape, weights.dtype),
            pltpu.VMEM(weights.shape, weights.dtype),
            pltpu.VMEM((count, rows, cols), block.dtype),
            pltpu.VMEM((count, rows, cols), block.dtype),
            pltpu.SemaphoreType.DMA((count,)),
            pltpu.SemaphoreType.DMA((count,)),
            pltpu.SemaphoreType.DMA((count,)),
            pltpu.SemaphoreType.DMA((count,)),
            pltpu.SemaphoreType.DMA((2,)),
            pltpu.SemaphoreType.DMA((3,)),
        ],
        compiler_params=pltpu.CompilerParams(
            collective_id=tag, has_side_effects=True, vmem_limit_bytes=60 * 1024 * 1024
        ),
        cost_estimate=pl.CostEstimate(
            flops=flops, bytes_accessed=4 * count * rows * cols * 2, transcendentals=count * rows * ff * 2
        ),
    )(block, weights)


def gather_group(block):
    count = lax.axis_size("group")
    pieces = [block]
    for shift in range(1, count):
        route = [(source, (source + shift) % count) for source in range(count)]
        pieces.append(lax.ppermute(block, "group", route))
    stacked = jnp.stack(pieces)
    order = (lax.axis_index("group") - jnp.arange(count)) % count
    return jnp.take(stacked, order, axis=0).reshape(count * block.shape[0], block.shape[1])


def rms_scale(values, gain):
    square = jnp.mean(values * values, axis=-1, keepdims=True)
    return (values * lax.rsqrt(square + norm_eps) * gain).astype(jnp.bfloat16)


def rotate(values, places):
    half_dim = values.shape[-1] // 2
    frequency = rope_base ** (-(jnp.arange(half_dim, dtype=jnp.float32) * 2.0 / values.shape[-1]))
    angle = places.astype(jnp.float32)[:, None] * frequency[None, :]
    cosine = jnp.cos(angle)[:, None, :]
    sine = jnp.sin(angle)[:, None, :]
    widened = values.astype(jnp.float32)
    first = widened[..., :half_dim]
    second = widened[..., half_dim:]
    return jnp.concatenate(
        [first * cosine - second * sine, second * cosine + first * sine], axis=-1
    ).astype(jnp.bfloat16)


def by_core(own_part, other_part):
    first = lax.axis_index("core") == 0
    return jnp.where(first, own_part, other_part), jnp.where(first, other_part, own_part)


def dot(acts, weight):
    return jnp.dot(acts, weight, preferred_element_type=jnp.float32)


def dot_t(acts, weight_t):
    return lax.dot_general(
        acts, weight_t, (((1,), (1,)), ((), ())), preferred_element_type=jnp.float32
    )


def core_rows(values, chips, rows_dev):
    blocks = values.reshape(chips, 2, rows_dev, *values.shape[1:])
    own = lax.dynamic_index_in_dim(blocks, lax.axis_index("core"), axis=1, keepdims=False)
    return own.reshape(chips * rows_dev, *values.shape[1:])


def body(
    hidden,
    request_of,
    positions,
    page_table,
    attn_gain,
    mlp_gain,
    wq,
    wk,
    wv,
    wo,
    w_gate,
    w_up,
    w_down,
):
    chips = lax.axis_size("chip")
    rows_dev = hidden.shape[0]
    tok_group = request_of.shape[0]
    bf = jnp.bfloat16
    residual = hidden.astype(jnp.float32)
    q_cols = wq.shape[1]
    kv_half = wk.shape[1]
    own_attn = jnp.concatenate([wq.astype(bf), wk.astype(bf), wv.astype(bf), wo.astype(bf).T], axis=1)
    own_attn = lax.all_gather(own_attn, "group", axis=0, tiled=True)
    normed = gather_chip(rms_scale(residual, attn_gain), 0)
    other_attn = swap_cores(own_attn)
    query_w = jnp.concatenate([own_attn[:, :q_cols], other_attn[:, :q_cols]], axis=1)
    out_w_t = jnp.concatenate(
        [own_attn[:, q_cols + 2 * kv_half :], other_attn[:, q_cols + 2 * kv_half :]], axis=1
    )
    key_lo, key_hi = by_core(own_attn[:, q_cols : q_cols + kv_half], other_attn[:, q_cols : q_cols + kv_half])
    value_lo, value_hi = by_core(
        own_attn[:, q_cols + kv_half : q_cols + 2 * kv_half],
        other_attn[:, q_cols + kv_half : q_cols + 2 * kv_half],
    )
    key_w = jnp.concatenate([key_lo, key_hi], axis=1)
    value_w = jnp.concatenate([value_lo, value_hi], axis=1)
    ff_cols = w_gate.shape[1]
    own_mlp = jnp.concatenate([w_gate.astype(bf), w_up.astype(bf), w_down.astype(bf).T], axis=1)
    own_mlp = lax.all_gather(own_mlp, "group", axis=0, tiled=True)
    half_pos = core_rows(positions, chips, rows_dev)
    half_req = core_rows(request_of, chips, rows_dev)
    heads = 2 * q_cols // HD
    queries = rotate(dot(normed, query_w).astype(bf).reshape(-1, heads, HD), half_pos)
    keys_half = rotate(dot(normed, key_w).astype(bf).reshape(-1, 1, HD), half_pos)
    values_half = dot(normed, value_w).astype(bf).reshape(-1, 1, HD)
    kv_own = jnp.stack([keys_half[:, 0], values_half[:, 0]], axis=1)
    kv_other = swap_cores(kv_own)
    kv_lo, kv_hi = by_core(kv_own, kv_other)
    kv_rows = jnp.stack(
        [kv_lo.reshape(chips, rows_dev, 2, HD), kv_hi.reshape(chips, rows_dev, 2, HD)], axis=1
    ).reshape(tok_group, 2, HD)
    earlier_rows = min(MAXLEN, tok_group)
    earlier = from_behind(kv_rows[tok_group - earlier_rows :], "group", 1)
    all_rows = jnp.concatenate([earlier, kv_rows], axis=0)
    all_keys = all_rows[:, 0]
    all_values = all_rows[:, 1]
    first_request = request_of[0]
    first_position = positions[0]
    same_local = (half_req[:, None] == request_of[None, :]) & (
        positions[None, :] <= half_pos[:, None]
    )
    same_earlier = (half_req[:, None] == first_request) & (
        jnp.arange(earlier_rows)[None, :] >= earlier_rows - first_position
    )
    visible = jnp.concatenate([same_earlier, same_local], axis=1)
    scores = jnp.einsum(
        "qhd,kd->hqk", queries, all_keys, preferred_element_type=jnp.float32
    ) * HD ** (-0.5)
    scores = jnp.where(visible[None], scores, -1e30)
    row_peak = jnp.max(scores, axis=-1, keepdims=True)
    probs = jnp.where(visible[None], jnp.exp(scores - row_peak), 0.0)
    total = jnp.sum(probs, axis=-1, keepdims=True)
    mixed_heads = jnp.einsum(
        "hqk,kd->qhd", probs.astype(bf), all_values, preferred_element_type=jnp.float32
    ) / jnp.transpose(total, (1, 0, 2))
    attended = mixed_heads.astype(bf).reshape(-1, heads * HD)
    attn_part = dot_t(attended, out_w_t)
    attn_sum = scatter_chip(attn_part.astype(bf), 1)
    mixed = residual + attn_sum
    partials = fused_mlp(rms_scale(mixed, mlp_gain), own_mlp, 2)
    layer_out = (mixed + jnp.sum(partials.astype(jnp.float32), axis=0)).astype(bf)
    pages = page_table.shape[1]
    changed = jnp.concatenate(
        [jnp.ones((1,), jnp.int32), (request_of[1:] != request_of[:-1]).astype(jnp.int32)]
    )
    opens = jnp.maximum(changed, (positions % PAGE == 0).astype(jnp.int32))
    logical = jnp.cumsum(opens) - 1
    chosen = jnp.sum(
        jnp.where(logical[:, None] == jnp.arange(pages)[None, :], page_table, 0), axis=1
    )
    target = chosen * PAGE + positions % PAGE
    own_slice = lax.dynamic_index_in_dim(kv_rows, lax.axis_index("core"), axis=1, keepdims=False)
    width = own_slice.shape[1]
    cache = jnp.zeros((pages * PAGE, width), jnp.bfloat16).at[target].set(own_slice)
    return (layer_out, cache.reshape(pages, PAGE, width))


def solution(mesh):
    groups, tensors = mesh.devices.shape
    split = Mesh(mesh.devices.reshape(groups, tensors // 2, 2), ("group", "chip", "core"))
    tensor = ("chip", "core")
    placed = (
        P(("group",) + tensor, None),
        P("group"),
        P("group"),
        P("group", None),
        P(),
        P(),
        P("group", tensor),
        P("group", tensor),
        P("group", tensor),
        P(tensor, "group"),
        P("group", tensor),
        P("group", tensor),
        P(tensor, "group"),
    )
    return jax.shard_map(
        body,
        mesh=split,
        in_specs=placed,
        out_specs=(P(("group",) + tensor, None), P("group", None, tensor)),
        check_vma=False,
    )
```
